32 devices in a mesh: gx: 16 (over z, y, x), gy: 2 (over core).
Axes of the slice: x: 2, y: 2, z: 4, core: 2. Of those that a mesh axis runs over, the one named last changes fastest.
Arguments:
- right_side: float32 [64, 128, 128], P('gx', 'gy'), may hold values from -12 to 12
- phase: int32 [64, 128, 128], P('gx', 'gy'), may hold values from 0 to 1, as said below
Outputs:
- scaled_solution: float32 [64, 128, 128], P('gx', 'gy')
- residual: float32 [64, 128, 128], P('gx', 'gy')
The draws below stay inside these ranges and needn't reach their ends.
Inputs may be any that keep to these rules, and one draw needn't show every extreme that they name: `phase`: constant on each 2 x 2 x 2 block of cells that starts at even indices.
All inputs are finite; a program needn't handle non-finite values.
Results may differ from the reference program's by a relative error of at most 0.0024.
Values may be sent and summed in bfloat16 or wider, within the bound.
A program may use at most 64 MiB of HBM per device.

```python
import jax
import jax.numpy as jnp

NZ = 128
LEVELS = 6
NU = 2
COARSE_SWEEPS = 6
NX = 64
NY = 128


def draw_phase(key, part):
    blocks = jax.random.randint(jax.random.fold_in(key, 3), (NX // 2, NY // 2, NZ // 2), 0, 2, dtype=jnp.int32)
    return jnp.repeat(jnp.repeat(jnp.repeat(blocks, 2, 0), 2, 1), 2, 2)


def draw_right_side(key, part):
    noise = jax.random.normal(jax.random.fold_in(key, 11), (NX, NY, NZ), jnp.float32)
    values = noise
    return jnp.clip(values, -12.0, 12.0)


def setup_inputs(seed: int = 0) -> dict:
    splits = jax.random.split(jax.random.key(seed), 3)
    right_side = draw_right_side(jax.random.fold_in(splits[2], 71), 0)
    phase = draw_phase(jax.random.fold_in(splits[2], 71), 0)
    return dict(right_side=right_side, phase=phase)


OMEGA = 0.8


def harmonic(lower_cell, upper_cell):
    lower_value = jnp.where(lower_cell > 0, lower_cell, upper_cell)
    upper_value = jnp.where(upper_cell > 0, upper_cell, lower_cell)
    return (2.0 * lower_value * upper_value / (lower_value + upper_value)).astype(jnp.bfloat16)


def face_table(widened):
    face_x = harmonic(widened[:-1, 1:-1], widened[1:, 1:-1])
    face_y = harmonic(widened[1:-1, :-1], widened[1:-1, 1:])
    interior = jnp.pad(widened[1:-1, 1:-1], ((0, 0), (0, 0), (1, 1)), mode="edge")
    face_z = harmonic(interior[:, :, :-1], interior[:, :, 1:])
    return (face_x, face_y, face_z)


def pair_sum(values, dimension):
    dims_list = list(values.shape)
    dims_list[dimension:dimension + 1] = [dims_list[dimension] // 2, 2]
    return jnp.sum(values.reshape(dims_list), axis=dimension + 1)


def coarsen(faces):
    face_x, face_y, face_z = faces
    new_x = 0.25 * pair_sum(pair_sum(face_x.astype(jnp.float32)[0::2], 1), 2)
    new_y = 0.25 * pair_sum(pair_sum(face_y.astype(jnp.float32)[:, 0::2], 0), 2)
    new_z = 0.25 * pair_sum(pair_sum(face_z.astype(jnp.float32)[:, :, 0::2], 0), 1)
    return (new_x.astype(jnp.bfloat16), new_y.astype(jnp.bfloat16), new_z.astype(jnp.bfloat16))


def restrict(remainder):
    return 0.5 * pair_sum(pair_sum(pair_sum(remainder, 0), 1), 2)


def prolong(coarse):
    return jnp.repeat(jnp.repeat(jnp.repeat(coarse, 2, 0), 2, 1), 2, 2)


def centre_weight(faces):
    face_x, face_y, face_z = faces
    return (face_x[:-1].astype(jnp.float32) + face_x[1:].astype(jnp.float32)
            + face_y[:, :-1].astype(jnp.float32) + face_y[:, 1:].astype(jnp.float32)
            + face_z[:, :, :-1].astype(jnp.float32) + face_z[:, :, 1:].astype(jnp.float32))


def weighted(widened, faces):
    face_x, face_y, face_z = faces
    z_padded = jnp.pad(widened[1:-1, 1:-1], ((0, 0), (0, 0), (1, 1)))
    return (face_x[:-1] * widened[:-2, 1:-1] + face_x[1:] * widened[2:, 1:-1]
            + face_y[:, :-1] * widened[1:-1, :-2] + face_y[:, 1:] * widened[1:-1, 2:]
            + face_z[:, :, :-1] * z_padded[:, :, :-2] + face_z[:, :, 1:] * z_padded[:, :, 2:])


def cycle(source, faces, level_index):
    centre = centre_weight(faces)

    def operate(field):
        return centre * field - weighted(jnp.pad(field, ((1, 1), (1, 1), (0, 0))), faces)

    def smooth(field):
        return field + OMEGA * (source - operate(field)) / centre

    field = jnp.zeros_like(source)
    if level_index == LEVELS:
        for repeat in range(COARSE_SWEEPS):
            field = smooth(field)
        return field
    for repeat in range(NU):
        field = smooth(field)
    remainder = source - operate(field)
    coarse = cycle(restrict(remainder), coarsen(faces), level_index + 1)
    field = field + prolong(coarse)
    for repeat in range(NU):
        field = smooth(field)
    return field


def reference(right_side, phase):
    cell_beta = jnp.where(phase == 1, 1000.0, 1.0).astype(jnp.float32)
    widened = jnp.pad(cell_beta, ((1, 1), (1, 1), (0, 0)), mode="edge")
    faces = face_table(widened)
    solution = cycle(right_side, faces, 0)
    centre = centre_weight(faces)
    applied = centre * solution - weighted(jnp.pad(solution, ((1, 1), (1, 1), (0, 0))), faces)
    return centre * solution, right_side - applied
```

```python
import functools

import jax
import jax.numpy as jnp
import numpy as np
from jax import lax
from jax.experimental import pallas as pl
from jax.experimental.pallas import tpu as pltpu
from jax.sharding import PartitionSpec as P

LEVELS = 6
NU = 2
COARSE_SWEEPS = 6
OMEGA = 0.8
LIQUID, GAS = 1.0, 1000.0
MIXED = float(np.asarray(2.0 * LIQUID * GAS / (LIQUID + GAS), jnp.bfloat16))
MESH = pl.DeviceIdType.MESH
REACH = 3
EDGE = 8
EDGE_PHASE = 16
UNROLL = 16
LARGE = 1 << 20


def each(count, body):
    if count <= UNROLL:
        for i in range(count):
            body(i)
    else:
        lax.fori_loop(0, count, lambda i, carry: (body(i), carry)[1], 0)


def index_along(shape, axis):
    return lax.broadcasted_iota(jnp.int32, shape, axis)


def roll(x, shift, axis):
    return pltpu.roll(x, shift % x.shape[axis], axis)


def lane_bit(x, step):
    return index_along(x.shape, x.ndim - 1) // step % 2


def even_part(x, step):
    return jnp.where(lane_bit(x, step) == 0, x, roll(x, step, x.ndim - 1))


def odd_part(x, step):
    return jnp.where(lane_bit(x, step) == 1, x, roll(x, -step, x.ndim - 1))


def pair_lanes(x, step):
    axis = x.ndim - 1
    return x + jnp.where(lane_bit(x, step) == 0, roll(x, -step, axis), roll(x, step, axis))


def harmonic(a, b):
    low, high = jnp.minimum(a, b), jnp.maximum(a, b)
    return jnp.where((low == 0.0) | (low == high), high, MIXED)


def store(ref, i, value):
    ref[i] = value.astype(ref.dtype)


def wide(ref, i):
    return ref[i].astype(jnp.float32)


def quarter(x):
    return (0.25 * x).astype(jnp.bfloat16).astype(jnp.float32)


def kernel(ngx, ngy, counts, f_hbm, phase_hbm, scaled_ref, rest_ref, *refs):
    gx, gy = lax.axis_index("gx"), lax.axis_index("gy")
    n = ngx * ngy
    me = gx * ngy + gy
    lx, ly, nz = f_hbm.shape
    by, cy = ly // 2, ly // 4
    refs = list(refs)

    def take(count):
        out = refs[:count]
        del refs[:count]
        return out

    (w0, wn, wp, w1, gf, gt, g2) = take(7)
    (phase_ref, p_pack, f_pack, g1_pack, f2_pack, t_pack, g2_pack, temp) = take(8)
    (b1, e2) = take(2)
    level_refs = [take(10) for _ in range(LEVELS + 1)]
    (s0, r0, sf, rf, s1, r1, sp, rp, sg, rg, st, rt, si) = take(13)

    own_f = w0.at[pl.ds(lx, lx), pl.ds(EDGE, ly), :]
    load_phase = pltpu.make_async_copy(phase_hbm, phase_ref, si.at[0])
    load_f = pltpu.make_async_copy(f_hbm, own_f, si.at[1])
    load_phase.start()
    load_f.start()

    for start in (0, EDGE + ly):
        w0[:, pl.ds(start, EDGE), :] = jnp.zeros((3 * lx, EDGE, nz), w0.dtype)
    wn[...] = jnp.zeros(wn.shape, wn.dtype)
    wp[...] = jnp.zeros(wp.shape, wp.dtype)
    w1[...] = jnp.zeros(w1.shape, w1.dtype)

    barrier = pltpu.get_barrier_semaphore()

    def greet(k, carry):
        other = (me + k) % n
        pl.semaphore_signal(barrier, inc=1, device_id=(other // ngy, other % ngy), device_id_type=MESH)
        return carry

    lax.fori_loop(1, n, greet, 0)

    for l in range(LEVELS + 1):
        for v in level_refs[l][:2]:
            zero = jnp.zeros(v.shape[1:], v.dtype)
            v[0] = zero
            v[v.shape[0] - 1] = zero

    load_phase.wait()
    for plane in range(0, lx, 4):
        beta = [
            jnp.where(phase_ref[plane + 2 * k, pl.ds(0, by, 2), :] == 1, GAS, LIQUID) for k in range(2)
        ]
        p_pack[0] = jnp.where(lane_bit(beta[0], 1) == 0, beta[0], beta[1]).astype(jnp.bfloat16)
    load_f.wait()
    f_pack[...] = own_f[...].astype(jnp.bfloat16)

    pl.semaphore_wait(barrier, n - 1)

    def window_copy(src, dst, send, recv, reach, edge, half, d, e, slot, low_row, toward):
        lead, rows = src.shape[0], src.shape[1]
        plane, planes = 0, lead
        if half is not None and d != 0:
            planes = lead // 2
            plane = planes if (toward > 0) == (half == 0) else 0
        k = (d + reach) * 3 + e + 1
        sems = dict(
            send_sem=send.at[k], recv_sem=recv.at[slot * 3 + 1 - low_row],
            device_id=(gx + d, gy + e), device_id_type=MESH,
        )
        if half is not None and e == 0:
            side = 0 if toward > 0 else lead
            return pltpu.make_async_remote_copy(
                src_ref=f_pack.at[pl.ds(plane, planes)], dst_ref=wn.at[pl.ds(side + plane, planes)], **sems
            )
        count = rows if e == 0 else edge
        source = src.at[pl.ds(plane, planes), pl.ds(rows - edge if e == 1 else 0, count), :]
        start = {0: edge, 1: 0, -1: edge + rows}[low_row]
        target = dst.at[pl.ds(slot * lead + plane, planes), pl.ds(start, count), :]
        return pltpu.make_async_remote_copy(src_ref=source, dst_ref=target, **sems)

    def window(low, high):
        for e in (0, 1, -1):
            for d in sorted(range(-high, high + 1), key=abs):
                if (d, e) != (0, 0) and abs(d) >= low:
                    there = (gx + d >= 0) & (gx + d < ngx) & (gy + e >= 0) & (gy + e < ngy)
                    yield d, e, there

    def window_send(refs, low, high, half=None):
        reach = refs[4]
        for d, e, there in window(low, high):
            @pl.when(there)
            def _():
                window_copy(*refs, half, d, e, reach - d, e, d).start()

    def window_wait(refs, low, high, half=None):
        reach = refs[4]
        for d, e, there in window(low, high):
            @pl.when(there)
            def _():
                window_copy(*refs, half, d, e, reach + d, -e, -d).wait_recv()

    def window_done(refs, low, high, half=None):
        reach = refs[4]
        for d, e, there in window(low, high):
            @pl.when(there)
            def _():
                window_copy(*refs, half, d, e, reach - d, e, d).wait_send()

    def gather_send(src, dst, k):
        def body(t, carry):
            other = (me + t) % n
            pltpu.make_async_remote_copy(
                src_ref=src, dst_ref=dst.at[pl.ds(me, 1)], send_sem=sg.at[k], recv_sem=rg.at[k],
                device_id=(other // ngy, other % ngy), device_id_type=MESH,
            ).start()
            return carry

        lax.fori_loop(1, n, body, 0)

    def gather_all(dst, k):
        every = dst.at[pl.ds(0, n - 1)]
        return pltpu.make_async_remote_copy(
            src_ref=every, dst_ref=every, send_sem=sg.at[k], recv_sem=rg.at[k],
            device_id=(gx, (gy + 1) % ngy), device_id_type=MESH,
        )

    def top_copy(j, other):
        return pltpu.make_async_remote_copy(
            src_ref=t_pack, dst_ref=gt.at[pl.ds(j, 1)], send_sem=st.at[0], recv_sem=rt.at[j],
            device_id=(other // ngy, other % ngy), device_id_type=MESH,
        )

    phase_window = (p_pack, wp, sp, rp, REACH, EDGE_PHASE)
    near_window = (own_f, w0, s0, r0, 1, EDGE)
    far_window = (own_f, w0, sf, rf, 1, EDGE)
    coarse_window = (g1_pack, w1, s1, r1, REACH, EDGE)
    window_send(phase_window, 0, 1)
    window_send(near_window, 0, 1, 0)
    window_send(phase_window, 2, 2)
    wp[REACH, pl.ds(EDGE_PHASE, by), :] = p_pack[0]

    slots = temp.shape[0]

    def stretch(value, slot):
        rows = value.shape[0]
        temp[slot, pl.ds(0, rows, 2), :] = value
        temp[slot, pl.ds(1, rows, 2), :] = value

    def pair_rows(value, slot, first=True, second=True):
        rows = value.shape[0]
        temp[slot, pl.ds(0, rows), :] = value
        out = 0.0
        if first:
            out = out + temp[slot, pl.ds(0, rows // 2, 2), :]
        if second:
            out = out + temp[slot, pl.ds(1, rows // 2, 2), :]
        return out

    def neighbours(level, v_ref, i, step):
        (_, _, _, _, _, fx, fyl, fyh, fzl, fzh) = level
        v = v_ref[i + 1]
        return (
            wide(fx, i) * v_ref[i] + wide(fx, i + 1) * v_ref[i + 2]
            + wide(fyl, i) * roll(v, 1, 0) + wide(fyh, i) * roll(v, -1, 0)
            + wide(fzl, i) * roll(v, step, 1) + wide(fzh, i) * roll(v, -step, 1)
        )

    def sweep(level, source, target, step, first, last):
        f, inverse = level[2], level[3]

        def body(k):
            i = k + first
            target[i + 1] = (1.0 - OMEGA) * source[i + 1] + inverse[i] * (f[i] + neighbours(level, source, i, step))

        each(last - first, body)

    def rest_of(level, v_ref, i, step):
        return level[2][i] - level[4][i] * v_ref[i + 1] + neighbours(level, v_ref, i, step)

    def put_faces(level, i, inside, lows, step, edges):
        (_, _, _, inverse, centre, fx, fyl, fyh, fzl, fzh) = level
        (yl, yh, zl, zh) = lows
        total = wide(fx, i) + wide(fx, i + 1) + yl + yh + zl + zh
        inverse[i] = jnp.where(inside, OMEGA / jnp.where(inside, total, 1.0), 0.0)
        centre[i] = total
        lane = index_along(zl.shape, 1)
        fzl[i] = jnp.where(lane < step, 0.0, zl).astype(fzl.dtype)
        fzh[i] = jnp.where(lane >= nz - step, 0.0, zh).astype(fzh.dtype)
        if edges is not None:
            row = index_along(yl.shape, 0)
            yl = jnp.where(row == 0, 0.0, yl)
            yh = jnp.where(row >= edges - 1, 0.0, yh)
        fyl[i] = yl.astype(fyl.dtype)
        fyh[i] = yh.astype(fyh.dtype)

    def cell_faces(b, step):
        lane = index_along(b.shape, 1)
        yl, yh = harmonic(roll(b, 1, 0), b), harmonic(b, roll(b, -1, 0))
        zl = harmonic(jnp.where(lane < step, 0.0, roll(b, step, 1)), b)
        zh = harmonic(b, jnp.where(lane >= nz - step, 0.0, roll(b, -step, 1)))
        return yl, yh, zl, zh

    def phase_block(t):
        packed = wp[t].astype(jnp.float32)[EDGE_PHASE - EDGE : EDGE_PHASE + by + EDGE]
        b1[2 * t] = even_part(packed, 1)
        b1[2 * t + 1] = odd_part(packed, 1)

    window_wait(phase_window, 0, 1)
    for t in range(REACH - 1, REACH + 2):
        phase_block(t)

    level0 = list(level_refs[0])
    level0[2] = w0
    (va, vb, f0, inv0, c0, fx0) = level0[:6]
    rows0 = ly + 2 * EDGE
    blocks = 3 * lx // 2
    first_block = 2 * REACH - lx // 2
    planes0 = 3 * lx
    near0, near1 = lx - 2, 2 * lx + 2

    def fine_beta(j):
        slot = (j + 1) % slots
        stretch(b1[first_block + j], slot)
        return temp[slot, pl.ds(EDGE, rows0), :]

    def fine_faces(j):
        lows = cell_faces(beta0[j], 1)
        for i in (2 * j, 2 * j + 1):
            put_faces(level0, i, beta0[j] > 0.0, lows, 1, None)

    beta0 = [fine_beta(j) for j in range(blocks)]
    for j in range(blocks):
        if j > 0:
            fx0[2 * j] = harmonic(beta0[j - 1], beta0[j])
        fx0[2 * j + 1] = beta0[j]
    for j in range(near0 // 2, near1 // 2):
        fine_faces(j)

    window_wait(near_window, 0, 1, 0)
    for i in (lx - 2, lx - 1, 2 * lx, 2 * lx + 1):
        w0[i, pl.ds(EDGE, ly), :] = wn[i if i < lx else i - lx].astype(w0.dtype)
    for i in range(near0, near1):
        va[i + 1] = inv0[i] * w0[i]
    sweep(level0, va, vb, 1, near0 + 1, near1 - 1)
    rests = [rest_of(level0, vb, lx + i, 1)[EDGE : EDGE + ly] for i in range(lx)]
    coarse = [
        0.5 * pair_lanes(pair_rows(rests[2 * k] + rests[2 * k + 1], k % slots), 1) for k in range(lx // 2)
    ]
    packed = jnp.where(lane_bit(coarse[0], 1) == 0, coarse[0], coarse[1])
    g1_pack[0] = packed
    window_send(coarse_window, 0, 1)
    w1[REACH, pl.ds(EDGE, by), :] = packed

    own1 = 2 * REACH
    level1 = level_refs[1]
    (ua, ub, f1, inv1, c1, fx1) = level1[:6]
    planes1 = 2 * (2 * REACH + 1)
    near = range(own1 - 2, own1 + 4)

    def own_faces():
        own = slice(EDGE, EDGE + by)
        below, low, high, above = [b1[own1 + k] for k in range(-1, 3)]
        lane = index_along((by, nz), 1)
        pair = [low, high]
        mine = [b[own] for b in pair]
        x_low = quarter(pair_lanes(pair_rows(harmonic(below, low)[own], 0), 2))
        x_high = quarter(pair_lanes(pair_rows(harmonic(high, above)[own], 1), 2))
        y_low = sum(harmonic(roll(b, 1, 0), b)[own] for b in pair)
        y_high = sum(harmonic(b, roll(b, -1, 0))[own] for b in pair)
        z_low = sum(harmonic(jnp.where(lane < 2, 0.0, roll(b, 2, 1)), b) for b in mine)
        z_high = sum(harmonic(b, jnp.where(lane >= nz - 2, 0.0, roll(b, -2, 1))) for b in mine)
        y_low = quarter(pair_lanes(pair_rows(y_low, 2, second=False), 2))
        y_high = quarter(pair_lanes(pair_rows(y_high, 3, first=False), 2))
        z_low = quarter(even_part(pair_rows(z_low, 4), 2))
        z_high = quarter(odd_part(pair_rows(z_high, 5), 2))
        row, lane = index_along((cy, nz), 0), index_along((cy, nz), 1)
        corner = (row == cy - 2) & (lane // 4 == nz // 4 - 2)
        edge = jnp.where(corner, roll(roll(z_high, -1, 0), -4, 1), z_high)
        edge = jnp.where(row == cy - 1, y_high, edge)
        mixed = edge
        for k, value in enumerate((x_low, y_low, z_low)):
            mixed = jnp.where(lane % 4 == k, value, mixed)
        f2_pack[0] = mixed.astype(f2_pack.dtype)
        t_pack[0] = x_high.astype(t_pack.dtype)

    own_faces()
    gather_send(f2_pack, gf, 0)
    gf[me] = f2_pack[0]
    for j in range(ngy):
        @pl.when((gx == ngx - 1) & (gy == j))
        def _():
            def body(t, carry):
                top_copy(j, (me + t) % n).start()
                return carry

            lax.fori_loop(1, n, body, 0)
            gt[j] = t_pack[0]
    window_send(phase_window, REACH, REACH)

    window_wait(phase_window, 2, 2)
    phase_block(REACH - 2)
    phase_block(REACH + 2)
    for i in range(near[0], near[-1] + 2):
        fx1[i] = harmonic(b1[i - 1], b1[i])
    for i in near:
        put_faces(level1, i, b1[i] > 0.0, cell_faces(b1[i], 2), 2, None)

    def coarse_block(t):
        f1[2 * t] = even_part(w1[t], 1)
        f1[2 * t + 1] = odd_part(w1[t], 1)

    window_wait(coarse_window, 0, 1)
    for t in range(REACH - 1, REACH + 2):
        coarse_block(t)
    for i in near:
        ua[i + 1] = inv1[i] * f1[i]
    sweep(level1, ua, ub, 2, near[0] + 1, near[-1])
    rests = [rest_of(level1, ub, own1 + i, 2)[EDGE : EDGE + by] for i in range(2)]
    coarse = 0.5 * pair_lanes(pair_rows(rests[0] + rests[1], 0), 2)
    half = cy // 2
    packed = jnp.where(lane_bit(coarse[:half], 1) == 0, coarse[:half], coarse[half:])
    g2_pack[0] = packed
    gather_send(g2_pack, g2, 1)
    g2[me] = packed
    window_send(coarse_window, 2, REACH)
    window_send(far_window, 1, 1, 1)

    window_wait(phase_window, REACH, REACH)
    phase_block(0)
    phase_block(2 * REACH)
    far = [i for i in range(1, planes1 - 1) if i not in near]
    for i in range(1, planes1):
        if not near[0] <= i <= near[-1] + 1:
            fx1[i] = harmonic(b1[i - 1], b1[i])
    for i in far:
        put_faces(level1, i, b1[i] > 0.0, cell_faces(b1[i], 2), 2, None)

    gather_all(gf, 0).wait_recv()
    for j in range(ngy):
        @pl.when((gx < ngx - 1) | (gy != j))
        def _():
            top_copy(j, me).wait_recv()

    shape2 = counts[2]
    (nx2, ny2) = shape2
    level2 = level_refs[2]
    raw = level2[6:10]
    pick = (index_along((nz, 4 * nz), 0) == index_along((nz, 4 * nz), 1) % nz // 4 * 4 + index_along((nz, 4 * nz), 1) // nz)
    pick = jnp.where(pick, 1.0, 0.0).astype(jnp.bfloat16)

    def whole_plane(ref, k):
        return jnp.concatenate([ref[k * ngy + j].astype(jnp.float32) for j in range(ngy)], axis=0)

    def spread(x, columns):
        return jnp.dot(x.astype(jnp.bfloat16), columns, preferred_element_type=jnp.float32)

    def faces2(i):
        parts = spread(whole_plane(gf, i), pick)
        x_low, y_low, z_low, edge = [parts[:, k * nz : (k + 1) * nz] for k in range(4)]
        row, lane = index_along((ny2, nz), 0), index_along((ny2, nz), 1)
        y_high = jnp.where(row == ny2 - 1, edge, roll(y_low, -1, 0))
        z_edge = jnp.where(row % cy == cy - 1, roll(roll(edge, 1, 0), 4, 1), edge)
        z_high = jnp.where(lane >= nz - 4, z_edge, roll(z_low, -4, 1))
        store(level2[5], i, x_low)
        for ref, value in zip(raw, (y_low, y_high, z_low, z_high)):
            store(ref, i, value)

    each(nx2, faces2)
    store(level2[5], nx2, whole_plane(gt, 0))

    for l in range(2, LEVELS + 1):
        nx, ny = counts[l]
        step = 2**l
        level = level_refs[l]
        if l < LEVELS:
            finer, coarser = level_refs[l], level_refs[l + 1]
            size = max(ny // 2, 4)
            if ny // 2 < EDGE:
                for ref in coarser[5:10]:
                    ref[...] = jnp.zeros(ref.shape, ref.dtype)

            def put(ref, i, value):
                ref[i, pl.ds(0, size), :] = quarter(value).astype(ref.dtype)

            def coarsen(i):
                slot = 4 * (i % 2)
                (fx, yl, yh, zl, zh) = finer[5:10]
                a, b = 2 * i, 2 * i + 1
                put(coarser[5], i, pair_lanes(pair_rows(wide(fx, a), slot), step))
                put(coarser[6], i, pair_lanes(pair_rows(wide(yl, a) + wide(yl, b), slot + 1, second=False), step))
                put(coarser[7], i, pair_lanes(pair_rows(wide(yh, a) + wide(yh, b), slot + 2, first=False), step))
                put(coarser[8], i, even_part(pair_rows(wide(zl, a) + wide(zl, b), slot + 3), step))
                put(coarser[9], i, odd_part(pair_rows(wide(zh, a) + wide(zh, b), slot), step))

            each(nx // 2, coarsen)
            put(coarser[5], nx // 2, pair_lanes(pair_rows(wide(finer[5], nx), 5), step))

        def finish(i):
            lows = [wide(ref, i) for ref in level[6:10]]
            inside = index_along(lows[0].shape, 0) < ny
            put_faces(level, i, inside, lows, step, ny)

        each(nx, finish)

    window_wait(coarse_window, 2, REACH)
    for t in range(2 * REACH + 1):
        if abs(t - REACH) > 1:
            coarse_block(t)
    for i in far:
        ua[i + 1] = inv1[i] * f1[i]
    sweep(level1, ua, ub, 2, 2, near[0] + 1)
    sweep(level1, ua, ub, 2, near[-1], planes1 - 2)

    fx0[0] = harmonic(fine_beta(-1), beta0[0])
    fx0[planes0] = harmonic(beta0[blocks - 1], fine_beta(blocks))
    window_wait(far_window, 1, 1, 1)
    for i in range(planes0):
        if not near0 <= i < near1:
            if i % 2 == 0:
                fine_faces(i // 2)
            w0[i, pl.ds(EDGE, ly), :] = wn[i if i < lx else i - lx].astype(w0.dtype)
    for i in range(planes0):
        if not near0 <= i < near1:
            va[i + 1] = inv0[i] * w0[i]
    sweep(level0, va, vb, 1, 1, near0 + 1)
    sweep(level0, va, vb, 1, near1 - 1, planes0 - 1)

    gather_all(g2, 1).wait_recv()

    f2 = level2[2]

    def unpack(i):
        parts = []
        for j in range(ngy):
            pack = g2[i * ngy + j]
            parts += [even_part(pack, 1), odd_part(pack, 1)]
        f2[i] = jnp.concatenate(parts, axis=0)

    each(nx2, unpack)

    def cycle(l):
        nx, ny = counts[l]
        step = 2**l
        level = level_refs[l]
        (xa, xb, f, inverse) = level[:4]

        def begin(i):
            xa[i + 1] = inverse[i] * f[i]

        each(nx, begin)
        if l == LEVELS:
            for repeat in range(COARSE_SWEEPS - 1):
                sweep(level, xa, xb, step, 0, nx)
                xa, xb = xb, xa
            return xa
        for repeat in range(NU - 1):
            sweep(level, xa, xb, step, 0, nx)
            xa, xb = xb, xa
        f_next = level_refs[l + 1][2]
        size = max(ny // 2, 4)
        if ny // 2 < EDGE:
            f_next[...] = jnp.zeros(f_next.shape, f_next.dtype)

        def restrict(i):
            r = rest_of(level, xa, 2 * i, step) + rest_of(level, xa, 2 * i + 1, step)
            f_next[i, pl.ds(0, size), :] = 0.5 * pair_lanes(pair_rows(r, i % slots), step)

        each(nx // 2, restrict)
        fine = cycle(l + 1)

        def correct(i):
            slot = i % slots
            stretch(fine[i + 1], slot)
            e = temp[slot, pl.ds(0, xa.shape[1]), :]
            xb[2 * i + 1] = xa[2 * i + 1] + e
            xb[2 * i + 2] = xa[2 * i + 2] + e

        each(nx // 2, correct)
        xa, xb = xb, xa
        for repeat in range(NU):
            sweep(level, xa, xb, step, 0, nx)
            xa, xb = xb, xa
        return xa

    found = cycle(2)

    row2 = pl.multiple_of(gy * cy, 8)
    below2 = pl.multiple_of(jnp.maximum(gy * cy - EDGE, 0), 8)
    above2 = pl.multiple_of(jnp.minimum(gy * cy + cy, ny2 - EDGE), 8)
    for t in range(1, 2 * REACH):
        x = gx + t - REACH
        there = (x >= 0) & (x < nx2)
        plane = jnp.clip(x, 0, nx2 - 1) + 1
        e2[t, pl.ds(EDGE, cy), :] = jnp.where(there, found[plane, pl.ds(row2, cy), :], 0.0)
        low = found[plane, pl.ds(below2, EDGE), :]
        high = found[plane, pl.ds(above2, EDGE), :]
        e2[t, pl.ds(0, EDGE), :] = jnp.where(there & (gy > 0), low, 0.0)
        e2[t, pl.ds(EDGE + cy, EDGE), :] = jnp.where(there & (gy < ngy - 1), high, 0.0)

    for t in range(1, 2 * REACH):
        slot = t % slots
        stretch(e2[t], slot)
        e = temp[slot, pl.ds(EDGE, by + 2 * EDGE), :]
        ua[2 * t + 1] = ub[2 * t + 1] + e
        ua[2 * t + 2] = ub[2 * t + 2] + e
    sweep(level1, ua, ub, 2, 3, planes1 - 3)
    sweep(level1, ub, ua, 2, 4, planes1 - 4)

    for j in range(blocks):
        slot = j % slots
        stretch(ua[first_block + j + 1], slot)
        e = temp[slot, pl.ds(EDGE, rows0), :]
        va[2 * j + 1] = vb[2 * j + 1] + e
        va[2 * j + 2] = vb[2 * j + 2] + e
    sweep(level0, va, vb, 1, 2, planes0 - 2)
    sweep(level0, vb, va, 1, 3, planes0 - 3)
    for i in range(lx):
        product = c0[lx + i] * va[lx + i + 1]
        near_sum = neighbours(level0, va, lx + i, 1)
        own = slice(EDGE, EDGE + ly)
        scaled_ref[i] = product[own]
        rest_ref[i] = w0[lx + i, pl.ds(EDGE, ly), :] - product[own] + near_sum[own]

    window_done(phase_window, 0, REACH)
    window_done(near_window, 0, 1, 0)
    window_done(far_window, 1, 1, 1)
    window_done(coarse_window, 0, REACH)
    gather_all(gf, 0).wait_send()
    gather_all(g2, 1).wait_send()

    @pl.when(gx == ngx - 1)
    def _():
        every = gf.at[pl.ds(0, n - 1)]
        pltpu.make_async_remote_copy(
            src_ref=every, dst_ref=every, send_sem=st.at[0], recv_sem=rt.at[0],
            device_id=(gx, (gy + 1) % ngy), device_id_type=MESH,
        ).wait_send()


def write(scaled_ref, rest_ref, scaled_out, rest_out, sems):
    copies = [
        pltpu.make_async_copy(source, target, sems.at[k])
        for k, (source, target) in enumerate(((scaled_ref, scaled_out), (rest_ref, rest_out)))
    ]
    for copy in copies:
        copy.start()
    for copy in copies:
        copy.wait()


def solution(mesh):
    ngx, ngy = mesh.shape["gx"], mesh.shape["gy"]
    n = ngx * ngy

    def on_device(right_side, phase):
        lx, ly, nz = right_side.shape
        assert lx == 4 and ly % 32 == 0 and NU == 2
        by, cy = ly // 2, ly // 4
        counts = [(lx * ngx >> l, ly * ngy >> l) for l in range(LEVELS + 1)]
        blocks = 2 * REACH + 1

        def level_scratch(planes, rows, padded_source=False):
            shapes = [planes + 2, planes + 2, planes, planes, planes, planes + 1] + [planes] * 4
            if padded_source:
                shapes[2] = 1
            large = planes * rows * nz * 4 >= LARGE
            types = [jnp.float32] * 5 + [jnp.bfloat16 if large else jnp.float32] * 5
            return [pltpu.VMEM((k, rows, nz), dtype) for k, dtype in zip(shapes, types)]

        scratch = [
            pltpu.VMEM((3 * lx, ly + 2 * EDGE, nz), jnp.float32),
            pltpu.VMEM((2 * lx, ly, nz), jnp.bfloat16),
            pltpu.VMEM((blocks, by + 2 * EDGE_PHASE, nz), jnp.bfloat16),
            pltpu.VMEM((blocks, by + 2 * EDGE, nz), jnp.float32),
            pltpu.VMEM((n, cy, nz), jnp.bfloat16),
            pltpu.VMEM((ngy, cy, nz), jnp.bfloat16),
            pltpu.VMEM((n, cy // 2, nz), jnp.float32),
            pltpu.VMEM((lx, ly, nz), jnp.int32),
            pltpu.VMEM((1, by, nz), jnp.bfloat16),
            pltpu.VMEM((lx, ly, nz), jnp.bfloat16),
            pltpu.VMEM((1, by, nz), jnp.float32),
            pltpu.VMEM((1, cy, nz), jnp.bfloat16),
            pltpu.VMEM((1, cy, nz), jnp.bfloat16),
            pltpu.VMEM((1, cy // 2, nz), jnp.float32),
            pltpu.VMEM((8, max(2 * (by + 2 * EDGE), 2 * counts[2][1], 2 * (cy + 2 * EDGE)), nz), jnp.float32),
            pltpu.VMEM((2 * blocks, by + 2 * EDGE, nz), jnp.float32),
            pltpu.VMEM((blocks, cy + 2 * EDGE, nz), jnp.float32),
        ]
        scratch += level_scratch(3 * lx, ly + 2 * EDGE, True)
        scratch += level_scratch(2 * blocks, by + 2 * EDGE)
        for l in range(2, LEVELS + 1):
            scratch += level_scratch(counts[l][0], max(counts[l][1], EDGE))
        scratch += [pltpu.SemaphoreType.DMA((9,))] * 4
        scratch += [pltpu.SemaphoreType.DMA((3 * blocks,))] * 4
        scratch += [pltpu.SemaphoreType.DMA((2,))] * 2
        scratch += [pltpu.SemaphoreType.DMA((1,)), pltpu.SemaphoreType.DMA((ngy,)), pltpu.SemaphoreType.DMA((2,))]
        anywhere = pl.BlockSpec(memory_space=pl.ANY)
        inside = pl.BlockSpec(memory_space=pltpu.VMEM)
        right_side, phase = [pltpu.with_memory_space_constraint(x, pltpu.HBM) for x in (right_side, phase)]
        found = pl.pallas_call(
            functools.partial(kernel, ngx, ngy, counts),
            out_shape=[pltpu.VMEM(right_side.shape, jnp.float32)] * 2,
            in_specs=[anywhere] * 2,
            out_specs=[inside] * 2,
            scratch_shapes=scratch,
            compiler_params=pltpu.CompilerParams(
                collective_id=0, has_side_effects=True, vmem_limit_bytes=64_000_000
            ),
        )(right_side, phase)
        return pl.pallas_call(
            write,
            out_shape=[jax.ShapeDtypeStruct(right_side.shape, jnp.float32)] * 2,
            in_specs=[inside] * 2,
            out_specs=[anywhere] * 2,
            scratch_shapes=[pltpu.SemaphoreType.DMA((2,))],
        )(*[pltpu.with_memory_space_constraint(x, pltpu.VMEM) for x in found])

    placed = P("gx", "gy", None)
    return jax.shard_map(
        on_device, mesh=mesh, in_specs=(placed, placed), out_specs=(placed, placed), check_vma=False
    )
```

```python
import functools

import jax
import jax.numpy as jnp
import numpy as np
from jax import lax
from jax.experimental import pallas as pl
from jax.experimental.pallas import tpu as pltpu
from jax.sharding import PartitionSpec as P

LEVELS = 6
NU = 2
COARSE_SWEEPS = 6
OMEGA = 0.8
LIQUID, GAS = 1.0, 1000.0
MIXED = float(np.asarray(2.0 * LIQUID * GAS / (LIQUID + GAS), jnp.bfloat16))
MESH = pl.DeviceIdType.MESH
REACH = 3
HALO = 6
EDGE = 8
EDGE_PHASE = 16
UNROLL = 16
LARGE = 1 << 20


def each(count, body):
    if count <= UNROLL:
        for i in range(count):
            body(i)
    else:
        lax.fori_loop(0, count, lambda i, carry: (body(i), carry)[1], 0)


def index_along(shape, axis):
    return lax.broadcasted_iota(jnp.int32, shape, axis)


def roll(x, shift, axis):
    return pltpu.roll(x, shift % x.shape[axis], axis)


def lane_bit(x, step):
    return index_along(x.shape, x.ndim - 1) // step % 2


def even_part(x, step):
    return jnp.where(lane_bit(x, step) == 0, x, roll(x, step, x.ndim - 1))


def odd_part(x, step):
    return jnp.where(lane_bit(x, step) == 1, x, roll(x, -step, x.ndim - 1))


def pair_lanes(x, step):
    axis = x.ndim - 1
    return x + jnp.where(lane_bit(x, step) == 0, roll(x, -step, axis), roll(x, step, axis))


def harmonic(a, b):
    low, high = jnp.minimum(a, b), jnp.maximum(a, b)
    return jnp.where((low == 0.0) | (low == high), high, MIXED)


def store(ref, i, value):
    ref[i] = value.astype(ref.dtype)


def wide(ref, i):
    return ref[i].astype(jnp.float32)


def quarter(x):
    return (0.25 * x).astype(jnp.bfloat16).astype(jnp.float32)


def kernel(ngx, ngy, counts, f_hbm, phase_hbm, scaled_ref, rest_ref, *refs):
    gx, gy = lax.axis_index("gx"), lax.axis_index("gy")
    n = ngx * ngy
    me = gx * ngy + gy
    lx, ly, nz = f_hbm.shape
    by, cy = ly // 2, ly // 4
    refs = list(refs)

    def take(count):
        out = refs[:count]
        del refs[:count]
        return out

    (w0, wn, wc, wp, w1, wh, gf, gt, g2) = take(9)
    (phase_ref, p_pack, f_pack, c_pack, g1_pack, h_pack, f2_pack, t_pack, g2_pack, temp) = take(10)
    (b1, e2) = take(2)
    level_refs = [take(10) for _ in range(LEVELS + 1)]
    (s0, r0, s1, r1, sp, rp, sg, rg, st, rt, si) = take(11)

    own_f = w0.at[pl.ds(HALO, lx), pl.ds(EDGE, ly), :]
    load_phase = pltpu.make_async_copy(phase_hbm, phase_ref, si.at[0])
    load_f = pltpu.make_async_copy(f_hbm, own_f, si.at[1])
    load_phase.start()
    load_f.start()

    for start in (0, EDGE + ly):
        w0[:, pl.ds(start, EDGE), :] = jnp.zeros((w0.shape[0], EDGE, nz), w0.dtype)
    for ref in (wn, wc, wp, w1, wh):
        ref[...] = jnp.zeros(ref.shape, ref.dtype)

    barrier = pltpu.get_barrier_semaphore()

    def greet(k, carry):
        other = (me + k) % n
        pl.semaphore_signal(barrier, inc=1, device_id=(other // ngy, other % ngy), device_id_type=MESH)
        return carry

    lax.fori_loop(1, n, greet, 0)

    for l in range(LEVELS + 1):
        for v in level_refs[l][:2]:
            zero = jnp.zeros(v.shape[1:], v.dtype)
            v[0] = zero
            v[v.shape[0] - 1] = zero

    load_phase.wait()
    for plane in range(0, lx, 4):
        beta = [
            jnp.where(phase_ref[plane + 2 * k, pl.ds(0, by, 2), :] == 1, GAS, LIQUID) for k in range(2)
        ]
        p_pack[0] = jnp.where(lane_bit(beta[0], 1) == 0, beta[0], beta[1]).astype(jnp.bfloat16)
    load_f.wait()
    f_pack[...] = own_f[...].astype(jnp.bfloat16)
    for side, start in enumerate((EDGE, ly)):
        for k in range(lx // 2):
            rows = [w0[HALO + 2 * k + i, pl.ds(start, EDGE), :] for i in range(2)]
            c_pack[side, k] = jnp.concatenate(rows, axis=0).astype(c_pack.dtype)

    pl.semaphore_wait(barrier, n - 1)

    def window_copy(src, dst, send, recv, reach, edge, d, e, to):
        lead, rows = src.shape[0], src.shape[1]
        count = rows if e == 0 else edge
        source = src.at[:, pl.ds(rows - edge if e == 1 else 0, count), :]
        start = {0: edge, 1: 0, -1: edge + rows}[e]
        target = dst.at[pl.ds((reach - d) * lead, lead), pl.ds(start, count), :]
        k = (d + reach) * 3 + e + 1
        return pltpu.make_async_remote_copy(
            src_ref=source, dst_ref=target, send_sem=send.at[k], recv_sem=recv.at[k],
            device_id=(gx + to * d, gy + to * e), device_id_type=MESH,
        )

    def source_copy(d, e, to):
        if e == 0 and abs(d) > 1:
            source, target = h_pack, wh.at[pl.ds(REACH - d, 1)]
        else:
            return window_copy(g1_pack, w1, s1, r1, REACH, EDGE, d, e, to)
        k = (d + REACH) * 3 + e + 1
        return pltpu.make_async_remote_copy(
            src_ref=source, dst_ref=target, send_sem=s1.at[k], recv_sem=r1.at[k],
            device_id=(gx + to * d, gy + to * e), device_id_type=MESH,
        )

    def phase_copy(d, e, to):
        return window_copy(p_pack, wp, sp, rp, REACH, EDGE_PHASE, d, e, to)

    def f_copy(d, e, to):
        first, count = {0: (0, lx), 1: (0, lx), -1: (0, lx), 2: (lx - 2, 2), -2: (0, 2)}[d]
        low = {0: 0, 1: HALO - lx, 2: 0, -1: HALO, -2: HALO + lx}[d]
        side = 0 if e == 1 else 1
        if d == 0:
            source = own_f.at[:, pl.ds(ly - EDGE if e == 1 else 0, EDGE), :]
            target = w0.at[pl.ds(HALO, lx), pl.ds(0 if e == 1 else EDGE + ly, EDGE), :]
        elif e == 0:
            source, target = f_pack.at[pl.ds(first, count)], wn.at[pl.ds(low, count)]
        else:
            source = c_pack.at[1 - side, pl.ds(first // 2, count // 2)]
            target = wc.at[side, pl.ds(low // 2, count // 2)]
        k = (d + 2) * 3 + e + 1
        return pltpu.make_async_remote_copy(
            src_ref=source, dst_ref=target, send_sem=s0.at[k], recv_sem=r0.at[k],
            device_id=(gx + to * d, gy + to * e), device_id_type=MESH,
        )

    def each_near(low, high, body, near=None, to=1):
        for e in (0, 1, -1):
            for d in sorted(range(-high, high + 1), key=abs):
                if (d, e) != (0, 0) and (abs(d) >= low or (near is not None and e != 0)):
                    x, y = gx + to * d, gy + to * e
                    pl.when((x >= 0) & (x < ngx) & (y >= 0) & (y < ngy))(functools.partial(body, d, e))

    def window_send(copy, low, high, near=None):
        each_near(low, high, lambda d, e: copy(d, e, 1).start(), near)

    def window_wait(copy, low, high, near=None):
        each_near(low, high, lambda d, e: copy(d, e, -1).wait_recv(), near, -1)

    def window_done(copy, low, high, near=None):
        each_near(low, high, lambda d, e: copy(d, e, 1).wait_send(), near)

    def gather_send(src, dst, k):
        def body(t, carry):
            other = (me + t) % n
            pltpu.make_async_remote_copy(
                src_ref=src, dst_ref=dst.at[pl.ds(me, 1)], send_sem=sg.at[k], recv_sem=rg.at[k],
                device_id=(other // ngy, other % ngy), device_id_type=MESH,
            ).start()
            return carry

        lax.fori_loop(1, n, body, 0)

    def gather_all(dst, k):
        every = dst.at[pl.ds(0, n - 1)]
        return pltpu.make_async_remote_copy(
            src_ref=every, dst_ref=every, send_sem=sg.at[k], recv_sem=rg.at[k],
            device_id=(gx, (gy + 1) % ngy), device_id_type=MESH,
        )

    def top_copy(j, other):
        return pltpu.make_async_remote_copy(
            src_ref=t_pack, dst_ref=gt.at[pl.ds(j, 1)], send_sem=st.at[0], recv_sem=rt.at[j],
            device_id=(other // ngy, other % ngy), device_id_type=MESH,
        )

    window_send(phase_copy, 0, 2)
    window_send(f_copy, 0, 2)
    wp[REACH, pl.ds(EDGE_PHASE, by), :] = p_pack[0]

    slots = temp.shape[0]

    def stretch(value, slot):
        rows = value.shape[0]
        temp[slot, pl.ds(0, rows, 2), :] = value
        temp[slot, pl.ds(1, rows, 2), :] = value

    def pair_rows(value, slot, first=True, second=True):
        rows = value.shape[0]
        temp[slot, pl.ds(0, rows), :] = value
        out = 0.0
        if first:
            out = out + temp[slot, pl.ds(0, rows // 2, 2), :]
        if second:
            out = out + temp[slot, pl.ds(1, rows // 2, 2), :]
        return out

    def neighbours(level, v_ref, i, step):
        (_, _, _, _, _, fx, fyl, fyh, fzl, fzh) = level
        v = v_ref[i + 1]
        return (
            wide(fx, i) * v_ref[i] + wide(fx, i + 1) * v_ref[i + 2]
            + wide(fyl, i) * roll(v, 1, 0) + wide(fyh, i) * roll(v, -1, 0)
            + wide(fzl, i) * roll(v, step, 1) + wide(fzh, i) * roll(v, -step, 1)
        )

    def sweep(level, source, target, step, first, last):
        f, inverse = level[2], level[3]

        def body(k):
            i = k + first
            target[i + 1] = (1.0 - OMEGA) * source[i + 1] + inverse[i] * (f[i] + neighbours(level, source, i, step))

        each(last - first, body)

    def rest_of(level, v_ref, i, step):
        return level[2][i] - level[4][i] * v_ref[i + 1] + neighbours(level, v_ref, i, step)

    def put_faces(level, i, inside, lows, step, edges):
        (_, _, _, inverse, centre, fx, fyl, fyh, fzl, fzh) = level
        (yl, yh, zl, zh) = lows
        total = wide(fx, i) + wide(fx, i + 1) + yl + yh + zl + zh
        inverse[i] = jnp.where(inside, OMEGA / jnp.where(inside, total, 1.0), 0.0)
        centre[i] = total
        lane = index_along(zl.shape, 1)
        fzl[i] = jnp.where(lane < step, 0.0, zl).astype(fzl.dtype)
        fzh[i] = jnp.where(lane >= nz - step, 0.0, zh).astype(fzh.dtype)
        if edges is not None:
            row = index_along(yl.shape, 0)
            yl = jnp.where(row == 0, 0.0, yl)
            yh = jnp.where(row >= edges - 1, 0.0, yh)
        fyl[i] = yl.astype(fyl.dtype)
        fyh[i] = yh.astype(fyh.dtype)

    def cell_faces(b, step):
        lane = index_along(b.shape, 1)
        yl, yh = harmonic(roll(b, 1, 0), b), harmonic(b, roll(b, -1, 0))
        zl = harmonic(jnp.where(lane < step, 0.0, roll(b, step, 1)), b)
        zh = harmonic(b, jnp.where(lane >= nz - step, 0.0, roll(b, -step, 1)))
        return yl, yh, zl, zh

    def phase_block(t):
        packed = wp[t].astype(jnp.float32)[EDGE_PHASE - EDGE : EDGE_PHASE + by + EDGE]
        b1[2 * t] = even_part(packed, 1)
        b1[2 * t + 1] = odd_part(packed, 1)

    window_wait(phase_copy, 0, 2)
    for t in range(REACH - 2, REACH + 3):
        phase_block(t)

    level0 = list(level_refs[0])
    level0[2] = w0
    (va, vb, f0, inv0, c0, fx0) = level0[:6]
    rows0 = ly + 2 * EDGE
    planes0 = lx + 2 * HALO
    blocks = planes0 // 2
    own1 = 2 * REACH
    first_block = own1 - HALO // 2

    def fine_beta(j):
        slot = (j + 1) % slots
        stretch(b1[first_block + j], slot)
        return temp[slot, pl.ds(EDGE, rows0), :]

    def fine_faces(j):
        lows = cell_faces(beta0[j], 1)
        for i in (2 * j, 2 * j + 1):
            put_faces(level0, i, beta0[j] > 0.0, lows, 1, None)

    beta0 = [fine_beta(j) for j in range(-1, blocks + 1)]
    for j in range(blocks + 1):
        fx0[2 * j] = harmonic(beta0[j], beta0[j + 1])
        if j < blocks:
            fx0[2 * j + 1] = beta0[j + 1]
    beta0 = beta0[1:-1]
    for j in range(blocks):
        fine_faces(j)

    level1 = level_refs[1]
    (ua, ub, f1, inv1, c1, fx1) = level1[:6]
    planes1 = 2 * (2 * REACH + 1)
    near = range(own1 - 2, own1 + 4)

    def own_faces():
        own = slice(EDGE, EDGE + by)
        below, low, high, above = [b1[own1 + k] for k in range(-1, 3)]
        lane = index_along((by, nz), 1)
        pair = [low, high]
        mine = [b[own] for b in pair]
        x_low = quarter(pair_lanes(pair_rows(harmonic(below, low)[own], 0), 2))
        x_high = quarter(pair_lanes(pair_rows(harmonic(high, above)[own], 1), 2))
        y_low = sum(harmonic(roll(b, 1, 0), b)[own] for b in pair)
        y_high = sum(harmonic(b, roll(b, -1, 0))[own] for b in pair)
        z_low = sum(harmonic(jnp.where(lane < 2, 0.0, roll(b, 2, 1)), b) for b in mine)
        z_high = sum(harmonic(b, jnp.where(lane >= nz - 2, 0.0, roll(b, -2, 1))) for b in mine)
        y_low = quarter(pair_lanes(pair_rows(y_low, 2, second=False), 2))
        y_high = quarter(pair_lanes(pair_rows(y_high, 3, first=False), 2))
        z_low = quarter(even_part(pair_rows(z_low, 4), 2))
        z_high = quarter(odd_part(pair_rows(z_high, 5), 2))
        row, lane = index_along((cy, nz), 0), index_along((cy, nz), 1)
        corner = (row == cy - 2) & (lane // 4 == nz // 4 - 2)
        edge = jnp.where(corner, roll(roll(z_high, -1, 0), -4, 1), z_high)
        edge = jnp.where(row == cy - 1, y_high, edge)
        mixed = edge
        for k, value in enumerate((x_low, y_low, z_low)):
            mixed = jnp.where(lane % 4 == k, value, mixed)
        f2_pack[0] = mixed.astype(f2_pack.dtype)
        t_pack[0] = x_high.astype(t_pack.dtype)

    own_faces()
    gather_send(f2_pack, gf, 0)
    gf[me] = f2_pack[0]
    for j in range(ngy):
        @pl.when((gx == ngx - 1) & (gy == j))
        def _():
            def body(t, carry):
                top_copy(j, (me + t) % n).start()
                return carry

            lax.fori_loop(1, n, body, 0)
            gt[j] = t_pack[0]
    window_send(phase_copy, REACH, REACH)

    for i in range(near[0], near[-1] + 2):
        fx1[i] = harmonic(b1[i - 1], b1[i])
    for i in near:
        put_faces(level1, i, b1[i] > 0.0, cell_faces(b1[i], 2), 2, None)

    for i in near:
        f1[i] = jnp.zeros(f1.shape[1:], f1.dtype)

    window_wait(f_copy, 0, 2)
    for i in range(2 * HALO):
        plane = i if i < HALO else i + lx
        w0[plane, pl.ds(EDGE, ly), :] = wn[i].astype(w0.dtype)
    for i in range(HALO):
        for side, start in enumerate((0, EDGE + ly)):
            rows = wc[side, i].astype(w0.dtype)
            plane = 2 * i if 2 * i < HALO else 2 * i + lx
            w0[plane, pl.ds(start, EDGE), :] = rows[:EDGE]
            w0[plane + 1, pl.ds(start, EDGE), :] = rows[EDGE:]
    for i in range(planes0):
        va[i + 1] = inv0[i] * w0[i]
    sweep(level0, va, vb, 1, 1, planes0 - 1)

    def source_plane(k):
        plane = 2 * (near[0] + k - first_block)
        r = rest_of(level0, vb, plane, 1) + rest_of(level0, vb, plane + 1, 1)
        f1[near[0] + k, pl.ds(EDGE // 2, rows0 // 2), :] = 0.5 * pair_lanes(pair_rows(r, k % slots), 1)

    for k in range(len(near)):
        source_plane(k)
    coarse = [f1[own1 + k, pl.ds(EDGE, by), :] for k in range(2)]
    packed = jnp.where(lane_bit(coarse[0], 1) == 0, coarse[0], coarse[1])
    g1_pack[0] = packed
    h_pack[0] = packed.astype(h_pack.dtype)
    window_send(source_copy, 2, REACH, True)

    for i in near:
        ua[i + 1] = inv1[i] * f1[i]
    sweep(level1, ua, ub, 2, near[0] + 1, near[-1])
    rests = [rest_of(level1, ub, own1 + i, 2)[EDGE : EDGE + by] for i in range(2)]
    coarse = 0.5 * pair_lanes(pair_rows(rests[0] + rests[1], 0), 2)
    half = cy // 2
    packed = jnp.where(lane_bit(coarse[:half], 1) == 0, coarse[:half], coarse[half:])
    g2_pack[0] = packed
    gather_send(g2_pack, g2, 1)
    g2[me] = packed

    window_wait(phase_copy, REACH, REACH)
    phase_block(0)
    phase_block(2 * REACH)
    far = [i for i in range(1, planes1 - 1) if i not in near]
    for i in range(1, planes1):
        if not near[0] <= i <= near[-1] + 1:
            fx1[i] = harmonic(b1[i - 1], b1[i])
    for i in far:
        put_faces(level1, i, b1[i] > 0.0, cell_faces(b1[i], 2), 2, None)

    gather_all(gf, 0).wait_recv()
    for j in range(ngy):
        @pl.when((gx < ngx - 1) | (gy != j))
        def _():
            top_copy(j, me).wait_recv()

    shape2 = counts[2]
    (nx2, ny2) = shape2
    level2 = level_refs[2]
    raw = level2[6:10]
    pick = (index_along((nz, 4 * nz), 0) == index_along((nz, 4 * nz), 1) % nz // 4 * 4 + index_along((nz, 4 * nz), 1) // nz)
    pick = jnp.where(pick, 1.0, 0.0).astype(jnp.bfloat16)

    def whole_plane(ref, k):
        return jnp.concatenate([ref[k * ngy + j].astype(jnp.float32) for j in range(ngy)], axis=0)

    def spread(x, columns):
        return jnp.dot(x.astype(jnp.bfloat16), columns, preferred_element_type=jnp.float32)

    def faces2(i):
        parts = spread(whole_plane(gf, i), pick)
        x_low, y_low, z_low, edge = [parts[:, k * nz : (k + 1) * nz] for k in range(4)]
        row, lane = index_along((ny2, nz), 0), index_along((ny2, nz), 1)
        y_high = jnp.where(row == ny2 - 1, edge, roll(y_low, -1, 0))
        z_edge = jnp.where(row % cy == cy - 1, roll(roll(edge, 1, 0), 4, 1), edge)
        z_high = jnp.where(lane >= nz - 4, z_edge, roll(z_low, -4, 1))
        store(level2[5], i, x_low)
        for ref, value in zip(raw, (y_low, y_high, z_low, z_high)):
            store(ref, i, value)

    each(nx2, faces2)
    store(level2[5], nx2, whole_plane(gt, 0))

    for l in range(2, LEVELS + 1):
        nx, ny = counts[l]
        step = 2**l
        level = level_refs[l]
        if l < LEVELS:
            finer, coarser = level_refs[l], level_refs[l + 1]
            size = max(ny // 2, 4)
            if ny // 2 < EDGE:
                for ref in coarser[5:10]:
                    ref[...] = jnp.zeros(ref.shape, ref.dtype)

            def put(ref, i, value):
                ref[i, pl.ds(0, size), :] = quarter(value).astype(ref.dtype)

            def coarsen(i):
                slot = 4 * (i % 2)
                (fx, yl, yh, zl, zh) = finer[5:10]
                a, b = 2 * i, 2 * i + 1
                put(coarser[5], i, pair_lanes(pair_rows(wide(fx, a), slot), step))
                put(coarser[6], i, pair_lanes(pair_rows(wide(yl, a) + wide(yl, b), slot + 1, second=False), step))
                put(coarser[7], i, pair_lanes(pair_rows(wide(yh, a) + wide(yh, b), slot + 2, first=False), step))
                put(coarser[8], i, even_part(pair_rows(wide(zl, a) + wide(zl, b), slot + 3), step))
                put(coarser[9], i, odd_part(pair_rows(wide(zh, a) + wide(zh, b), slot), step))

            each(nx // 2, coarsen)
            put(coarser[5], nx // 2, pair_lanes(pair_rows(wide(finer[5], nx), 5), step))

        def finish(i):
            lows = [wide(ref, i) for ref in level[6:10]]
            inside = index_along(lows[0].shape, 0) < ny
            put_faces(level, i, inside, lows, step, ny)

        each(nx, finish)

    window_wait(source_copy, 2, REACH, True)
    for t in range(2 * REACH + 1):
        for k, part in enumerate((even_part, odd_part)):
            i = 2 * t + k
            if abs(t - REACH) > 1:
                f1[i] = part(w1[t], 1)
                f1[i, pl.ds(EDGE, by), :] = part(wh[t].astype(jnp.float32), 1)
            else:
                for start in (0, EDGE + by):
                    f1[i, pl.ds(start, EDGE), :] = part(w1[t, pl.ds(start, EDGE), :], 1)
    for i in range(1, planes1 - 1):
        ua[i + 1] = inv1[i] * f1[i]
    sweep(level1, ua, ub, 2, 2, planes1 - 2)

    gather_all(g2, 1).wait_recv()

    f2 = level2[2]

    def unpack(i):
        parts = []
        for j in range(ngy):
            pack = g2[i * ngy + j]
            parts += [even_part(pack, 1), odd_part(pack, 1)]
        f2[i] = jnp.concatenate(parts, axis=0)

    each(nx2, unpack)

    def cycle(l):
        nx, ny = counts[l]
        step = 2**l
        level = level_refs[l]
        (xa, xb, f, inverse) = level[:4]

        def begin(i):
            xa[i + 1] = inverse[i] * f[i]

        each(nx, begin)
        if l == LEVELS:
            for repeat in range(COARSE_SWEEPS - 1):
                sweep(level, xa, xb, step, 0, nx)
                xa, xb = xb, xa
            return xa
        for repeat in range(NU - 1):
            sweep(level, xa, xb, step, 0, nx)
            xa, xb = xb, xa
        f_next = level_refs[l + 1][2]
        size = max(ny // 2, 4)
        if ny // 2 < EDGE:
            f_next[...] = jnp.zeros(f_next.shape, f_next.dtype)

        def restrict(i):
            r = rest_of(level, xa, 2 * i, step) + rest_of(level, xa, 2 * i + 1, step)
            f_next[i, pl.ds(0, size), :] = 0.5 * pair_lanes(pair_rows(r, i % slots), step)

        each(nx // 2, restrict)
        fine = cycle(l + 1)

        def correct(i):
            slot = i % slots
            stretch(fine[i + 1], slot)
            e = temp[slot, pl.ds(0, xa.shape[1]), :]
            xb[2 * i + 1] = xa[2 * i + 1] + e
            xb[2 * i + 2] = xa[2 * i + 2] + e

        each(nx // 2, correct)
        xa, xb = xb, xa
        for repeat in range(NU):
            sweep(level, xa, xb, step, 0, nx)
            xa, xb = xb, xa
        return xa

    found = cycle(2)

    row2 = pl.multiple_of(gy * cy, 8)
    below2 = pl.multiple_of(jnp.maximum(gy * cy - EDGE, 0), 8)
    above2 = pl.multiple_of(jnp.minimum(gy * cy + cy, ny2 - EDGE), 8)
    for t in range(1, 2 * REACH):
        x = gx + t - REACH
        there = (x >= 0) & (x < nx2)
        plane = jnp.clip(x, 0, nx2 - 1) + 1
        e2[t, pl.ds(EDGE, cy), :] = jnp.where(there, found[plane, pl.ds(row2, cy), :], 0.0)
        low = found[plane, pl.ds(below2, EDGE), :]
        high = found[plane, pl.ds(above2, EDGE), :]
        e2[t, pl.ds(0, EDGE), :] = jnp.where(there & (gy > 0), low, 0.0)
        e2[t, pl.ds(EDGE + cy, EDGE), :] = jnp.where(there & (gy < ngy - 1), high, 0.0)

    for t in range(1, 2 * REACH):
        slot = t % slots
        stretch(e2[t], slot)
        e = temp[slot, pl.ds(EDGE, by + 2 * EDGE), :]
        ua[2 * t + 1] = ub[2 * t + 1] + e
        ua[2 * t + 2] = ub[2 * t + 2] + e
    sweep(level1, ua, ub, 2, 3, planes1 - 3)
    sweep(level1, ub, ua, 2, 4, planes1 - 4)

    for j in range(1, blocks - 1):
        slot = j % slots
        stretch(ua[first_block + j + 1], slot)
        e = temp[slot, pl.ds(EDGE, rows0), :]
        va[2 * j + 1] = vb[2 * j + 1] + e
        va[2 * j + 2] = vb[2 * j + 2] + e
    sweep(level0, va, vb, 1, HALO - 2, HALO + lx + 2)
    sweep(level0, vb, va, 1, HALO - 1, HALO + lx + 1)
    for i in range(lx):
        k = HALO + i
        product = c0[k] * va[k + 1]
        near_sum = neighbours(level0, va, k, 1)
        own = slice(EDGE, EDGE + ly)
        scaled_ref[i] = product[own]
        rest_ref[i] = w0[k, pl.ds(EDGE, ly), :] - product[own] + near_sum[own]

    window_done(phase_copy, 0, REACH)
    window_done(f_copy, 0, 2)
    window_done(source_copy, 2, REACH, True)
    gather_all(gf, 0).wait_send()
    gather_all(g2, 1).wait_send()

    @pl.when(gx == ngx - 1)
    def _():
        every = gf.at[pl.ds(0, n - 1)]
        pltpu.make_async_remote_copy(
            src_ref=every, dst_ref=every, send_sem=st.at[0], recv_sem=rt.at[0],
            device_id=(gx, (gy + 1) % ngy), device_id_type=MESH,
        ).wait_send()


def write(scaled_ref, rest_ref, scaled_out, rest_out, sems):
    copies = [
        pltpu.make_async_copy(source, target, sems.at[k])
        for k, (source, target) in enumerate(((scaled_ref, scaled_out), (rest_ref, rest_out)))
    ]
    for copy in copies:
        copy.start()
    for copy in copies:
        copy.wait()


def solution(mesh):
    ngx, ngy = mesh.shape["gx"], mesh.shape["gy"]
    n = ngx * ngy

    def on_device(right_side, phase):
        lx, ly, nz = right_side.shape
        assert lx == 4 and ly % 32 == 0 and NU == 2
        by, cy = ly // 2, ly // 4
        counts = [(lx * ngx >> l, ly * ngy >> l) for l in range(LEVELS + 1)]
        blocks = 2 * REACH + 1

        def level_scratch(planes, rows, padded_source=False):
            shapes = [planes + 2, planes + 2, planes, planes, planes, planes + 1] + [planes] * 4
            if padded_source:
                shapes[2] = 1
            large = planes * rows * nz * 4 >= LARGE
            types = [jnp.float32] * 5 + [jnp.bfloat16 if large else jnp.float32] * 5
            return [pltpu.VMEM((k, rows, nz), dtype) for k, dtype in zip(shapes, types)]

        scratch = [
            pltpu.VMEM((lx + 2 * HALO, ly + 2 * EDGE, nz), jnp.float32),
            pltpu.VMEM((2 * HALO, ly, nz), jnp.bfloat16),
            pltpu.VMEM((2, HALO, 2 * EDGE, nz), jnp.bfloat16),
            pltpu.VMEM((blocks, by + 2 * EDGE_PHASE, nz), jnp.bfloat16),
            pltpu.VMEM((blocks, by + 2 * EDGE, nz), jnp.float32),
            pltpu.VMEM((blocks, by, nz), jnp.bfloat16),
            pltpu.VMEM((n, cy, nz), jnp.bfloat16),
            pltpu.VMEM((ngy, cy, nz), jnp.bfloat16),
            pltpu.VMEM((n, cy // 2, nz), jnp.float32),
            pltpu.VMEM((lx, ly, nz), jnp.int32),
            pltpu.VMEM((1, by, nz), jnp.bfloat16),
            pltpu.VMEM((lx, ly, nz), jnp.bfloat16),
            pltpu.VMEM((2, lx // 2, 2 * EDGE, nz), jnp.bfloat16),
            pltpu.VMEM((1, by, nz), jnp.float32),
            pltpu.VMEM((1, by, nz), jnp.bfloat16),
            pltpu.VMEM((1, cy, nz), jnp.bfloat16),
            pltpu.VMEM((1, cy, nz), jnp.bfloat16),
            pltpu.VMEM((1, cy // 2, nz), jnp.float32),
            pltpu.VMEM((8, max(2 * (by + 2 * EDGE), 2 * counts[2][1], 2 * (cy + 2 * EDGE)), nz), jnp.float32),
            pltpu.VMEM((2 * blocks, by + 2 * EDGE, nz), jnp.float32),
            pltpu.VMEM((blocks, cy + 2 * EDGE, nz), jnp.float32),
        ]
        scratch += level_scratch(lx + 2 * HALO, ly + 2 * EDGE, True)
        scratch += level_scratch(2 * blocks, by + 2 * EDGE)
        for l in range(2, LEVELS + 1):
            scratch += level_scratch(counts[l][0], max(counts[l][1], EDGE))
        scratch += [pltpu.SemaphoreType.DMA((15,))] * 2
        scratch += [pltpu.SemaphoreType.DMA((3 * blocks,))] * 4
        scratch += [pltpu.SemaphoreType.DMA((2,))] * 2
        scratch += [pltpu.SemaphoreType.DMA((1,)), pltpu.SemaphoreType.DMA((ngy,)), pltpu.SemaphoreType.DMA((2,))]
        anywhere = pl.BlockSpec(memory_space=pl.ANY)
        inside = pl.BlockSpec(memory_space=pltpu.VMEM)
        right_side, phase = [pltpu.with_memory_space_constraint(x, pltpu.HBM) for x in (right_side, phase)]
        found = pl.pallas_call(
            functools.partial(kernel, ngx, ngy, counts),
            out_shape=[pltpu.VMEM(right_side.shape, jnp.float32)] * 2,
            in_specs=[anywhere] * 2,
            out_specs=[inside] * 2,
            scratch_shapes=scratch,
            compiler_params=pltpu.CompilerParams(
                collective_id=0, has_side_effects=True, vmem_limit_bytes=64_000_000
            ),
        )(right_side, phase)
        return pl.pallas_call(
            write,
            out_shape=[jax.ShapeDtypeStruct(right_side.shape, jnp.float32)] * 2,
            in_specs=[inside] * 2,
            out_specs=[anywhere] * 2,
            scratch_shapes=[pltpu.SemaphoreType.DMA((2,))],
        )(*[pltpu.with_memory_space_constraint(x, pltpu.VMEM) for x in found])

    placed = P("gx", "gy", None)
    return jax.shard_map(
        on_device, mesh=mesh, in_specs=(placed, placed), out_specs=(placed, placed), check_vma=False
    )
```

```python
import functools

import jax
import jax.numpy as jnp
import numpy as np
from jax import lax
from jax.experimental import pallas as pl
from jax.experimental.pallas import tpu as pltpu
from jax.sharding import PartitionSpec as P

LEVELS = 6
NU = 2
COARSE_SWEEPS = 6
OMEGA = 0.8
LIQUID, GAS = 1.0, 1000.0
MIXED = float(np.asarray(2.0 * LIQUID * GAS / (LIQUID + GAS), jnp.bfloat16))
MESH = pl.DeviceIdType.MESH
REACH = 3
HALO = 6
EDGE = 8
EDGE_PHASE = 16
UNROLL = 16
LARGE = 1 << 20


def each(count, body):
    if count <= UNROLL:
        for i in range(count):
            body(i)
    else:
        lax.fori_loop(0, count, lambda i, carry: (body(i), carry)[1], 0)


def index_along(shape, axis):
    return lax.broadcasted_iota(jnp.int32, shape, axis)


def roll(x, shift, axis):
    return pltpu.roll(x, shift % x.shape[axis], axis)


def lane_bit(x, step):
    return index_along(x.shape, x.ndim - 1) // step % 2


def even_part(x, step):
    return jnp.where(lane_bit(x, step) == 0, x, roll(x, step, x.ndim - 1))


def odd_part(x, step):
    return jnp.where(lane_bit(x, step) == 1, x, roll(x, -step, x.ndim - 1))


def pair_lanes(x, step):
    axis = x.ndim - 1
    return x + jnp.where(lane_bit(x, step) == 0, roll(x, -step, axis), roll(x, step, axis))


def harmonic(a, b):
    low, high = jnp.minimum(a, b), jnp.maximum(a, b)
    return jnp.where((low == 0.0) | (low == high), high, MIXED)


def store(ref, i, value):
    ref[i] = value.astype(ref.dtype)


def wide(ref, i):
    return ref[i].astype(jnp.float32)


def quarter(x):
    return (0.25 * x).astype(jnp.bfloat16).astype(jnp.float32)


def kernel(ngx, ngy, counts, f_hbm, phase_hbm, scaled_ref, rest_ref, *refs):
    gx, gy = lax.axis_index("gx"), lax.axis_index("gy")
    n = ngx * ngy
    me = gx * ngy + gy
    lx, ly, nz = f_hbm.shape
    by, cy = ly // 2, ly // 4
    refs = list(refs)

    def take(count):
        out = refs[:count]
        del refs[:count]
        return out

    (w0, wn, wc, wp, w1, wh, gf, gt, g2) = take(9)
    (phase_ref, p_pack, f_pack, c_pack, g1_pack, h_pack, f2_pack, t_pack, g2_pack, temp) = take(10)
    (b1, e2) = take(2)
    level_refs = [take(10) for _ in range(LEVELS + 1)]
    (s0, r0, s1, r1, sp, rp, sg, rg, st, rt, si, all_in) = take(12)

    own_f = w0.at[pl.ds(HALO, lx), pl.ds(EDGE, ly), :]
    load_phase = pltpu.make_async_copy(phase_hbm, phase_ref, si.at[0])
    load_f = pltpu.make_async_copy(f_hbm, own_f, si.at[1])
    load_phase.start()
    load_f.start()

    for start in (0, EDGE + ly):
        w0[:, pl.ds(start, EDGE), :] = jnp.zeros((w0.shape[0], EDGE, nz), w0.dtype)
    for ref in (wn, wc, wp, w1, wh):
        ref[...] = jnp.zeros(ref.shape, ref.dtype)

    barrier = pltpu.get_barrier_semaphore()

    m = max(k for k in range(1, ngx + 1) if ngx % k == 0 and k * k <= ngx)
    greeted = 0

    def greet(x, y, there):
        pl.when(there)(
            lambda: pl.semaphore_signal(barrier, inc=1, device_id=(x, y), device_id_type=MESH)
        )
        return greeted + jnp.where(there, 1, 0)

    mates = [(c * m + gx % m, gy, gx // m != c) for c in range(ngx // m)]
    for x, y, there in mates:
        greeted = greet(x, y, there & (jnp.abs(x - gx) > REACH))
    for e in (0, 1, -1):
        for d in range(-REACH, REACH + 1):
            if (d, e) != (0, 0):
                x, y = gx + d, gy + e
                greeted = greet(x, y, (x >= 0) & (x < ngx) & (y >= 0) & (y < ngy))
    for a in range(m):
        for y in range(ngy):
            x = gx // m * m + a
            column = (x == gx) & (y == gy)
            if m - 1 > REACH or ngy > 2:
                greeted = greet(x, y, ((jnp.abs(x - gx) > REACH) | (jnp.abs(y - gy) > 1)) & ~column)

    for l in range(LEVELS + 1):
        for v in level_refs[l][:2]:
            zero = jnp.zeros(v.shape[1:], v.dtype)
            v[0] = zero
            v[v.shape[0] - 1] = zero

    load_phase.wait()
    for plane in range(0, lx, 4):
        beta = [
            jnp.where(phase_ref[plane + 2 * k, pl.ds(0, by, 2), :] == 1, GAS, LIQUID) for k in range(2)
        ]
        p_pack[0] = jnp.where(lane_bit(beta[0], 1) == 0, beta[0], beta[1]).astype(jnp.bfloat16)
    load_f.wait()
    f_pack[...] = own_f[...].astype(jnp.bfloat16)
    for side, start in enumerate((EDGE, ly)):
        for k in range(lx // 2):
            rows = [w0[HALO + 2 * k + i, pl.ds(start, EDGE), :] for i in range(2)]
            c_pack[side, k] = jnp.concatenate(rows, axis=0).astype(c_pack.dtype)

    pl.semaphore_wait(barrier, greeted)

    def window_copy(src, dst, send, recv, reach, edge, d, e, to):
        lead, rows = src.shape[0], src.shape[1]
        count = rows if e == 0 else edge
        source = src.at[:, pl.ds(rows - edge if e == 1 else 0, count), :]
        start = {0: edge, 1: 0, -1: edge + rows}[e]
        target = dst.at[pl.ds((reach - d) * lead, lead), pl.ds(start, count), :]
        k = (d + reach) * 3 + e + 1
        return pltpu.make_async_remote_copy(
            src_ref=source, dst_ref=target, send_sem=send.at[k], recv_sem=recv.at[k],
            device_id=(gx + to * d, gy + to * e), device_id_type=MESH,
        )

    def source_copy(d, e, to):
        if e == 0 and abs(d) > 1:
            source, target = h_pack, wh.at[pl.ds(REACH - d, 1)]
        else:
            return window_copy(g1_pack, w1, s1, r1, REACH, EDGE, d, e, to)
        k = (d + REACH) * 3 + e + 1
        return pltpu.make_async_remote_copy(
            src_ref=source, dst_ref=target, send_sem=s1.at[k], recv_sem=r1.at[k],
            device_id=(gx + to * d, gy + to * e), device_id_type=MESH,
        )

    def phase_copy(d, e, to):
        return window_copy(p_pack, wp, sp, rp, REACH, EDGE_PHASE, d, e, to)

    def f_copy(d, e, to):
        first, count = {0: (0, lx), 1: (0, lx), -1: (0, lx), 2: (lx - 2, 2), -2: (0, 2)}[d]
        low = {0: 0, 1: HALO - lx, 2: 0, -1: HALO, -2: HALO + lx}[d]
        side = 0 if e == 1 else 1
        if d == 0:
            source = own_f.at[:, pl.ds(ly - EDGE if e == 1 else 0, EDGE), :]
            target = w0.at[pl.ds(HALO, lx), pl.ds(0 if e == 1 else EDGE + ly, EDGE), :]
        elif e == 0:
            source, target = f_pack.at[pl.ds(first, count)], wn.at[pl.ds(low, count)]
        else:
            source = c_pack.at[1 - side, pl.ds(first // 2, count // 2)]
            target = wc.at[side, pl.ds(low // 2, count // 2)]
        k = (d + 2) * 3 + e + 1
        return pltpu.make_async_remote_copy(
            src_ref=source, dst_ref=target, send_sem=s0.at[k], recv_sem=r0.at[k],
            device_id=(gx + to * d, gy + to * e), device_id_type=MESH,
        )

    def each_near(low, high, body, near=None, to=1):
        for e in (0, 1, -1):
            for d in sorted(range(-high, high + 1), key=abs):
                if (d, e) != (0, 0) and (abs(d) >= low or (near is not None and e != 0)):
                    x, y = gx + to * d, gy + to * e
                    pl.when((x >= 0) & (x < ngx) & (y >= 0) & (y < ngy))(functools.partial(body, d, e))

    def window_send(copy, low, high, near=None):
        each_near(low, high, lambda d, e: copy(d, e, 1).start(), near)

    def window_wait(copy, low, high, near=None):
        each_near(low, high, lambda d, e: copy(d, e, -1).wait_recv(), near, -1)

    def window_done(copy, low, high, near=None):
        each_near(low, high, lambda d, e: copy(d, e, 1).wait_send(), near)

    def gather_send(src, dst, k):
        def body(t, carry):
            other = jnp.where(t <= me, t - 1, t)
            pltpu.make_async_remote_copy(
                src_ref=src, dst_ref=dst.at[pl.ds(me, 1)], send_sem=sg.at[k], recv_sem=rg.at[k],
                device_id=(other // ngy, other % ngy), device_id_type=MESH,
            ).start()
            return carry

        lax.fori_loop(1, n, body, 0)

    def gather_all(dst, k):
        every = dst.at[pl.ds(0, n - 1)]
        return pltpu.make_async_remote_copy(
            src_ref=every, dst_ref=every, send_sem=sg.at[k], recv_sem=rg.at[k],
            device_id=(gx, (gy + 1) % ngy), device_id_type=MESH,
        )

    def top_copy(j, other):
        return pltpu.make_async_remote_copy(
            src_ref=t_pack, dst_ref=gt.at[pl.ds(j, 1)], send_sem=st.at[0], recv_sem=rt.at[j],
            device_id=(other // ngy, other % ngy), device_id_type=MESH,
        )

    window_send(phase_copy, 0, 2)
    window_send(f_copy, 0, 2)
    for x, y, there in mates:
        pl.when(there)(functools.partial(pl.semaphore_signal, all_in, inc=1, device_id=(x, y), device_id_type=MESH))
    wp[REACH, pl.ds(EDGE_PHASE, by), :] = p_pack[0]

    slots = temp.shape[0]

    def stretch(value, slot):
        rows = value.shape[0]
        temp[slot, pl.ds(0, rows, 2), :] = value
        temp[slot, pl.ds(1, rows, 2), :] = value

    def pair_rows(value, slot, first=True, second=True):
        rows = value.shape[0]
        temp[slot, pl.ds(0, rows), :] = value
        out = 0.0
        if first:
            out = out + temp[slot, pl.ds(0, rows // 2, 2), :]
        if second:
            out = out + temp[slot, pl.ds(1, rows // 2, 2), :]
        return out

    def neighbours(level, v_ref, i, step):
        (_, _, _, _, _, fx, fyl, fyh, fzl, fzh) = level
        v = v_ref[i + 1]
        return (
            wide(fx, i) * v_ref[i] + wide(fx, i + 1) * v_ref[i + 2]
            + wide(fyl, i) * roll(v, 1, 0) + wide(fyh, i) * roll(v, -1, 0)
            + wide(fzl, i) * roll(v, step, 1) + wide(fzh, i) * roll(v, -step, 1)
        )

    def sweep(level, source, target, step, first, last):
        f, inverse = level[2], level[3]

        def body(k):
            i = k + first
            target[i + 1] = (1.0 - OMEGA) * source[i + 1] + inverse[i] * (f[i] + neighbours(level, source, i, step))

        each(last - first, body)

    def rest_of(level, v_ref, i, step):
        return level[2][i] - level[4][i] * v_ref[i + 1] + neighbours(level, v_ref, i, step)

    def put_faces(level, i, inside, lows, step, edges):
        (_, _, _, inverse, centre, fx, fyl, fyh, fzl, fzh) = level
        (yl, yh, zl, zh) = lows
        total = wide(fx, i) + wide(fx, i + 1) + yl + yh + zl + zh
        inverse[i] = jnp.where(inside, OMEGA / jnp.where(inside, total, 1.0), 0.0)
        centre[i] = total
        lane = index_along(zl.shape, 1)
        fzl[i] = jnp.where(lane < step, 0.0, zl).astype(fzl.dtype)
        fzh[i] = jnp.where(lane >= nz - step, 0.0, zh).astype(fzh.dtype)
        if edges is not None:
            row = index_along(yl.shape, 0)
            yl = jnp.where(row == 0, 0.0, yl)
            yh = jnp.where(row >= edges - 1, 0.0, yh)
        fyl[i] = yl.astype(fyl.dtype)
        fyh[i] = yh.astype(fyh.dtype)

    def cell_faces(b, step):
        lane = index_along(b.shape, 1)
        yl, yh = harmonic(roll(b, 1, 0), b), harmonic(b, roll(b, -1, 0))
        zl = harmonic(jnp.where(lane < step, 0.0, roll(b, step, 1)), b)
        zh = harmonic(b, jnp.where(lane >= nz - step, 0.0, roll(b, -step, 1)))
        return yl, yh, zl, zh

    def phase_block(t):
        packed = wp[t].astype(jnp.float32)[EDGE_PHASE - EDGE : EDGE_PHASE + by + EDGE]
        b1[2 * t] = even_part(packed, 1)
        b1[2 * t + 1] = odd_part(packed, 1)

    window_wait(phase_copy, 0, 2)
    for t in range(REACH - 2, REACH + 3):
        phase_block(t)

    level0 = list(level_refs[0])
    level0[2] = w0
    (va, vb, f0, inv0, c0, fx0) = level0[:6]
    rows0 = ly + 2 * EDGE
    planes0 = lx + 2 * HALO
    blocks = planes0 // 2
    own1 = 2 * REACH
    first_block = own1 - HALO // 2

    def fine_beta(j):
        slot = (j + 1) % slots
        stretch(b1[first_block + j], slot)
        return temp[slot, pl.ds(EDGE, rows0), :]

    def fine_faces(j):
        lows = cell_faces(beta0[j], 1)
        for i in (2 * j, 2 * j + 1):
            put_faces(level0, i, beta0[j] > 0.0, lows, 1, None)

    beta0 = [fine_beta(j) for j in range(-1, blocks + 1)]
    for j in range(blocks + 1):
        fx0[2 * j] = harmonic(beta0[j], beta0[j + 1])
        if j < blocks:
            fx0[2 * j + 1] = beta0[j + 1]
    beta0 = beta0[1:-1]
    for j in range(blocks):
        fine_faces(j)

    level1 = level_refs[1]
    (ua, ub, f1, inv1, c1, fx1) = level1[:6]
    planes1 = 2 * (2 * REACH + 1)
    near = range(own1 - 2, own1 + 4)

    def own_faces():
        own = slice(EDGE, EDGE + by)
        below, low, high, above = [b1[own1 + k] for k in range(-1, 3)]
        lane = index_along((by, nz), 1)
        pair = [low, high]
        mine = [b[own] for b in pair]
        x_low = quarter(pair_lanes(pair_rows(harmonic(below, low)[own], 0), 2))
        x_high = quarter(pair_lanes(pair_rows(harmonic(high, above)[own], 1), 2))
        y_low = sum(harmonic(roll(b, 1, 0), b)[own] for b in pair)
        y_high = sum(harmonic(b, roll(b, -1, 0))[own] for b in pair)
        z_low = sum(harmonic(jnp.where(lane < 2, 0.0, roll(b, 2, 1)), b) for b in mine)
        z_high = sum(harmonic(b, jnp.where(lane >= nz - 2, 0.0, roll(b, -2, 1))) for b in mine)
        y_low = quarter(pair_lanes(pair_rows(y_low, 2, second=False), 2))
        y_high = quarter(pair_lanes(pair_rows(y_high, 3, first=False), 2))
        z_low = quarter(even_part(pair_rows(z_low, 4), 2))
        z_high = quarter(odd_part(pair_rows(z_high, 5), 2))
        row, lane = index_along((cy, nz), 0), index_along((cy, nz), 1)
        corner = (row == cy - 2) & (lane // 4 == nz // 4 - 2)
        edge = jnp.where(corner, roll(roll(z_high, -1, 0), -4, 1), z_high)
        edge = jnp.where(row == cy - 1, y_high, edge)
        mixed = edge
        for k, value in enumerate((x_low, y_low, z_low)):
            mixed = jnp.where(lane % 4 == k, value, mixed)
        f2_pack[0] = mixed.astype(f2_pack.dtype)
        t_pack[0] = x_high.astype(t_pack.dtype)

    own_faces()
    pl.semaphore_wait(all_in, ngx // m - 1)
    gather_send(f2_pack, gf, 0)
    gf[me] = f2_pack[0]
    for j in range(ngy):
        @pl.when((gx == ngx - 1) & (gy == j))
        def _():
            def body(t, carry):
                top_copy(j, (me + t) % n).start()
                return carry

            lax.fori_loop(1, n, body, 0)
            gt[j] = t_pack[0]
    window_send(phase_copy, REACH, REACH)

    for i in range(near[0], near[-1] + 2):
        fx1[i] = harmonic(b1[i - 1], b1[i])
    for i in near:
        put_faces(level1, i, b1[i] > 0.0, cell_faces(b1[i], 2), 2, None)

    for i in near:
        f1[i] = jnp.zeros(f1.shape[1:], f1.dtype)

    window_wait(f_copy, 0, 2)
    for i in range(2 * HALO):
        plane = i if i < HALO else i + lx
        w0[plane, pl.ds(EDGE, ly), :] = wn[i].astype(w0.dtype)
    for i in range(HALO):
        for side, start in enumerate((0, EDGE + ly)):
            rows = wc[side, i].astype(w0.dtype)
            plane = 2 * i if 2 * i < HALO else 2 * i + lx
            w0[plane, pl.ds(start, EDGE), :] = rows[:EDGE]
            w0[plane + 1, pl.ds(start, EDGE), :] = rows[EDGE:]
    for i in range(planes0):
        va[i + 1] = inv0[i] * w0[i]
    sweep(level0, va, vb, 1, 1, planes0 - 1)

    def source_plane(k):
        plane = 2 * (near[0] + k - first_block)
        r = rest_of(level0, vb, plane, 1) + rest_of(level0, vb, plane + 1, 1)
        f1[near[0] + k, pl.ds(EDGE // 2, rows0 // 2), :] = 0.5 * pair_lanes(pair_rows(r, k % slots), 1)

    for k in range(len(near)):
        source_plane(k)
    coarse = [f1[own1 + k, pl.ds(EDGE, by), :] for k in range(2)]
    packed = jnp.where(lane_bit(coarse[0], 1) == 0, coarse[0], coarse[1])
    g1_pack[0] = packed
    h_pack[0] = packed.astype(h_pack.dtype)
    window_send(source_copy, 2, REACH, True)

    for i in near:
        ua[i + 1] = inv1[i] * f1[i]
    sweep(level1, ua, ub, 2, near[0] + 1, near[-1])
    rests = [rest_of(level1, ub, own1 + i, 2)[EDGE : EDGE + by] for i in range(2)]
    coarse = 0.5 * pair_lanes(pair_rows(rests[0] + rests[1], 0), 2)
    half = cy // 2
    packed = jnp.where(lane_bit(coarse[:half], 1) == 0, coarse[:half], coarse[half:])
    g2_pack[0] = packed
    gather_send(g2_pack, g2, 1)
    g2[me] = packed

    window_wait(phase_copy, REACH, REACH)
    phase_block(0)
    phase_block(2 * REACH)
    far = [i for i in range(1, planes1 - 1) if i not in near]
    for i in range(1, planes1):
        if not near[0] <= i <= near[-1] + 1:
            fx1[i] = harmonic(b1[i - 1], b1[i])
    for i in far:
        put_faces(level1, i, b1[i] > 0.0, cell_faces(b1[i], 2), 2, None)

    gather_all(gf, 0).wait_recv()
    for j in range(ngy):
        @pl.when((gx < ngx - 1) | (gy != j))
        def _():
            top_copy(j, me).wait_recv()

    shape2 = counts[2]
    (nx2, ny2) = shape2
    level2 = level_refs[2]
    raw = level2[6:10]
    pick = (index_along((nz, 4 * nz), 0) == index_along((nz, 4 * nz), 1) % nz // 4 * 4 + index_along((nz, 4 * nz), 1) // nz)
    pick = jnp.where(pick, 1.0, 0.0).astype(jnp.bfloat16)

    def whole_plane(ref, k):
        return jnp.concatenate([ref[k * ngy + j].astype(jnp.float32) for j in range(ngy)], axis=0)

    def spread(x, columns):
        return jnp.dot(x.astype(jnp.bfloat16), columns, preferred_element_type=jnp.float32)

    def faces2(i):
        parts = spread(whole_plane(gf, i), pick)
        x_low, y_low, z_low, edge = [parts[:, k * nz : (k + 1) * nz] for k in range(4)]
        row, lane = index_along((ny2, nz), 0), index_along((ny2, nz), 1)
        y_high = jnp.where(row == ny2 - 1, edge, roll(y_low, -1, 0))
        z_edge = jnp.where(row % cy == cy - 1, roll(roll(edge, 1, 0), 4, 1), edge)
        z_high = jnp.where(lane >= nz - 4, z_edge, roll(z_low, -4, 1))
        store(level2[5], i, x_low)
        for ref, value in zip(raw, (y_low, y_high, z_low, z_high)):
            store(ref, i, value)

    each(nx2, faces2)
    store(level2[5], nx2, whole_plane(gt, 0))

    for l in range(2, LEVELS + 1):
        nx, ny = counts[l]
        step = 2**l
        level = level_refs[l]
        if l < LEVELS:
            finer, coarser = level_refs[l], level_refs[l + 1]
            size = max(ny // 2, 4)
            if ny // 2 < EDGE:
                for ref in coarser[5:10]:
                    ref[...] = jnp.zeros(ref.shape, ref.dtype)

            def put(ref, i, value):
                ref[i, pl.ds(0, size), :] = quarter(value).astype(ref.dtype)

            def coarsen(i):
                slot = 4 * (i % 2)
                (fx, yl, yh, zl, zh) = finer[5:10]
                a, b = 2 * i, 2 * i + 1
                put(coarser[5], i, pair_lanes(pair_rows(wide(fx, a), slot), step))
                put(coarser[6], i, pair_lanes(pair_rows(wide(yl, a) + wide(yl, b), slot + 1, second=False), step))
                put(coarser[7], i, pair_lanes(pair_rows(wide(yh, a) + wide(yh, b), slot + 2, first=False), step))
                put(coarser[8], i, even_part(pair_rows(wide(zl, a) + wide(zl, b), slot + 3), step))
                put(coarser[9], i, odd_part(pair_rows(wide(zh, a) + wide(zh, b), slot), step))

            each(nx // 2, coarsen)
            put(coarser[5], nx // 2, pair_lanes(pair_rows(wide(finer[5], nx), 5), step))

        def finish(i):
            lows = [wide(ref, i) for ref in level[6:10]]
            inside = index_along(lows[0].shape, 0) < ny
            put_faces(level, i, inside, lows, step, ny)

        each(nx, finish)

    window_wait(source_copy, 2, REACH, True)
    for t in range(2 * REACH + 1):
        for k, part in enumerate((even_part, odd_part)):
            i = 2 * t + k
            if abs(t - REACH) > 1:
                f1[i] = part(w1[t], 1)
                f1[i, pl.ds(EDGE, by), :] = part(wh[t].astype(jnp.float32), 1)
            else:
                for start in (0, EDGE + by):
                    f1[i, pl.ds(start, EDGE), :] = part(w1[t, pl.ds(start, EDGE), :], 1)
    for i in range(1, planes1 - 1):
        ua[i + 1] = inv1[i] * f1[i]
    sweep(level1, ua, ub, 2, 2, planes1 - 2)

    gather_all(g2, 1).wait_recv()

    f2 = level2[2]

    def unpack(i):
        parts = []
        for j in range(ngy):
            pack = g2[i * ngy + j]
            parts += [even_part(pack, 1), odd_part(pack, 1)]
        f2[i] = jnp.concatenate(parts, axis=0)

    each(nx2, unpack)

    def cycle(l):
        nx, ny = counts[l]
        step = 2**l
        level = level_refs[l]
        (xa, xb, f, inverse) = level[:4]

        def begin(i):
            xa[i + 1] = inverse[i] * f[i]

        each(nx, begin)
        if l == LEVELS:
            for repeat in range(COARSE_SWEEPS - 1):
                sweep(level, xa, xb, step, 0, nx)
                xa, xb = xb, xa
            return xa
        for repeat in range(NU - 1):
            sweep(level, xa, xb, step, 0, nx)
            xa, xb = xb, xa
        f_next = level_refs[l + 1][2]
        size = max(ny // 2, 4)
        if ny // 2 < EDGE:
            f_next[...] = jnp.zeros(f_next.shape, f_next.dtype)

        def restrict(i):
            r = rest_of(level, xa, 2 * i, step) + rest_of(level, xa, 2 * i + 1, step)
            f_next[i, pl.ds(0, size), :] = 0.5 * pair_lanes(pair_rows(r, i % slots), step)

        each(nx // 2, restrict)
        fine = cycle(l + 1)

        def correct(i):
            slot = i % slots
            stretch(fine[i + 1], slot)
            e = temp[slot, pl.ds(0, xa.shape[1]), :]
            xb[2 * i + 1] = xa[2 * i + 1] + e
            xb[2 * i + 2] = xa[2 * i + 2] + e

        each(nx // 2, correct)
        xa, xb = xb, xa
        for repeat in range(NU):
            sweep(level, xa, xb, step, 0, nx)
            xa, xb = xb, xa
        return xa

    found = cycle(2)

    row2 = pl.multiple_of(gy * cy, 8)
    below2 = pl.multiple_of(jnp.maximum(gy * cy - EDGE, 0), 8)
    above2 = pl.multiple_of(jnp.minimum(gy * cy + cy, ny2 - EDGE), 8)
    for t in range(1, 2 * REACH):
        x = gx + t - REACH
        there = (x >= 0) & (x < nx2)
        plane = jnp.clip(x, 0, nx2 - 1) + 1
        e2[t, pl.ds(EDGE, cy), :] = jnp.where(there, found[plane, pl.ds(row2, cy), :], 0.0)
        low = found[plane, pl.ds(below2, EDGE), :]
        high = found[plane, pl.ds(above2, EDGE), :]
        e2[t, pl.ds(0, EDGE), :] = jnp.where(there & (gy > 0), low, 0.0)
        e2[t, pl.ds(EDGE + cy, EDGE), :] = jnp.where(there & (gy < ngy - 1), high, 0.0)

    for t in range(1, 2 * REACH):
        slot = t % slots
        stretch(e2[t], slot)
        e = temp[slot, pl.ds(EDGE, by + 2 * EDGE), :]
        ua[2 * t + 1] = ub[2 * t + 1] + e
        ua[2 * t + 2] = ub[2 * t + 2] + e
    sweep(level1, ua, ub, 2, 3, planes1 - 3)
    sweep(level1, ub, ua, 2, 4, planes1 - 4)

    for j in range(1, blocks - 1):
        slot = j % slots
        stretch(ua[first_block + j + 1], slot)
        e = temp[slot, pl.ds(EDGE, rows0), :]
        va[2 * j + 1] = vb[2 * j + 1] + e
        va[2 * j + 2] = vb[2 * j + 2] + e
    sweep(level0, va, vb, 1, HALO - 2, HALO + lx + 2)
    sweep(level0, vb, va, 1, HALO - 1, HALO + lx + 1)
    for i in range(lx):
        k = HALO + i
        product = c0[k] * va[k + 1]
        near_sum = neighbours(level0, va, k, 1)
        own = slice(EDGE, EDGE + ly)
        scaled_ref[i] = product[own]
        rest_ref[i] = w0[k, pl.ds(EDGE, ly), :] - product[own] + near_sum[own]

    window_done(phase_copy, 0, REACH)
    window_done(f_copy, 0, 2)
    window_done(source_copy, 2, REACH, True)
    gather_all(gf, 0).wait_send()
    gather_all(g2, 1).wait_send()

    @pl.when(gx == ngx - 1)
    def _():
        every = gf.at[pl.ds(0, n - 1)]
        pltpu.make_async_remote_copy(
            src_ref=every, dst_ref=every, send_sem=st.at[0], recv_sem=rt.at[0],
            device_id=(gx, (gy + 1) % ngy), device_id_type=MESH,
        ).wait_send()


def write(scaled_ref, rest_ref, scaled_out, rest_out, sems):
    copies = [
        pltpu.make_async_copy(source, target, sems.at[k])
        for k, (source, target) in enumerate(((scaled_ref, scaled_out), (rest_ref, rest_out)))
    ]
    for copy in copies:
        copy.start()
    for copy in copies:
        copy.wait()


def solution(mesh):
    ngx, ngy = mesh.shape["gx"], mesh.shape["gy"]
    n = ngx * ngy

    def on_device(right_side, phase):
        lx, ly, nz = right_side.shape
        assert lx == 4 and ly % 32 == 0 and NU == 2
        by, cy = ly // 2, ly // 4
        counts = [(lx * ngx >> l, ly * ngy >> l) for l in range(LEVELS + 1)]
        blocks = 2 * REACH + 1

        def level_scratch(planes, rows, padded_source=False):
            shapes = [planes + 2, planes + 2, planes, planes, planes, planes + 1] + [planes] * 4
            if padded_source:
                shapes[2] = 1
            large = planes * rows * nz * 4 >= LARGE
            types = [jnp.float32] * 5 + [jnp.bfloat16 if large else jnp.float32] * 5
            return [pltpu.VMEM((k, rows, nz), dtype) for k, dtype in zip(shapes, types)]

        scratch = [
            pltpu.VMEM((lx + 2 * HALO, ly + 2 * EDGE, nz), jnp.float32),
            pltpu.VMEM((2 * HALO, ly, nz), jnp.bfloat16),
            pltpu.VMEM((2, HALO, 2 * EDGE, nz), jnp.bfloat16),
            pltpu.VMEM((blocks, by + 2 * EDGE_PHASE, nz), jnp.bfloat16),
            pltpu.VMEM((blocks, by + 2 * EDGE, nz), jnp.float32),
            pltpu.VMEM((blocks, by, nz), jnp.bfloat16),
            pltpu.VMEM((n, cy, nz), jnp.bfloat16),
            pltpu.VMEM((ngy, cy, nz), jnp.bfloat16),
            pltpu.VMEM((n, cy // 2, nz), jnp.float32),
            pltpu.VMEM((lx, ly, nz), jnp.int32),
            pltpu.VMEM((1, by, nz), jnp.bfloat16),
            pltpu.VMEM((lx, ly, nz), jnp.bfloat16),
            pltpu.VMEM((2, lx // 2, 2 * EDGE, nz), jnp.bfloat16),
            pltpu.VMEM((1, by, nz), jnp.float32),
            pltpu.VMEM((1, by, nz), jnp.bfloat16),
            pltpu.VMEM((1, cy, nz), jnp.bfloat16),
            pltpu.VMEM((1, cy, nz), jnp.bfloat16),
            pltpu.VMEM((1, cy // 2, nz), jnp.float32),
            pltpu.VMEM((8, max(2 * (by + 2 * EDGE), 2 * counts[2][1], 2 * (cy + 2 * EDGE)), nz), jnp.float32),
            pltpu.VMEM((2 * blocks, by + 2 * EDGE, nz), jnp.float32),
            pltpu.VMEM((blocks, cy + 2 * EDGE, nz), jnp.float32),
        ]
        scratch += level_scratch(lx + 2 * HALO, ly + 2 * EDGE, True)
        scratch += level_scratch(2 * blocks, by + 2 * EDGE)
        for l in range(2, LEVELS + 1):
            scratch += level_scratch(counts[l][0], max(counts[l][1], EDGE))
        scratch += [pltpu.SemaphoreType.DMA((15,))] * 2
        scratch += [pltpu.SemaphoreType.DMA((3 * blocks,))] * 4
        scratch += [pltpu.SemaphoreType.DMA((2,))] * 2
        scratch += [pltpu.SemaphoreType.DMA((1,)), pltpu.SemaphoreType.DMA((ngy,)), pltpu.SemaphoreType.DMA((2,))]
        scratch += [pltpu.SemaphoreType.REGULAR]
        anywhere = pl.BlockSpec(memory_space=pl.ANY)
        inside = pl.BlockSpec(memory_space=pltpu.VMEM)
        right_side, phase = [pltpu.with_memory_space_constraint(x, pltpu.HBM) for x in (right_side, phase)]
        found = pl.pallas_call(
            functools.partial(kernel, ngx, ngy, counts),
            out_shape=[pltpu.VMEM(right_side.shape, jnp.float32)] * 2,
            in_specs=[anywhere] * 2,
            out_specs=[inside] * 2,
            scratch_shapes=scratch,
            compiler_params=pltpu.CompilerParams(
                collective_id=0, has_side_effects=True, vmem_limit_bytes=64_000_000
            ),
        )(right_side, phase)
        return pl.pallas_call(
            write,
            out_shape=[jax.ShapeDtypeStruct(right_side.shape, jnp.float32)] * 2,
            in_specs=[inside] * 2,
            out_specs=[anywhere] * 2,
            scratch_shapes=[pltpu.SemaphoreType.DMA((2,))],
        )(*[pltpu.with_memory_space_constraint(x, pltpu.VMEM) for x in found])

    placed = P("gx", "gy", None)
    return jax.shard_map(
        on_device, mesh=mesh, in_specs=(placed, placed), out_specs=(placed, placed), check_vma=False
    )
```

```python
import functools

import jax
import jax.numpy as jnp
import numpy as np
from jax import lax
from jax.experimental import pallas as pl
from jax.experimental.pallas import tpu as pltpu
from jax.sharding import PartitionSpec as P

LEVELS = 6
NU = 2
COARSE_SWEEPS = 6
OMEGA = 0.8
LIQUID, GAS = 1.0, 1000.0
MIXED = float(np.asarray(2.0 * LIQUID * GAS / (LIQUID + GAS), jnp.bfloat16))
MESH = pl.DeviceIdType.MESH
REACH = 3
HALO = 6
EDGE = 8
EDGE_PHASE = 16
UNROLL = 16
LARGE = 1 << 20


def each(count, body):
    if count <= UNROLL:
        for i in range(count):
            body(i)
    else:
        lax.fori_loop(0, count, lambda i, carry: (body(i), carry)[1], 0)


def index_along(shape, axis):
    return lax.broadcasted_iota(jnp.int32, shape, axis)


def roll(x, shift, axis):
    return pltpu.roll(x, shift % x.shape[axis], axis)


def lane_bit(x, step):
    return index_along(x.shape, x.ndim - 1) // step % 2


def even_part(x, step):
    return jnp.where(lane_bit(x, step) == 0, x, roll(x, step, x.ndim - 1))


def odd_part(x, step):
    return jnp.where(lane_bit(x, step) == 1, x, roll(x, -step, x.ndim - 1))


def pair_lanes(x, step):
    axis = x.ndim - 1
    return x + jnp.where(lane_bit(x, step) == 0, roll(x, -step, axis), roll(x, step, axis))


def harmonic(a, b):
    low, high = jnp.minimum(a, b), jnp.maximum(a, b)
    return jnp.where((low == 0.0) | (low == high), high, MIXED)


def store(ref, i, value):
    ref[i] = value.astype(ref.dtype)


def wide(ref, i):
    return ref[i].astype(jnp.float32)


def quarter(x):
    return (0.25 * x).astype(jnp.bfloat16).astype(jnp.float32)


def kernel(ngx, ngy, counts, f_hbm, phase_hbm, scaled_ref, rest_ref, *refs):
    gx, gy = lax.axis_index("gx"), lax.axis_index("gy")
    n = ngx * ngy
    me = gx * ngy + gy
    lx, ly, nz = f_hbm.shape
    by, cy = ly // 2, ly // 4
    refs = list(refs)

    def take(count):
        out = refs[:count]
        del refs[:count]
        return out

    (w0, wn, wc, wp, w1, wh, gf, gt, g2) = take(9)
    (phase_ref, p_pack, f_pack, c_pack, g1_pack, h_pack, f2_pack, t_pack, g2_pack, temp) = take(10)
    (b1, e2) = take(2)
    level_refs = [take(10) for _ in range(LEVELS + 1)]
    (s0, r0, s1, r1, sp, rp, sg, rg, st, rt, sr, rr, si, all_in) = take(14)

    own_f = w0.at[pl.ds(HALO, lx), pl.ds(EDGE, ly), :]
    load_phase = pltpu.make_async_copy(phase_hbm, phase_ref, si.at[0])
    load_f = pltpu.make_async_copy(f_hbm, own_f, si.at[1])
    load_phase.start()
    load_f.start()

    for start in (0, EDGE + ly):
        w0[:, pl.ds(start, EDGE), :] = jnp.zeros((w0.shape[0], EDGE, nz), w0.dtype)
    for ref in (wn, wc, wp, w1, wh):
        ref[...] = jnp.zeros(ref.shape, ref.dtype)

    barrier = pltpu.get_barrier_semaphore()

    m = max(k for k in range(1, ngx + 1) if ngx % k == 0 and k * k <= ngx)
    greeted = 0

    def greet(x, y, there):
        pl.when(there)(
            lambda: pl.semaphore_signal(barrier, inc=1, device_id=(x, y), device_id_type=MESH)
        )
        return greeted + jnp.where(there, 1, 0)

    mates = [(c * m + gx % m, gy, gx // m != c) for c in range(ngx // m)]
    for x, y, there in mates:
        greeted = greet(x, y, there & (jnp.abs(x - gx) > REACH))
    for e in (0, 1, -1):
        for d in range(-REACH, REACH + 1):
            if (d, e) != (0, 0):
                x, y = gx + d, gy + e
                greeted = greet(x, y, (x >= 0) & (x < ngx) & (y >= 0) & (y < ngy))
    for a in range(m):
        for y in range(ngy):
            x = gx // m * m + a
            column = (x == gx) & (y == gy)
            if m - 1 > REACH or ngy > 2:
                greeted = greet(x, y, ((jnp.abs(x - gx) > REACH) | (jnp.abs(y - gy) > 1)) & ~column)

    for l in range(LEVELS + 1):
        for v in level_refs[l][:2]:
            zero = jnp.zeros(v.shape[1:], v.dtype)
            v[0] = zero
            v[v.shape[0] - 1] = zero

    load_phase.wait()
    for plane in range(0, lx, 4):
        beta = [
            jnp.where(phase_ref[plane + 2 * k, pl.ds(0, by, 2), :] == 1, GAS, LIQUID) for k in range(2)
        ]
        p_pack[0] = jnp.where(lane_bit(beta[0], 1) == 0, beta[0], beta[1]).astype(jnp.bfloat16)
    load_f.wait()
    f_pack[...] = own_f[...].astype(jnp.bfloat16)
    for side, start in enumerate((EDGE, ly)):
        for k in range(lx // 2):
            rows = [w0[HALO + 2 * k + i, pl.ds(start, EDGE), :] for i in range(2)]
            c_pack[side, k] = jnp.concatenate(rows, axis=0).astype(c_pack.dtype)

    pl.semaphore_wait(barrier, greeted)

    def window_copy(src, dst, send, recv, reach, edge, d, e, to):
        lead, rows = src.shape[0], src.shape[1]
        count = rows if e == 0 else edge
        source = src.at[:, pl.ds(rows - edge if e == 1 else 0, count), :]
        start = {0: edge, 1: 0, -1: edge + rows}[e]
        target = dst.at[pl.ds((reach - d) * lead, lead), pl.ds(start, count), :]
        k = (d + reach) * 3 + e + 1
        return pltpu.make_async_remote_copy(
            src_ref=source, dst_ref=target, send_sem=send.at[k], recv_sem=recv.at[k],
            device_id=(gx + to * d, gy + to * e), device_id_type=MESH,
        )

    def source_copy(d, e, to):
        if e == 0 and abs(d) > 1:
            source, target = h_pack, wh.at[pl.ds(REACH - d, 1)]
        else:
            return window_copy(g1_pack, w1, s1, r1, REACH, EDGE, d, e, to)
        k = (d + REACH) * 3 + e + 1
        return pltpu.make_async_remote_copy(
            src_ref=source, dst_ref=target, send_sem=s1.at[k], recv_sem=r1.at[k],
            device_id=(gx + to * d, gy + to * e), device_id_type=MESH,
        )

    def phase_copy(d, e, to):
        return window_copy(p_pack, wp, sp, rp, REACH, EDGE_PHASE, d, e, to)

    def f_copy(d, e, to):
        first, count = {0: (0, lx), 1: (0, lx), -1: (0, lx), 2: (lx - 2, 2), -2: (0, 2)}[d]
        low = {0: 0, 1: HALO - lx, 2: 0, -1: HALO, -2: HALO + lx}[d]
        side = 0 if e == 1 else 1
        if d == 0:
            source = own_f.at[:, pl.ds(ly - EDGE if e == 1 else 0, EDGE), :]
            target = w0.at[pl.ds(HALO, lx), pl.ds(0 if e == 1 else EDGE + ly, EDGE), :]
        elif e == 0:
            source, target = f_pack.at[pl.ds(first, count)], wn.at[pl.ds(low, count)]
        else:
            source = c_pack.at[1 - side, pl.ds(first // 2, count // 2)]
            target = wc.at[side, pl.ds(low // 2, count // 2)]
        k = (d + 2) * 3 + e + 1
        return pltpu.make_async_remote_copy(
            src_ref=source, dst_ref=target, send_sem=s0.at[k], recv_sem=r0.at[k],
            device_id=(gx + to * d, gy + to * e), device_id_type=MESH,
        )

    def each_near(low, high, body, near=None, to=1):
        for e in (0, 1, -1):
            for d in sorted(range(-high, high + 1), key=abs):
                if (d, e) != (0, 0) and (abs(d) >= low or (near is not None and e != 0)):
                    x, y = gx + to * d, gy + to * e
                    pl.when((x >= 0) & (x < ngx) & (y >= 0) & (y < ngy))(functools.partial(body, d, e))

    def window_send(copy, low, high, near=None):
        each_near(low, high, lambda d, e: copy(d, e, 1).start(), near)

    def window_wait(copy, low, high, near=None):
        each_near(low, high, lambda d, e: copy(d, e, -1).wait_recv(), near, -1)

    def window_done(copy, low, high, near=None):
        each_near(low, high, lambda d, e: copy(d, e, 1).wait_send(), near)

    def gather_send(src, dst, k):
        def body(t, carry):
            other = jnp.where(t <= me, t - 1, t)
            pltpu.make_async_remote_copy(
                src_ref=src, dst_ref=dst.at[pl.ds(me, 1)], send_sem=sg.at[k], recv_sem=rg.at[k],
                device_id=(other // ngy, other % ngy), device_id_type=MESH,
            ).start()
            return carry

        lax.fori_loop(1, n, body, 0)

    def gather_all(dst, k):
        every = dst.at[pl.ds(0, n - 1)]
        return pltpu.make_async_remote_copy(
            src_ref=every, dst_ref=every, send_sem=sg.at[k], recv_sem=rg.at[k],
            device_id=(gx, (gy + 1) % ngy), device_id_type=MESH,
        )

    def top_copy(j, other):
        return pltpu.make_async_remote_copy(
            src_ref=t_pack, dst_ref=gt.at[j], send_sem=st.at[0], recv_sem=rt.at[j],
            device_id=(other // ngy, other % ngy), device_id_type=MESH,
        )

    window_send(phase_copy, 0, 2)
    window_send(f_copy, 0, 2)
    for x, y, there in mates:
        pl.when(there)(functools.partial(pl.semaphore_signal, all_in, inc=1, device_id=(x, y), device_id_type=MESH))
    wp[REACH, pl.ds(EDGE_PHASE, by), :] = p_pack[0]

    slots = temp.shape[0]

    def stretch(value, slot):
        rows = value.shape[0]
        temp[slot, pl.ds(0, rows, 2), :] = value
        temp[slot, pl.ds(1, rows, 2), :] = value

    def pair_rows(value, slot, first=True, second=True):
        rows = value.shape[0]
        temp[slot, pl.ds(0, rows), :] = value
        out = 0.0
        if first:
            out = out + temp[slot, pl.ds(0, rows // 2, 2), :]
        if second:
            out = out + temp[slot, pl.ds(1, rows // 2, 2), :]
        return out

    def neighbours(level, v_ref, i, step):
        (_, _, _, _, _, fx, fyl, fyh, fzl, fzh) = level
        v = v_ref[i + 1]
        return (
            wide(fx, i) * v_ref[i] + wide(fx, i + 1) * v_ref[i + 2]
            + wide(fyl, i) * roll(v, 1, 0) + wide(fyh, i) * roll(v, -1, 0)
            + wide(fzl, i) * roll(v, step, 1) + wide(fzh, i) * roll(v, -step, 1)
        )

    def sweep(level, source, target, step, first, last):
        f, inverse = level[2], level[3]

        def body(k):
            i = k + first
            target[i + 1] = (1.0 - OMEGA) * source[i + 1] + inverse[i] * (f[i] + neighbours(level, source, i, step))

        each(last - first, body)

    def rest_of(level, v_ref, i, step):
        return level[2][i] - level[4][i] * v_ref[i + 1] + neighbours(level, v_ref, i, step)

    def put_faces(level, i, inside, lows, step, edges):
        (_, _, _, inverse, centre, fx, fyl, fyh, fzl, fzh) = level
        (yl, yh, zl, zh) = lows
        total = wide(fx, i) + wide(fx, i + 1) + yl + yh + zl + zh
        inverse[i] = jnp.where(inside, OMEGA / jnp.where(inside, total, 1.0), 0.0)
        centre[i] = total
        lane = index_along(zl.shape, 1)
        fzl[i] = jnp.where(lane < step, 0.0, zl).astype(fzl.dtype)
        fzh[i] = jnp.where(lane >= nz - step, 0.0, zh).astype(fzh.dtype)
        if edges is not None:
            row = index_along(yl.shape, 0)
            yl = jnp.where(row == 0, 0.0, yl)
            yh = jnp.where(row >= edges - 1, 0.0, yh)
        fyl[i] = yl.astype(fyl.dtype)
        fyh[i] = yh.astype(fyh.dtype)

    def cell_faces(b, step):
        lane = index_along(b.shape, 1)
        yl, yh = harmonic(roll(b, 1, 0), b), harmonic(b, roll(b, -1, 0))
        zl = harmonic(jnp.where(lane < step, 0.0, roll(b, step, 1)), b)
        zh = harmonic(b, jnp.where(lane >= nz - step, 0.0, roll(b, -step, 1)))
        return yl, yh, zl, zh

    def phase_block(t):
        packed = wp[t].astype(jnp.float32)[EDGE_PHASE - EDGE : EDGE_PHASE + by + EDGE]
        b1[2 * t] = even_part(packed, 1)
        b1[2 * t + 1] = odd_part(packed, 1)

    window_wait(phase_copy, 0, 1)
    for t in range(REACH - 1, REACH + 2):
        phase_block(t)

    own1 = 2 * REACH
    level1 = level_refs[1]
    (ua, ub, f1, inv1, c1, fx1) = level1[:6]
    planes1 = 2 * (2 * REACH + 1)
    near = range(own1 - 2, own1 + 4)

    def own_faces():
        own = slice(EDGE, EDGE + by)
        below, low, high, above = [b1[own1 + k] for k in range(-1, 3)]
        lane = index_along((by, nz), 1)
        pair = [low, high]
        mine = [b[own] for b in pair]
        x_low = quarter(pair_lanes(pair_rows(harmonic(below, low)[own], 0), 2))
        x_high = quarter(pair_lanes(pair_rows(harmonic(high, above)[own], 1), 2))
        y_low = sum(harmonic(roll(b, 1, 0), b)[own] for b in pair)
        y_high = sum(harmonic(b, roll(b, -1, 0))[own] for b in pair)
        z_low = sum(harmonic(jnp.where(lane < 2, 0.0, roll(b, 2, 1)), b) for b in mine)
        z_high = sum(harmonic(b, jnp.where(lane >= nz - 2, 0.0, roll(b, -2, 1))) for b in mine)
        y_low = quarter(pair_lanes(pair_rows(y_low, 2, second=False), 2))
        y_high = quarter(pair_lanes(pair_rows(y_high, 3, first=False), 2))
        z_low = quarter(even_part(pair_rows(z_low, 4), 2))
        z_high = quarter(odd_part(pair_rows(z_high, 5), 2))
        row, lane = index_along((cy, nz), 0), index_along((cy, nz), 1)
        corner = (row == cy - 2) & (lane // 4 == nz // 4 - 2)
        edge = jnp.where(corner, roll(roll(z_high, -1, 0), -4, 1), z_high)
        edge = jnp.where(row == cy - 1, y_high, edge)
        mixed = edge
        for k, value in enumerate((x_low, y_low, z_low)):
            mixed = jnp.where(lane % 4 == k, value, mixed)
        f2_pack[0] = mixed.astype(f2_pack.dtype)
        t_pack[0] = x_high.astype(t_pack.dtype)

    own_faces()
    pl.semaphore_wait(all_in, ngx // m - 1)
    def column_copy(t):
        other = jnp.where(t <= gx, t - 1, t)
        return pltpu.make_async_remote_copy(
            src_ref=f2_pack, dst_ref=gf.at[gy, pl.ds(gx, 1)], send_sem=sg.at[0], recv_sem=rg.at[0],
            device_id=(other, gy), device_id_type=MESH,
        )

    lax.fori_loop(1, ngx, lambda t, carry: (column_copy(t).start(), carry)[1], 0)
    gf[gy, gx] = f2_pack[0]
    for j in range(ngy):
        @pl.when((gx == ngx - 1) & (gy == j))
        def _():
            def body(t, carry):
                top_copy(j, (me + t) % n).start()
                return carry

            lax.fori_loop(1, n, body, 0)
            gt[j, 0] = t_pack[0]
    window_wait(phase_copy, 2, 2)
    phase_block(REACH - 2)
    phase_block(REACH + 2)

    level0 = list(level_refs[0])
    level0[2] = w0
    (va, vb, f0, inv0, c0, fx0) = level0[:6]
    rows0 = ly + 2 * EDGE
    planes0 = lx + 2 * HALO
    blocks = planes0 // 2
    first_block = own1 - HALO // 2

    def fine_beta(j):
        slot = (j + 1) % slots
        stretch(b1[first_block + j], slot)
        return temp[slot, pl.ds(EDGE, rows0), :]

    def fine_faces(j):
        lows = cell_faces(beta0[j], 1)
        for i in (2 * j, 2 * j + 1):
            put_faces(level0, i, beta0[j] > 0.0, lows, 1, None)

    beta0 = [fine_beta(j) for j in range(-1, blocks + 1)]
    for j in range(blocks + 1):
        fx0[2 * j] = harmonic(beta0[j], beta0[j + 1])
        if j < blocks:
            fx0[2 * j + 1] = beta0[j + 1]
    beta0 = beta0[1:-1]
    for j in range(blocks):
        fine_faces(j)

    window_send(phase_copy, REACH, REACH)

    for i in range(near[0], near[-1] + 2):
        fx1[i] = harmonic(b1[i - 1], b1[i])
    for i in near:
        put_faces(level1, i, b1[i] > 0.0, cell_faces(b1[i], 2), 2, None)

    for i in near:
        f1[i] = jnp.zeros(f1.shape[1:], f1.dtype)

    window_wait(f_copy, 0, 2)
    for i in range(2 * HALO):
        plane = i if i < HALO else i + lx
        w0[plane, pl.ds(EDGE, ly), :] = wn[i].astype(w0.dtype)
    for i in range(HALO):
        for side, start in enumerate((0, EDGE + ly)):
            rows = wc[side, i].astype(w0.dtype)
            plane = 2 * i if 2 * i < HALO else 2 * i + lx
            w0[plane, pl.ds(start, EDGE), :] = rows[:EDGE]
            w0[plane + 1, pl.ds(start, EDGE), :] = rows[EDGE:]
    for i in range(planes0):
        va[i + 1] = inv0[i] * w0[i]
    sweep(level0, va, vb, 1, 1, planes0 - 1)

    def source_plane(k):
        plane = 2 * (near[0] + k - first_block)
        r = rest_of(level0, vb, plane, 1) + rest_of(level0, vb, plane + 1, 1)
        f1[near[0] + k, pl.ds(EDGE // 2, rows0 // 2), :] = 0.5 * pair_lanes(pair_rows(r, k % slots), 1)

    for k in range(len(near)):
        source_plane(k)
    coarse = [f1[own1 + k, pl.ds(EDGE, by), :] for k in range(2)]
    packed = jnp.where(lane_bit(coarse[0], 1) == 0, coarse[0], coarse[1])
    g1_pack[0] = packed
    h_pack[0] = packed.astype(h_pack.dtype)
    window_send(source_copy, 2, REACH, True)

    for i in near:
        ua[i + 1] = inv1[i] * f1[i]
    sweep(level1, ua, ub, 2, near[0] + 1, near[-1])
    rests = [rest_of(level1, ub, own1 + i, 2)[EDGE : EDGE + by] for i in range(2)]
    coarse = 0.5 * pair_lanes(pair_rows(rests[0] + rests[1], 0), 2)
    half = cy // 2
    packed = jnp.where(lane_bit(coarse[:half], 1) == 0, coarse[:half], coarse[half:])
    g2_pack[0] = packed
    gather_send(g2_pack, g2, 1)
    g2[me] = packed

    window_wait(phase_copy, REACH, REACH)
    phase_block(0)
    phase_block(2 * REACH)
    far = [i for i in range(1, planes1 - 1) if i not in near]
    for i in range(1, planes1):
        if not near[0] <= i <= near[-1] + 1:
            fx1[i] = harmonic(b1[i - 1], b1[i])
    for i in far:
        put_faces(level1, i, b1[i] > 0.0, cell_faces(b1[i], 2), 2, None)

    def column_all():
        every = gf.at[pl.ds(gy, 1), pl.ds(0, ngx - 1)]
        return pltpu.make_async_remote_copy(
            src_ref=every, dst_ref=every, send_sem=sg.at[0], recv_sem=rg.at[0],
            device_id=(gx, (gy + 1) % ngy), device_id_type=MESH,
        )

    def row_copy(k, to):
        part = gf.at[pl.ds(gy if to > 0 else (gy + ngy - k) % ngy, 1)]
        return pltpu.make_async_remote_copy(
            src_ref=part, dst_ref=part, send_sem=sr.at[k], recv_sem=rr.at[k],
            device_id=(gx, (gy + ngy + to * k) % ngy), device_id_type=MESH,
        )

    column_all().wait_recv()
    for k in range(1, ngy):
        row_copy(k, 1).start()
    for k in range(1, ngy):
        row_copy(k, -1).wait_recv()
    for j in range(ngy):
        @pl.when((gx < ngx - 1) | (gy != j))
        def _():
            top_copy(j, me).wait_recv()

    shape2 = counts[2]
    (nx2, ny2) = shape2
    level2 = level_refs[2]
    raw = level2[6:10]
    pick = (index_along((nz, 4 * nz), 0) == index_along((nz, 4 * nz), 1) % nz // 4 * 4 + index_along((nz, 4 * nz), 1) // nz)
    pick = jnp.where(pick, 1.0, 0.0).astype(jnp.bfloat16)

    def whole_plane(ref, k):
        return jnp.concatenate([ref[j, k].astype(jnp.float32) for j in range(ngy)], axis=0)

    def spread(x, columns):
        return jnp.dot(x.astype(jnp.bfloat16), columns, preferred_element_type=jnp.float32)

    def faces2(i):
        parts = spread(whole_plane(gf, i), pick)
        x_low, y_low, z_low, edge = [parts[:, k * nz : (k + 1) * nz] for k in range(4)]
        row, lane = index_along((ny2, nz), 0), index_along((ny2, nz), 1)
        y_high = jnp.where(row == ny2 - 1, edge, roll(y_low, -1, 0))
        z_edge = jnp.where(row % cy == cy - 1, roll(roll(edge, 1, 0), 4, 1), edge)
        z_high = jnp.where(lane >= nz - 4, z_edge, roll(z_low, -4, 1))
        store(level2[5], i, x_low)
        for ref, value in zip(raw, (y_low, y_high, z_low, z_high)):
            store(ref, i, value)

    each(nx2, faces2)
    store(level2[5], nx2, whole_plane(gt, 0))

    for l in range(2, LEVELS + 1):
        nx, ny = counts[l]
        step = 2**l
        level = level_refs[l]
        if l < LEVELS:
            finer, coarser = level_refs[l], level_refs[l + 1]
            size = max(ny // 2, 4)
            if ny // 2 < EDGE:
                for ref in coarser[5:10]:
                    ref[...] = jnp.zeros(ref.shape, ref.dtype)

            def put(ref, i, value):
                ref[i, pl.ds(0, size), :] = quarter(value).astype(ref.dtype)

            def coarsen(i):
                slot = 4 * (i % 2)
                (fx, yl, yh, zl, zh) = finer[5:10]
                a, b = 2 * i, 2 * i + 1
                put(coarser[5], i, pair_lanes(pair_rows(wide(fx, a), slot), step))
                put(coarser[6], i, pair_lanes(pair_rows(wide(yl, a) + wide(yl, b), slot + 1, second=False), step))
                put(coarser[7], i, pair_lanes(pair_rows(wide(yh, a) + wide(yh, b), slot + 2, first=False), step))
                put(coarser[8], i, even_part(pair_rows(wide(zl, a) + wide(zl, b), slot + 3), step))
                put(coarser[9], i, odd_part(pair_rows(wide(zh, a) + wide(zh, b), slot), step))

            each(nx // 2, coarsen)
            put(coarser[5], nx // 2, pair_lanes(pair_rows(wide(finer[5], nx), 5), step))

        def finish(i):
            lows = [wide(ref, i) for ref in level[6:10]]
            inside = index_along(lows[0].shape, 0) < ny
            put_faces(level, i, inside, lows, step, ny)

        each(nx, finish)

    window_wait(source_copy, 2, REACH, True)
    for t in range(2 * REACH + 1):
        for k, part in enumerate((even_part, odd_part)):
            i = 2 * t + k
            if abs(t - REACH) > 1:
                f1[i] = part(w1[t], 1)
                f1[i, pl.ds(EDGE, by), :] = part(wh[t].astype(jnp.float32), 1)
            else:
                for start in (0, EDGE + by):
                    f1[i, pl.ds(start, EDGE), :] = part(w1[t, pl.ds(start, EDGE), :], 1)
    for i in range(1, planes1 - 1):
        ua[i + 1] = inv1[i] * f1[i]
    sweep(level1, ua, ub, 2, 2, planes1 - 2)

    gather_all(g2, 1).wait_recv()

    f2 = level2[2]

    def unpack(i):
        parts = []
        for j in range(ngy):
            pack = g2[i * ngy + j]
            parts += [even_part(pack, 1), odd_part(pack, 1)]
        f2[i] = jnp.concatenate(parts, axis=0)

    each(nx2, unpack)

    def cycle(l):
        nx, ny = counts[l]
        step = 2**l
        level = level_refs[l]
        (xa, xb, f, inverse) = level[:4]

        def begin(i):
            xa[i + 1] = inverse[i] * f[i]

        each(nx, begin)
        if l == LEVELS:
            for repeat in range(COARSE_SWEEPS - 1):
                sweep(level, xa, xb, step, 0, nx)
                xa, xb = xb, xa
            return xa
        for repeat in range(NU - 1):
            sweep(level, xa, xb, step, 0, nx)
            xa, xb = xb, xa
        f_next = level_refs[l + 1][2]
        size = max(ny // 2, 4)
        if ny // 2 < EDGE:
            f_next[...] = jnp.zeros(f_next.shape, f_next.dtype)

        def restrict(i):
            r = rest_of(level, xa, 2 * i, step) + rest_of(level, xa, 2 * i + 1, step)
            f_next[i, pl.ds(0, size), :] = 0.5 * pair_lanes(pair_rows(r, i % slots), step)

        each(nx // 2, restrict)
        fine = cycle(l + 1)

        def correct(i):
            slot = i % slots
            stretch(fine[i + 1], slot)
            e = temp[slot, pl.ds(0, xa.shape[1]), :]
            xb[2 * i + 1] = xa[2 * i + 1] + e
            xb[2 * i + 2] = xa[2 * i + 2] + e

        each(nx // 2, correct)
        xa, xb = xb, xa
        for repeat in range(NU):
            sweep(level, xa, xb, step, 0, nx)
            xa, xb = xb, xa
        return xa

    found = cycle(2)

    row2 = pl.multiple_of(gy * cy, 8)
    below2 = pl.multiple_of(jnp.maximum(gy * cy - EDGE, 0), 8)
    above2 = pl.multiple_of(jnp.minimum(gy * cy + cy, ny2 - EDGE), 8)
    for t in range(1, 2 * REACH):
        x = gx + t - REACH
        there = (x >= 0) & (x < nx2)
        plane = jnp.clip(x, 0, nx2 - 1) + 1
        e2[t, pl.ds(EDGE, cy), :] = jnp.where(there, found[plane, pl.ds(row2, cy), :], 0.0)
        low = found[plane, pl.ds(below2, EDGE), :]
        high = found[plane, pl.ds(above2, EDGE), :]
        e2[t, pl.ds(0, EDGE), :] = jnp.where(there & (gy > 0), low, 0.0)
        e2[t, pl.ds(EDGE + cy, EDGE), :] = jnp.where(there & (gy < ngy - 1), high, 0.0)

    for t in range(1, 2 * REACH):
        slot = t % slots
        stretch(e2[t], slot)
        e = temp[slot, pl.ds(EDGE, by + 2 * EDGE), :]
        ua[2 * t + 1] = ub[2 * t + 1] + e
        ua[2 * t + 2] = ub[2 * t + 2] + e
    sweep(level1, ua, ub, 2, 3, planes1 - 3)
    sweep(level1, ub, ua, 2, 4, planes1 - 4)

    for j in range(1, blocks - 1):
        slot = j % slots
        stretch(ua[first_block + j + 1], slot)
        e = temp[slot, pl.ds(EDGE, rows0), :]
        va[2 * j + 1] = vb[2 * j + 1] + e
        va[2 * j + 2] = vb[2 * j + 2] + e
    sweep(level0, va, vb, 1, HALO - 2, HALO + lx + 2)
    sweep(level0, vb, va, 1, HALO - 1, HALO + lx + 1)
    for i in range(lx):
        k = HALO + i
        product = c0[k] * va[k + 1]
        near_sum = neighbours(level0, va, k, 1)
        own = slice(EDGE, EDGE + ly)
        scaled_ref[i] = product[own]
        rest_ref[i] = w0[k, pl.ds(EDGE, ly), :] - product[own] + near_sum[own]

    window_done(phase_copy, 0, REACH)
    window_done(f_copy, 0, 2)
    window_done(source_copy, 2, REACH, True)
    column_all().wait_send()
    for k in range(1, ngy):
        row_copy(k, 1).wait_send()
    gather_all(g2, 1).wait_send()

    @pl.when(gx == ngx - 1)
    def _():
        every = g2.at[pl.ds(0, n - 1)]
        pltpu.make_async_remote_copy(
            src_ref=every, dst_ref=every, send_sem=st.at[0], recv_sem=rt.at[0],
            device_id=(gx, (gy + 1) % ngy), device_id_type=MESH,
        ).wait_send()


def write(scaled_ref, rest_ref, scaled_out, rest_out, sems):
    copies = [
        pltpu.make_async_copy(source, target, sems.at[k])
        for k, (source, target) in enumerate(((scaled_ref, scaled_out), (rest_ref, rest_out)))
    ]
    for copy in copies:
        copy.start()
    for copy in copies:
        copy.wait()


def solution(mesh):
    ngx, ngy = mesh.shape["gx"], mesh.shape["gy"]
    n = ngx * ngy

    def on_device(right_side, phase):
        lx, ly, nz = right_side.shape
        assert lx == 4 and ly % 32 == 0 and NU == 2
        by, cy = ly // 2, ly // 4
        counts = [(lx * ngx >> l, ly * ngy >> l) for l in range(LEVELS + 1)]
        blocks = 2 * REACH + 1

        def level_scratch(planes, rows, padded_source=False):
            shapes = [planes + 2, planes + 2, planes, planes, planes, planes + 1] + [planes] * 4
            if padded_source:
                shapes[2] = 1
            large = planes * rows * nz * 4 >= LARGE
            types = [jnp.float32] * 5 + [jnp.bfloat16 if large else jnp.float32] * 5
            return [pltpu.VMEM((k, rows, nz), dtype) for k, dtype in zip(shapes, types)]

        scratch = [
            pltpu.VMEM((lx + 2 * HALO, ly + 2 * EDGE, nz), jnp.float32),
            pltpu.VMEM((2 * HALO, ly, nz), jnp.bfloat16),
            pltpu.VMEM((2, HALO, 2 * EDGE, nz), jnp.bfloat16),
            pltpu.VMEM((blocks, by + 2 * EDGE_PHASE, nz), jnp.bfloat16),
            pltpu.VMEM((blocks, by + 2 * EDGE, nz), jnp.float32),
            pltpu.VMEM((blocks, by, nz), jnp.bfloat16),
            pltpu.VMEM((ngy, ngx, cy, nz), jnp.bfloat16),
            pltpu.VMEM((ngy, 1, cy, nz), jnp.bfloat16),
            pltpu.VMEM((n, cy // 2, nz), jnp.float32),
            pltpu.VMEM((lx, ly, nz), jnp.int32),
            pltpu.VMEM((1, by, nz), jnp.bfloat16),
            pltpu.VMEM((lx, ly, nz), jnp.bfloat16),
            pltpu.VMEM((2, lx // 2, 2 * EDGE, nz), jnp.bfloat16),
            pltpu.VMEM((1, by, nz), jnp.float32),
            pltpu.VMEM((1, by, nz), jnp.bfloat16),
            pltpu.VMEM((1, cy, nz), jnp.bfloat16),
            pltpu.VMEM((1, cy, nz), jnp.bfloat16),
            pltpu.VMEM((1, cy // 2, nz), jnp.float32),
            pltpu.VMEM((8, max(2 * (by + 2 * EDGE), 2 * counts[2][1], 2 * (cy + 2 * EDGE)), nz), jnp.float32),
            pltpu.VMEM((2 * blocks, by + 2 * EDGE, nz), jnp.float32),
            pltpu.VMEM((blocks, cy + 2 * EDGE, nz), jnp.float32),
        ]
        scratch += level_scratch(lx + 2 * HALO, ly + 2 * EDGE, True)
        scratch += level_scratch(2 * blocks, by + 2 * EDGE)
        for l in range(2, LEVELS + 1):
            scratch += level_scratch(counts[l][0], max(counts[l][1], EDGE))
        scratch += [pltpu.SemaphoreType.DMA((15,))] * 2
        scratch += [pltpu.SemaphoreType.DMA((3 * blocks,))] * 4
        scratch += [pltpu.SemaphoreType.DMA((2,))] * 2
        scratch += [pltpu.SemaphoreType.DMA((1,)), pltpu.SemaphoreType.DMA((ngy,))]
        scratch += [pltpu.SemaphoreType.DMA((ngy,)), pltpu.SemaphoreType.DMA((ngy,)), pltpu.SemaphoreType.DMA((2,))]
        scratch += [pltpu.SemaphoreType.REGULAR]
        anywhere = pl.BlockSpec(memory_space=pl.ANY)
        inside = pl.BlockSpec(memory_space=pltpu.VMEM)
        right_side, phase = [pltpu.with_memory_space_constraint(x, pltpu.HBM) for x in (right_side, phase)]
        found = pl.pallas_call(
            functools.partial(kernel, ngx, ngy, counts),
            out_shape=[pltpu.VMEM(right_side.shape, jnp.float32)] * 2,
            in_specs=[anywhere] * 2,
            out_specs=[inside] * 2,
            scratch_shapes=scratch,
            compiler_params=pltpu.CompilerParams(
                collective_id=0, has_side_effects=True, vmem_limit_bytes=64_000_000
            ),
        )(right_side, phase)
        return pl.pallas_call(
            write,
            out_shape=[jax.ShapeDtypeStruct(right_side.shape, jnp.float32)] * 2,
            in_specs=[inside] * 2,
            out_specs=[anywhere] * 2,
            scratch_shapes=[pltpu.SemaphoreType.DMA((2,))],
        )(*[pltpu.with_memory_space_constraint(x, pltpu.VMEM) for x in found])

    placed = P("gx", "gy", None)
    return jax.shard_map(
        on_device, mesh=mesh, in_specs=(placed, placed), out_specs=(placed, placed), check_vma=False
    )
```

```python
import functools

import jax
import jax.numpy as jnp
import numpy as np
from jax import lax
from jax.experimental import pallas as pl
from jax.experimental.pallas import tpu as pltpu
from jax.sharding import PartitionSpec as P

LEVELS = 6
NU = 2
COARSE_SWEEPS = 6
OMEGA = 0.8
LIQUID, GAS = 1.0, 1000.0
MIXED = float(np.asarray(2.0 * LIQUID * GAS / (LIQUID + GAS), jnp.bfloat16))
MESH = pl.DeviceIdType.MESH
REACH = 3
HALO = 6
PACK = 4
GROUPS = 4
EDGE = 8
EDGE_PHASE = 16
UNROLL = 16
LARGE = 1 << 20


def each(count, body):
    if count <= UNROLL:
        for i in range(count):
            body(i)
    else:
        lax.fori_loop(0, count, lambda i, carry: (body(i), carry)[1], 0)


def each_group(count, body):
    if count <= GROUPS:
        for i in range(count):
            body(i)
    else:
        lax.fori_loop(0, count, lambda i, carry: (body(i), carry)[1], 0)


def index_along(shape, axis):
    return lax.broadcasted_iota(jnp.int32, shape, axis)


def roll(x, shift, axis):
    return pltpu.roll(x, shift % x.shape[axis], axis)


def lane_bit(x, step):
    return index_along(x.shape, x.ndim - 1) // step % 2


def even_part(x, step):
    return jnp.where(lane_bit(x, step) == 0, x, roll(x, step, x.ndim - 1))


def odd_part(x, step):
    return jnp.where(lane_bit(x, step) == 1, x, roll(x, -step, x.ndim - 1))


def lanes_at(x, index):
    return jnp.take_along_axis(x, index, axis=1, mode="promise_in_bounds")


def pair_lanes(x, step):
    axis = x.ndim - 1
    return x + jnp.where(lane_bit(x, step) == 0, roll(x, -step, axis), roll(x, step, axis))


def harmonic(a, b):
    low, high = jnp.minimum(a, b), jnp.maximum(a, b)
    return jnp.where((low == 0.0) | (low == high), high, MIXED)


def store(ref, i, value):
    ref[i] = value.astype(ref.dtype)


def wide(ref, i):
    return ref[i].astype(jnp.float32)


def quarter(x):
    return (0.25 * x).astype(jnp.bfloat16).astype(jnp.float32)


def kernel(ngx, ngy, counts, f_hbm, phase_hbm, scaled_ref, rest_ref, *refs):
    gx, gy = lax.axis_index("gx"), lax.axis_index("gy")
    n = ngx * ngy
    me = gx * ngy + gy
    lx, ly, nz = f_hbm.shape
    by, cy = ly // 2, ly // 4
    refs = list(refs)

    def take(count):
        out = refs[:count]
        del refs[:count]
        return out

    (w0, wn, wc, wp, w1, wh, gf, gt, g2) = take(9)
    (phase_ref, p_pack, f_pack, c_pack, g1_pack, h_pack, f2_pack, t_pack, g2_pack, temp) = take(10)
    (b1, e2) = take(2)
    level_refs = [take(10 if l < 2 else 11) for l in range(LEVELS + 1)]
    apart_refs = [take(1)[0] for l in range(LEVELS + 1)]
    (s0, r0, s1, r1, sp, rp, sg, rg, st, rt, sr, rr, si, all_in) = take(14)

    own_f = w0.at[pl.ds(HALO, lx), pl.ds(EDGE, ly), :]
    load_phase = pltpu.make_async_copy(phase_hbm, phase_ref, si.at[0])
    load_f = pltpu.make_async_copy(f_hbm, own_f, si.at[1])
    load_phase.start()
    load_f.start()

    for start in (0, EDGE + ly):
        w0[:, pl.ds(start, EDGE), :] = jnp.zeros((w0.shape[0], EDGE, nz), w0.dtype)
    for ref in (wn, wc, wp, w1, wh):
        ref[...] = jnp.zeros(ref.shape, ref.dtype)

    barrier = pltpu.get_barrier_semaphore()

    m = max(k for k in range(1, ngx + 1) if ngx % k == 0 and k * k <= ngx)
    greeted = 0

    def greet(x, y, there):
        pl.when(there)(
            lambda: pl.semaphore_signal(barrier, inc=1, device_id=(x, y), device_id_type=MESH)
        )
        return greeted + jnp.where(there, 1, 0)

    mates = [(c * m + gx % m, gy, gx // m != c) for c in range(ngx // m)]
    for x, y, there in mates:
        greeted = greet(x, y, there & (jnp.abs(x - gx) > REACH))
    for e in (0, 1, -1):
        for d in range(-REACH, REACH + 1):
            if (d, e) != (0, 0):
                x, y = gx + d, gy + e
                greeted = greet(x, y, (x >= 0) & (x < ngx) & (y >= 0) & (y < ngy))
    for a in range(m):
        for y in range(ngy):
            x = gx // m * m + a
            column = (x == gx) & (y == gy)
            if m - 1 > REACH or ngy > 2:
                greeted = greet(x, y, ((jnp.abs(x - gx) > REACH) | (jnp.abs(y - gy) > 1)) & ~column)

    for l in range(2):
        for v in level_refs[l][:2]:
            zero = jnp.zeros(v.shape[1:], v.dtype)
            v[0] = zero
            v[v.shape[0] - 1] = zero

    load_phase.wait()
    for plane in range(0, lx, 4):
        beta = [
            jnp.where(phase_ref[plane + 2 * k, pl.ds(0, by, 2), :] == 1, GAS, LIQUID) for k in range(2)
        ]
        p_pack[0] = jnp.where(lane_bit(beta[0], 1) == 0, beta[0], beta[1]).astype(jnp.bfloat16)
    load_f.wait()
    f_pack[...] = own_f[...].astype(jnp.bfloat16)
    for side, start in enumerate((EDGE, ly)):
        for k in range(lx // 2):
            rows = [w0[HALO + 2 * k + i, pl.ds(start, EDGE), :] for i in range(2)]
            c_pack[side, k] = jnp.concatenate(rows, axis=0).astype(c_pack.dtype)

    pl.semaphore_wait(barrier, greeted)

    def window_copy(src, dst, send, recv, reach, edge, d, e, to):
        lead, rows = src.shape[0], src.shape[1]
        count = rows if e == 0 else edge
        source = src.at[:, pl.ds(rows - edge if e == 1 else 0, count), :]
        start = {0: edge, 1: 0, -1: edge + rows}[e]
        target = dst.at[pl.ds((reach - d) * lead, lead), pl.ds(start, count), :]
        k = (d + reach) * 3 + e + 1
        return pltpu.make_async_remote_copy(
            src_ref=source, dst_ref=target, send_sem=send.at[k], recv_sem=recv.at[k],
            device_id=(gx + to * d, gy + to * e), device_id_type=MESH,
        )

    def source_copy(d, e, to):
        if e == 0 and abs(d) > 1:
            source, target = h_pack, wh.at[pl.ds(REACH - d, 1)]
        else:
            return window_copy(g1_pack, w1, s1, r1, REACH, EDGE, d, e, to)
        k = (d + REACH) * 3 + e + 1
        return pltpu.make_async_remote_copy(
            src_ref=source, dst_ref=target, send_sem=s1.at[k], recv_sem=r1.at[k],
            device_id=(gx + to * d, gy + to * e), device_id_type=MESH,
        )

    def phase_copy(d, e, to):
        return window_copy(p_pack, wp, sp, rp, REACH, EDGE_PHASE, d, e, to)

    def f_copy(d, e, to):
        first, count = {0: (0, lx), 1: (0, lx), -1: (0, lx), 2: (lx - 2, 2), -2: (0, 2)}[d]
        low = {0: 0, 1: HALO - lx, 2: 0, -1: HALO, -2: HALO + lx}[d]
        side = 0 if e == 1 else 1
        if d == 0:
            source = own_f.at[:, pl.ds(ly - EDGE if e == 1 else 0, EDGE), :]
            target = w0.at[pl.ds(HALO, lx), pl.ds(0 if e == 1 else EDGE + ly, EDGE), :]
        elif e == 0:
            source, target = f_pack.at[pl.ds(first, count)], wn.at[pl.ds(low, count)]
        else:
            source = c_pack.at[1 - side, pl.ds(first // 2, count // 2)]
            target = wc.at[side, pl.ds(low // 2, count // 2)]
        k = (d + 2) * 3 + e + 1
        return pltpu.make_async_remote_copy(
            src_ref=source, dst_ref=target, send_sem=s0.at[k], recv_sem=r0.at[k],
            device_id=(gx + to * d, gy + to * e), device_id_type=MESH,
        )

    def each_near(low, high, body, near=None, to=1):
        for e in (0, 1, -1):
            for d in sorted(range(-high, high + 1), key=abs):
                if (d, e) != (0, 0) and (abs(d) >= low or (near is not None and e != 0)):
                    x, y = gx + to * d, gy + to * e
                    pl.when((x >= 0) & (x < ngx) & (y >= 0) & (y < ngy))(functools.partial(body, d, e))

    def window_send(copy, low, high, near=None):
        each_near(low, high, lambda d, e: copy(d, e, 1).start(), near)

    def window_wait(copy, low, high, near=None):
        each_near(low, high, lambda d, e: copy(d, e, -1).wait_recv(), near, -1)

    def window_done(copy, low, high, near=None):
        each_near(low, high, lambda d, e: copy(d, e, 1).wait_send(), near)

    def gather_send(src, dst, k):
        def body(t, carry):
            other = jnp.where(t <= me, t - 1, t)
            pltpu.make_async_remote_copy(
                src_ref=src, dst_ref=dst.at[pl.ds(me, 1)], send_sem=sg.at[k], recv_sem=rg.at[k],
                device_id=(other // ngy, other % ngy), device_id_type=MESH,
            ).start()
            return carry

        lax.fori_loop(1, n, body, 0)

    def gather_all(dst, k):
        every = dst.at[pl.ds(0, n - 1)]
        return pltpu.make_async_remote_copy(
            src_ref=every, dst_ref=every, send_sem=sg.at[k], recv_sem=rg.at[k],
            device_id=(gx, (gy + 1) % ngy), device_id_type=MESH,
        )

    def top_copy(j, other):
        return pltpu.make_async_remote_copy(
            src_ref=t_pack, dst_ref=gt.at[j], send_sem=st.at[0], recv_sem=rt.at[j],
            device_id=(other // ngy, other % ngy), device_id_type=MESH,
        )

    window_send(phase_copy, 0, 2)
    window_send(f_copy, 0, 2)
    for x, y, there in mates:
        pl.when(there)(functools.partial(pl.semaphore_signal, all_in, inc=1, device_id=(x, y), device_id_type=MESH))
    wp[REACH, pl.ds(EDGE_PHASE, by), :] = p_pack[0]

    slots = temp.shape[0]

    def stretch(value, slot):
        rows = value.shape[0]
        temp[slot, pl.ds(0, rows, 2), :] = value
        temp[slot, pl.ds(1, rows, 2), :] = value

    def pair_rows(value, slot, first=True, second=True):
        rows = value.shape[0]
        temp[slot, pl.ds(0, rows), :] = value
        out = 0.0
        if first:
            out = out + temp[slot, pl.ds(0, rows // 2, 2), :]
        if second:
            out = out + temp[slot, pl.ds(1, rows // 2, 2), :]
        return out

    def neighbours(level, v_ref, i, step):
        (_, _, _, _, _, fx, fyl, fyh, fzl, fzh) = level
        v = v_ref[i + 1]
        return (
            wide(fx, i) * v_ref[i] + wide(fx, i + 1) * v_ref[i + 2]
            + wide(fyl, i) * roll(v, 1, 0) + wide(fyh, i) * roll(v, -1, 0)
            + wide(fzl, i) * roll(v, step, 1) + wide(fzh, i) * roll(v, -step, 1)
        )

    def sweep(level, source, target, step, first, last):
        f, inverse = level[2], level[3]

        def body(k):
            i = k + first
            target[i + 1] = (1.0 - OMEGA) * source[i + 1] + inverse[i] * (f[i] + neighbours(level, source, i, step))

        each(last - first, body)

    def rest_of(level, v_ref, i, step):
        return level[2][i] - level[4][i] * v_ref[i + 1] + neighbours(level, v_ref, i, step)

    def put_faces(level, i, inside, lows, step, edges):
        (_, _, _, inverse, centre, fx, fyl, fyh, fzl, fzh) = level
        (yl, yh, zl, zh) = lows
        total = wide(fx, i) + wide(fx, i + 1) + yl + yh + zl + zh
        inverse[i] = jnp.where(inside, OMEGA / jnp.where(inside, total, 1.0), 0.0)
        centre[i] = total
        lane = index_along(zl.shape, 1)
        fzl[i] = jnp.where(lane < step, 0.0, zl).astype(fzl.dtype)
        fzh[i] = jnp.where(lane >= nz - step, 0.0, zh).astype(fzh.dtype)
        if edges is not None:
            row = index_along(yl.shape, 0)
            yl = jnp.where(row == 0, 0.0, yl)
            yh = jnp.where(row >= edges - 1, 0.0, yh)
        fyl[i] = yl.astype(fyl.dtype)
        fyh[i] = yh.astype(fyh.dtype)

    def cell_faces(b, step):
        lane = index_along(b.shape, 1)
        yl, yh = harmonic(roll(b, 1, 0), b), harmonic(b, roll(b, -1, 0))
        zl = harmonic(jnp.where(lane < step, 0.0, roll(b, step, 1)), b)
        zh = harmonic(b, jnp.where(lane >= nz - step, 0.0, roll(b, -step, 1)))
        return yl, yh, zl, zh

    def phase_block(t):
        packed = wp[t].astype(jnp.float32)[EDGE_PHASE - EDGE : EDGE_PHASE + by + EDGE]
        b1[2 * t] = even_part(packed, 1)
        b1[2 * t + 1] = odd_part(packed, 1)

    window_wait(phase_copy, 0, 1)
    for t in range(REACH - 1, REACH + 2):
        phase_block(t)

    own1 = 2 * REACH
    level1 = level_refs[1]
    (ua, ub, f1, inv1, c1, fx1) = level1[:6]
    planes1 = 2 * (2 * REACH + 1)
    near = range(own1 - 2, own1 + 4)

    def own_faces():
        own = slice(EDGE, EDGE + by)
        below, low, high, above = [b1[own1 + k] for k in range(-1, 3)]
        lane = index_along((by, nz), 1)
        pair = [low, high]
        mine = [b[own] for b in pair]
        x_low = quarter(pair_lanes(pair_rows(harmonic(below, low)[own], 0), 2))
        x_high = quarter(pair_lanes(pair_rows(harmonic(high, above)[own], 1), 2))
        y_low = sum(harmonic(roll(b, 1, 0), b)[own] for b in pair)
        y_high = sum(harmonic(b, roll(b, -1, 0))[own] for b in pair)
        z_low = sum(harmonic(jnp.where(lane < 2, 0.0, roll(b, 2, 1)), b) for b in mine)
        z_high = sum(harmonic(b, jnp.where(lane >= nz - 2, 0.0, roll(b, -2, 1))) for b in mine)
        y_low = quarter(pair_lanes(pair_rows(y_low, 2, second=False), 2))
        y_high = quarter(pair_lanes(pair_rows(y_high, 3, first=False), 2))
        z_low = quarter(even_part(pair_rows(z_low, 4), 2))
        z_high = quarter(odd_part(pair_rows(z_high, 5), 2))
        row, lane = index_along((cy, nz), 0), index_along((cy, nz), 1)
        corner = (row == cy - 2) & (lane // 4 == nz // 4 - 2)
        edge = jnp.where(corner, roll(roll(z_high, -1, 0), -4, 1), z_high)
        edge = jnp.where(row == cy - 1, y_high, edge)
        mixed = edge
        for k, value in enumerate((x_low, y_low, z_low)):
            mixed = jnp.where(lane % 4 == k, value, mixed)
        f2_pack[0] = mixed.astype(f2_pack.dtype)
        t_pack[0] = x_high.astype(t_pack.dtype)

    own_faces()
    pl.semaphore_wait(all_in, ngx // m - 1)
    def column_copy(t):
        other = jnp.where(t <= gx, t - 1, t)
        return pltpu.make_async_remote_copy(
            src_ref=f2_pack, dst_ref=gf.at[gy, pl.ds(gx, 1)], send_sem=sg.at[0], recv_sem=rg.at[0],
            device_id=(other, gy), device_id_type=MESH,
        )

    lax.fori_loop(1, ngx, lambda t, carry: (column_copy(t).start(), carry)[1], 0)
    gf[gy, gx] = f2_pack[0]
    for j in range(ngy):
        @pl.when((gx == ngx - 1) & (gy == j))
        def _():
            def body(t, carry):
                top_copy(j, (me + t) % n).start()
                return carry

            lax.fori_loop(1, n, body, 0)
            gt[j, 0] = t_pack[0]
    window_wait(phase_copy, 2, 2)
    phase_block(REACH - 2)
    phase_block(REACH + 2)

    level0 = list(level_refs[0])
    level0[2] = w0
    (va, vb, f0, inv0, c0, fx0) = level0[:6]
    rows0 = ly + 2 * EDGE
    planes0 = lx + 2 * HALO
    blocks = planes0 // 2
    first_block = own1 - HALO // 2

    def fine_beta(j):
        slot = (j + 1) % slots
        stretch(b1[first_block + j], slot)
        return temp[slot, pl.ds(EDGE, rows0), :]

    def fine_faces(j):
        lows = cell_faces(beta0[j], 1)
        for i in (2 * j, 2 * j + 1):
            put_faces(level0, i, beta0[j] > 0.0, lows, 1, None)

    beta0 = [fine_beta(j) for j in range(-1, blocks + 1)]
    for j in range(blocks + 1):
        fx0[2 * j] = harmonic(beta0[j], beta0[j + 1])
        if j < blocks:
            fx0[2 * j + 1] = beta0[j + 1]
    beta0 = beta0[1:-1]
    for j in range(blocks):
        fine_faces(j)

    window_send(phase_copy, REACH, REACH)

    for i in range(near[0], near[-1] + 2):
        fx1[i] = harmonic(b1[i - 1], b1[i])
    for i in near:
        put_faces(level1, i, b1[i] > 0.0, cell_faces(b1[i], 2), 2, None)

    for i in near:
        f1[i] = jnp.zeros(f1.shape[1:], f1.dtype)

    window_wait(f_copy, 0, 2)
    for i in range(2 * HALO):
        plane = i if i < HALO else i + lx
        w0[plane, pl.ds(EDGE, ly), :] = wn[i].astype(w0.dtype)
    for i in range(HALO):
        for side, start in enumerate((0, EDGE + ly)):
            rows = wc[side, i].astype(w0.dtype)
            plane = 2 * i if 2 * i < HALO else 2 * i + lx
            w0[plane, pl.ds(start, EDGE), :] = rows[:EDGE]
            w0[plane + 1, pl.ds(start, EDGE), :] = rows[EDGE:]
    for i in range(planes0):
        va[i + 1] = inv0[i] * w0[i]
    sweep(level0, va, vb, 1, 1, planes0 - 1)

    def source_plane(k):
        plane = 2 * (near[0] + k - first_block)
        r = rest_of(level0, vb, plane, 1) + rest_of(level0, vb, plane + 1, 1)
        f1[near[0] + k, pl.ds(EDGE // 2, rows0 // 2), :] = 0.5 * pair_lanes(pair_rows(r, k % slots), 1)

    for k in range(len(near)):
        source_plane(k)
    coarse = [f1[own1 + k, pl.ds(EDGE, by), :] for k in range(2)]
    packed = jnp.where(lane_bit(coarse[0], 1) == 0, coarse[0], coarse[1])
    g1_pack[0] = packed
    h_pack[0] = packed.astype(h_pack.dtype)
    window_send(source_copy, 2, REACH, True)

    for i in near:
        ua[i + 1] = inv1[i] * f1[i]
    sweep(level1, ua, ub, 2, near[0] + 1, near[-1])
    rests = [rest_of(level1, ub, own1 + i, 2)[EDGE : EDGE + by] for i in range(2)]
    coarse = 0.5 * pair_lanes(pair_rows(rests[0] + rests[1], 0), 2)
    half = cy // 2
    coarse = lanes_at(coarse, index_along(coarse.shape, 1) % (nz // PACK) * PACK)
    packed = jnp.where(lane_bit(coarse[:half], nz // PACK) == 0, coarse[:half], coarse[half:])
    g2_pack[0] = packed
    gather_send(g2_pack, g2, 1)
    g2[me] = packed

    window_wait(phase_copy, REACH, REACH)
    phase_block(0)
    phase_block(2 * REACH)
    far = [i for i in range(1, planes1 - 1) if i not in near]
    for i in range(1, planes1):
        if not near[0] <= i <= near[-1] + 1:
            fx1[i] = harmonic(b1[i - 1], b1[i])
    for i in far:
        put_faces(level1, i, b1[i] > 0.0, cell_faces(b1[i], 2), 2, None)

    def column_all():
        every = gf.at[pl.ds(gy, 1), pl.ds(0, ngx - 1)]
        return pltpu.make_async_remote_copy(
            src_ref=every, dst_ref=every, send_sem=sg.at[0], recv_sem=rg.at[0],
            device_id=(gx, (gy + 1) % ngy), device_id_type=MESH,
        )

    def row_copy(k, to):
        part = gf.at[pl.ds(gy if to > 0 else (gy + ngy - k) % ngy, 1)]
        return pltpu.make_async_remote_copy(
            src_ref=part, dst_ref=part, send_sem=sr.at[k], recv_sem=rr.at[k],
            device_id=(gx, (gy + ngy + to * k) % ngy), device_id_type=MESH,
        )

    column_all().wait_recv()
    for k in range(1, ngy):
        row_copy(k, 1).start()
    for k in range(1, ngy):
        row_copy(k, -1).wait_recv()
    for j in range(ngy):
        @pl.when((gx < ngx - 1) | (gy != j))
        def _():
            top_copy(j, me).wait_recv()

    shape2 = counts[2]
    (nx2, ny2) = shape2
    level2 = level_refs[2]
    span = nz // PACK

    def groups(l):
        return max(counts[l][0] // PACK, 1)

    def lane_step(l):
        return nz // min(counts[l][0], PACK)

    row_p, lane_p = index_along((nz, PACK * nz), 0), index_along((nz, PACK * nz), 1)
    picks = []
    for q in range(PACK):
        chosen = (row_p == PACK * (lane_p % span) + lane_p // nz) & (lane_p % nz // span == q)
        picks.append(jnp.where(chosen, 1.0, 0.0).astype(jnp.bfloat16))

    def whole_plane(ref, k):
        return jnp.concatenate([ref[j, k].astype(jnp.float32) for j in range(ngy)], axis=0)

    def spread(x, columns):
        return jnp.dot(x.astype(jnp.bfloat16), columns, preferred_element_type=jnp.float32)

    many = groups(2)
    row2, lane2 = index_along((ny2, nz), 0), index_along((ny2, nz), 1)

    def faces2(t):
        parts = sum(spread(whole_plane(gf, q * many + t), picks[q]) for q in range(PACK))
        x_low, y_low, z_low, edge = [parts[:, k * nz : (k + 1) * nz] for k in range(4)]
        y_high = jnp.where(row2 == ny2 - 1, edge, roll(y_low, -1, 0))
        z_edge = jnp.where(row2 % cy == cy - 1, roll(roll(edge, 1, 0), 1, 1), edge)
        z_high = jnp.where(lane2 % span == span - 1, z_edge, roll(z_low, -1, 1))
        for ref, value in zip(level2[5:6] + level2[7:], (x_low, y_low, y_high, z_low, z_high)):
            store(ref, t, value)

    each_group(many, faces2)
    top = spread(whole_plane(gt, 0), picks[PACK - 1])[:, :nz]

    def faces2_high(t):
        after = wide(level2[5], (t + 1) % many)
        around = jnp.where(lane2 >= nz - span, top, roll(after, -span, 1))
        store(level2[6], t, jnp.where(t == many - 1, around, after))

    each_group(many, faces2_high)

    for l in range(2, LEVELS + 1):
        nx, ny = counts[l]
        step, across, many = 2 ** (l - 2), lane_step(l), groups(l)
        level = level_refs[l]
        if l < LEVELS:
            coarser = level_refs[l + 1]
            size = max(ny // 2, 4)
            if ny // 2 < EDGE:
                for ref in coarser[5:]:
                    ref[...] = jnp.zeros(ref.shape, ref.dtype)

            def put(ref, s, value):
                ref[s, pl.ds(0, size), :] = quarter(value).astype(ref.dtype)

            def coarsen(s):
                slot = 4 * (s % 2)
                if many > 1:
                    low = lambda ref: wide(ref, 2 * s)
                    high = lambda ref: wide(ref, 2 * s + 1)
                    both = lambda ref: low(ref) + high(ref)
                else:
                    low = lambda ref: even_part(wide(ref, 0), across)
                    high = lambda ref: odd_part(wide(ref, 0), across)
                    both = lambda ref: pair_lanes(wide(ref, 0), across)
                (xl, xh, yl, yh, zl, zh) = level[5:]
                put(coarser[5], s, pair_lanes(pair_rows(low(xl), slot), step))
                put(coarser[6], s, pair_lanes(pair_rows(high(xh), slot + 1), step))
                put(coarser[7], s, pair_lanes(pair_rows(both(yl), slot + 2, second=False), step))
                put(coarser[8], s, pair_lanes(pair_rows(both(yh), slot + 3, first=False), step))
                put(coarser[9], s, even_part(pair_rows(both(zl), slot), step))
                put(coarser[10], s, odd_part(pair_rows(both(zh), slot + 1), step))

            each_group(groups(l + 1), coarsen)

        def finish(s):
            (xl, xh, yl, yh, zl, zh) = [wide(ref, s) for ref in level[5:]]
            row, lane = index_along(xl.shape, 0), index_along(xl.shape, 1)
            inside = row < ny
            total = xl + xh + yl + yh + zl + zh
            inverse = jnp.where(inside, OMEGA / jnp.where(inside, total, 1.0), 0.0)
            level[3][s] = inverse
            level[4][s] = jnp.where(inside, (1.0 / OMEGA) * total, 0.0)
            ends = (
                (lane < across) & (s == 0), (lane >= nz - across) & (s == many - 1), row == 0, row >= ny - 1,
                lane % span < step, lane % span >= span - step,
            )
            for ref, value, end in zip(level[5:], (xl, xh, yl, yh, zl, zh), ends):
                ref[s] = jnp.where(end, 0.0, value * inverse)

        each_group(many, finish)

    apart = next(
        (l for l in range(3, LEVELS + 1) if counts[l - 1][0] <= PACK and counts[l - 1][1] == EDGE), LEVELS + 1
    )

    def cells(l):
        return [(x, z) for x in range(counts[l][0]) for z in range(nz >> l)]

    def first_lane(l, x, z):
        return x * lane_step(l) + z * 2 ** (l - 2)

    def lane_of(value, lane):
        return lanes_at(value, jnp.full(value.shape, lane, jnp.int32))

    def set_apart(l):
        for k, ref in enumerate(level_refs[l][3:]):
            value = ref[0]
            for repeat in range((EDGE // counts[l][1]).bit_length() - 1):
                stretch(value, k)
                value = temp[k, pl.ds(0, EDGE), :]
            for i, (x, z) in enumerate(cells(l)):
                apart_refs[l][k, i] = lane_of(value, first_lane(l, x, z))

    for l in range(apart, LEVELS + 1):
        set_apart(l)

    window_wait(source_copy, 2, REACH, True)
    for t in range(2 * REACH + 1):
        for k, part in enumerate((even_part, odd_part)):
            i = 2 * t + k
            if abs(t - REACH) > 1:
                f1[i] = part(w1[t], 1)
                f1[i, pl.ds(EDGE, by), :] = part(wh[t].astype(jnp.float32), 1)
            else:
                for start in (0, EDGE + by):
                    f1[i, pl.ds(start, EDGE), :] = part(w1[t, pl.ds(start, EDGE), :], 1)
    for i in range(1, planes1 - 1):
        ua[i + 1] = inv1[i] * f1[i]
    sweep(level1, ua, ub, 2, 2, planes1 - 2)

    gather_all(g2, 1).wait_recv()

    f2 = level2[2]

    def unpack(t):
        place = index_along((half, nz), 1) // span
        for j in range(ngy):
            packs = [g2[(q * groups(2) + t) * ngy + j] for q in range(PACK)]
            moved = [roll(pack, span, 1) for pack in packs]
            for a in range(2):
                out = packs[a]
                for q in range(PACK):
                    out = jnp.where(place == q, packs[q] if q % 2 == a else moved[q], out)
                f2[t, pl.ds(j * cy + a * half, half), :] = out

    each_group(groups(2), unpack)

    def beside(l, v, s):
        many, across = groups(l), lane_step(l)
        low, high = v[(s + many - 1) % many], v[(s + 1) % many]
        if isinstance(s, int):
            low = roll(low, across, 1) if s == 0 else low
            high = roll(high, -across, 1) if s == many - 1 else high
        else:
            low = jnp.where(s == 0, roll(low, across, 1), low)
            high = jnp.where(s == many - 1, roll(high, -across, 1), high)
        return low, high

    def around(l, v, s):
        step = 2 ** (l - 2)
        faces = level_refs[l][5:]
        here = v[s]
        parts = [
            faces[4][s] * roll(here, step, 1) + faces[5][s] * roll(here, -step, 1),
            faces[2][s] * roll(here, 1, 0) + faces[3][s] * roll(here, -1, 0),
        ]
        if counts[l][0] == 2:
            parts.append((faces[0][s] + faces[1][s]) * roll(here, lane_step(l), 1))
        elif counts[l][0] > 1:
            low, high = beside(l, v, s)
            parts.append(faces[0][s] * low + faces[1][s] * high)
        return parts

    def made(l, ref, value):
        many = groups(l)
        if many <= GROUPS:
            return [value(s) for s in range(many)]
        each_group(many, lambda s: store(ref, s, value(s)))
        return ref

    def smooth(l, constant, v, ref):
        def value(s):
            parts = around(l, v, s)
            total = (1.0 - OMEGA) * v[s] + constant[s]
            return sum(parts[1:], parts[0]) + total

        return made(l, ref, value)

    def pair_copies(value, copies):
        even = index_along(value.shape, 0) // copies % 2 == 0
        return value + jnp.where(even, roll(value, -copies, 0), roll(value, copies, 0))

    def cycle_apart(l, f):
        copies = EDGE // counts[l][1]
        every = cells(l)
        weights = {c: [apart_refs[l][k, i] for k in range(8)] for i, c in enumerate(every)}
        constant = {c: weights[c][0] * f[c] for c in every}

        def smooth_apart(v):
            out = {}
            for x, z in every:
                here = v[x, z]
                (xl, xh, yl, yh, zl, zh) = weights[x, z][2:]
                out[x, z] = (yl * roll(here, copies, 0) + yh * roll(here, -copies, 0)) + (
                    (1.0 - OMEGA) * here + constant[x, z]
                )
                beside_x = [w * v[x + d, z] for w, d in ((xl, -1), (xh, 1)) if (x + d, z) in v]
                beside_z = [w * v[x, z + d] for w, d in ((zl, -1), (zh, 1)) if (x, z + d) in v]
                rest = beside_x + beside_z
                if rest:
                    out[x, z] = out[x, z] + sum(rest[1:], rest[0])
            return out

        v = constant
        for repeat in range((COARSE_SWEEPS if l == LEVELS else NU) - 1):
            v = smooth_apart(v)
        if l == LEVELS:
            return v
        later = smooth_apart(v)
        rest = {c: weights[c][1] * (later[c] - v[c]) for c in every}
        source = {}
        for x, z in cells(l + 1):
            total = sum(rest[2 * x + a, 2 * z + b] for a in range(2) for b in range(2))
            source[x, z] = 0.5 * pair_copies(total, copies)
        e = cycle_apart(l + 1, source)
        v = {(x, z): v[x, z] + e[x // 2, z // 2] for x, z in every}
        for repeat in range(NU):
            v = smooth_apart(v)
        return v

    def from_apart(l, rest):
        copies = EDGE // counts[l - 1][1]
        paired = pair_copies(rest, copies)
        source = {}
        for x, z in cells(l):
            lanes = [first_lane(l - 1, 2 * x + a, 2 * z + b) for a in range(2) for b in range(2)]
            parts = [lane_of(paired, lane) for lane in lanes]
            source[x, z] = 0.5 * ((parts[0] + parts[1]) + (parts[2] + parts[3]))
        e = cycle_apart(l, source)
        lane = index_along(rest.shape, 1)
        out = None
        for x in range(counts[l][0]):
            plane = e[x, 0]
            for z in range(1, nz >> l):
                plane = jnp.where(lane % span >= z * 2 ** (l - 2), e[x, z], plane)
            out = plane if out is None else jnp.where(lane >= x * lane_step(l), plane, out)
        return out

    def cycle(l):
        nx, ny = counts[l]
        (xa, xb, f, inverse, centre) = level_refs[l][:5]
        many, across = groups(l), lane_step(l)
        constant = made(l, f, lambda s: inverse[s] * f[s])
        x, free, other = constant, xa, xb
        for repeat in range((COARSE_SWEEPS if l == LEVELS else NU) - 1):
            x = smooth(l, constant, x, free)
            free, other = other, free
        if l == LEVELS:
            return x
        later = smooth(l, constant, x, free)

        def rest(s):
            return centre[s] * (later[s] - x[s])

        if l + 1 == apart:
            x = [x[0] + from_apart(l + 1, rest(0))]
            for repeat in range(NU):
                x = smooth(l, constant, x, free)
            return x
        f_next = level_refs[l + 1][2]
        size = max(ny // 2, 4)
        if ny // 2 < EDGE:
            f_next[...] = jnp.zeros(f_next.shape, f_next.dtype)

        def restrict(s):
            r = rest(2 * s) + rest(2 * s + 1) if many > 1 else pair_lanes(rest(0), across)
            f_next[s, pl.ds(0, size), :] = 0.5 * pair_lanes(pair_rows(r, s % slots), 2 ** (l - 2))

        each_group(groups(l + 1), restrict)
        fine = cycle(l + 1)
        rows = xa.shape[1]

        def correction(s):
            slot = s % slots
            stretch(fine[s], slot)
            return temp[slot, pl.ds(0, rows), :]

        if many <= GROUPS:
            added = [correction(s) for s in range(groups(l + 1))]
            x = [x[s] + added[s // 2 if many > 1 else 0] for s in range(many)]
        else:
            def correct(s):
                e = correction(s)
                for k in (2 * s, 2 * s + 1):
                    free[k] = x[k] + e

            each_group(groups(l + 1), correct)
            x, free, other = free, other, free
        for repeat in range(NU):
            x = smooth(l, constant, x, free)
            free, other = other, free
        return x

    found = cycle(2)
    found_ref = level_refs[2][0]
    for k in range(groups(2)):
        found_ref[k] = found[k]
    found = found_ref

    row2 = pl.multiple_of(gy * cy, 8)
    below2 = pl.multiple_of(jnp.maximum(gy * cy - EDGE, 0), 8)
    above2 = pl.multiple_of(jnp.minimum(gy * cy + cy, ny2 - EDGE), 8)
    for t in range(1, 2 * REACH):
        x = gx + t - REACH
        there = (x >= 0) & (x < nx2)
        plane = jnp.clip(x, 0, nx2 - 1)
        first, group = plane // groups(2) * span, plane % groups(2)
        ends = (gy > 0, True, gy < ngy - 1)
        for row, start, count, end in zip((below2, row2, above2), (0, EDGE, EDGE + cy), (EDGE, cy, EDGE), ends):
            part = found[group, pl.ds(row, count), :]
            part = lanes_at(part, first + index_along(part.shape, 1) // PACK)
            e2[t, pl.ds(start, count), :] = jnp.where(there & end, part, 0.0)

    for t in range(1, 2 * REACH):
        slot = t % slots
        stretch(e2[t], slot)
        e = temp[slot, pl.ds(EDGE, by + 2 * EDGE), :]
        ua[2 * t + 1] = ub[2 * t + 1] + e
        ua[2 * t + 2] = ub[2 * t + 2] + e
    sweep(level1, ua, ub, 2, 3, planes1 - 3)
    sweep(level1, ub, ua, 2, 4, planes1 - 4)

    for j in range(1, blocks - 1):
        slot = j % slots
        stretch(ua[first_block + j + 1], slot)
        e = temp[slot, pl.ds(EDGE, rows0), :]
        va[2 * j + 1] = vb[2 * j + 1] + e
        va[2 * j + 2] = vb[2 * j + 2] + e
    sweep(level0, va, vb, 1, HALO - 2, HALO + lx + 2)
    sweep(level0, vb, va, 1, HALO - 1, HALO + lx + 1)
    for i in range(lx):
        k = HALO + i
        product = c0[k] * va[k + 1]
        near_sum = neighbours(level0, va, k, 1)
        own = slice(EDGE, EDGE + ly)
        scaled_ref[i] = product[own]
        rest_ref[i] = w0[k, pl.ds(EDGE, ly), :] - product[own] + near_sum[own]

    window_done(phase_copy, 0, REACH)
    window_done(f_copy, 0, 2)
    window_done(source_copy, 2, REACH, True)
    column_all().wait_send()
    for k in range(1, ngy):
        row_copy(k, 1).wait_send()
    gather_all(g2, 1).wait_send()

    @pl.when(gx == ngx - 1)
    def _():
        every = g2.at[pl.ds(0, n - 1)]
        pltpu.make_async_remote_copy(
            src_ref=every, dst_ref=every, send_sem=st.at[0], recv_sem=rt.at[0],
            device_id=(gx, (gy + 1) % ngy), device_id_type=MESH,
        ).wait_send()


def write(scaled_ref, rest_ref, scaled_out, rest_out, sems):
    copies = [
        pltpu.make_async_copy(source, target, sems.at[k])
        for k, (source, target) in enumerate(((scaled_ref, scaled_out), (rest_ref, rest_out)))
    ]
    for copy in copies:
        copy.start()
    for copy in copies:
        copy.wait()


def solution(mesh):
    ngx, ngy = mesh.shape["gx"], mesh.shape["gy"]
    n = ngx * ngy

    def on_device(right_side, phase):
        lx, ly, nz = right_side.shape
        assert lx == 4 and ly % 32 == 0 and NU == 2
        by, cy = ly // 2, ly // 4
        counts = [(lx * ngx >> l, ly * ngy >> l) for l in range(LEVELS + 1)]
        blocks = 2 * REACH + 1

        def level_scratch(planes, rows, padded_source=False):
            shapes = [planes + 2, planes + 2, planes, planes, planes, planes + 1] + [planes] * 4
            if padded_source:
                shapes[2] = 1
            large = planes * rows * nz * 4 >= LARGE
            types = [jnp.float32] * 5 + [jnp.bfloat16 if large else jnp.float32] * 5
            return [pltpu.VMEM((k, rows, nz), dtype) for k, dtype in zip(shapes, types)]

        def packed_scratch(many, rows):
            return [pltpu.VMEM((many, rows, nz), jnp.float32)] * 11

        assert counts[2][0] % PACK == 0 and nz >> 2 == nz // PACK
        scratch = [
            pltpu.VMEM((lx + 2 * HALO, ly + 2 * EDGE, nz), jnp.float32),
            pltpu.VMEM((2 * HALO, ly, nz), jnp.bfloat16),
            pltpu.VMEM((2, HALO, 2 * EDGE, nz), jnp.bfloat16),
            pltpu.VMEM((blocks, by + 2 * EDGE_PHASE, nz), jnp.bfloat16),
            pltpu.VMEM((blocks, by + 2 * EDGE, nz), jnp.float32),
            pltpu.VMEM((blocks, by, nz), jnp.bfloat16),
            pltpu.VMEM((ngy, ngx, cy, nz), jnp.bfloat16),
            pltpu.VMEM((ngy, 1, cy, nz), jnp.bfloat16),
            pltpu.VMEM((n, cy // 2, nz), jnp.float32),
            pltpu.VMEM((lx, ly, nz), jnp.int32),
            pltpu.VMEM((1, by, nz), jnp.bfloat16),
            pltpu.VMEM((lx, ly, nz), jnp.bfloat16),
            pltpu.VMEM((2, lx // 2, 2 * EDGE, nz), jnp.bfloat16),
            pltpu.VMEM((1, by, nz), jnp.float32),
            pltpu.VMEM((1, by, nz), jnp.bfloat16),
            pltpu.VMEM((1, cy, nz), jnp.bfloat16),
            pltpu.VMEM((1, cy, nz), jnp.bfloat16),
            pltpu.VMEM((1, cy // 2, nz), jnp.float32),
            pltpu.VMEM((8, max(2 * (by + 2 * EDGE), 2 * counts[2][1], 2 * (cy + 2 * EDGE)), nz), jnp.float32),
            pltpu.VMEM((2 * blocks, by + 2 * EDGE, nz), jnp.float32),
            pltpu.VMEM((blocks, cy + 2 * EDGE, nz), jnp.float32),
        ]
        scratch += level_scratch(lx + 2 * HALO, ly + 2 * EDGE, True)
        scratch += level_scratch(2 * blocks, by + 2 * EDGE)
        for l in range(2, LEVELS + 1):
            scratch += packed_scratch(max(counts[l][0] // PACK, 1), max(counts[l][1], EDGE))
        for l in range(LEVELS + 1):
            small = counts[l][1] < EDGE
            scratch += [pltpu.VMEM((8, counts[l][0] * (nz >> l) if small else 1, EDGE, nz), jnp.float32)]
        scratch += [pltpu.SemaphoreType.DMA((15,))] * 2
        scratch += [pltpu.SemaphoreType.DMA((3 * blocks,))] * 4
        scratch += [pltpu.SemaphoreType.DMA((2,))] * 2
        scratch += [pltpu.SemaphoreType.DMA((1,)), pltpu.SemaphoreType.DMA((ngy,))]
        scratch += [pltpu.SemaphoreType.DMA((ngy,)), pltpu.SemaphoreType.DMA((ngy,)), pltpu.SemaphoreType.DMA((2,))]
        scratch += [pltpu.SemaphoreType.REGULAR]
        anywhere = pl.BlockSpec(memory_space=pl.ANY)
        inside = pl.BlockSpec(memory_space=pltpu.VMEM)
        right_side, phase = [pltpu.with_memory_space_constraint(x, pltpu.HBM) for x in (right_side, phase)]
        found = pl.pallas_call(
            functools.partial(kernel, ngx, ngy, counts),
            out_shape=[pltpu.VMEM(right_side.shape, jnp.float32)] * 2,
            in_specs=[anywhere] * 2,
            out_specs=[inside] * 2,
            scratch_shapes=scratch,
            compiler_params=pltpu.CompilerParams(
                collective_id=0, has_side_effects=True, vmem_limit_bytes=64_000_000
            ),
        )(right_side, phase)
        return pl.pallas_call(
            write,
            out_shape=[jax.ShapeDtypeStruct(right_side.shape, jnp.float32)] * 2,
            in_specs=[inside] * 2,
            out_specs=[anywhere] * 2,
            scratch_shapes=[pltpu.SemaphoreType.DMA((2,))],
        )(*[pltpu.with_memory_space_constraint(x, pltpu.VMEM) for x in found])

    placed = P("gx", "gy", None)
    return jax.shard_map(
        on_device, mesh=mesh, in_specs=(placed, placed), out_specs=(placed, placed), check_vma=False
    )
```

```python
import functools

import jax
import jax.numpy as jnp
import numpy as np
from jax import lax
from jax.experimental import pallas as pl
from jax.experimental.pallas import tpu as pltpu
from jax.sharding import PartitionSpec as P

LEVELS = 6
NU = 2
COARSE_SWEEPS = 6
OMEGA = 0.8
LIQUID, GAS = 1.0, 1000.0
MIXED = float(np.asarray(2.0 * LIQUID * GAS / (LIQUID + GAS), jnp.bfloat16))
MESH = pl.DeviceIdType.MESH
REACH = 3
HALO = 6
PACK = 4
GROUPS = 4
EDGE = 8
EDGE_PHASE = 16
UNROLL = 16
LARGE = 1 << 20


def each(count, body):
    if count <= UNROLL:
        for i in range(count):
            body(i)
    else:
        lax.fori_loop(0, count, lambda i, carry: (body(i), carry)[1], 0)


def each_group(count, body):
    if count <= GROUPS:
        for i in range(count):
            body(i)
    else:
        lax.fori_loop(0, count, lambda i, carry: (body(i), carry)[1], 0)


def index_along(shape, axis):
    return lax.broadcasted_iota(jnp.int32, shape, axis)


def roll(x, shift, axis):
    return pltpu.roll(x, shift % x.shape[axis], axis)


def lane_bit(x, step):
    return index_along(x.shape, x.ndim - 1) // step % 2


def even_part(x, step):
    return jnp.where(lane_bit(x, step) == 0, x, roll(x, step, x.ndim - 1))


def odd_part(x, step):
    return jnp.where(lane_bit(x, step) == 1, x, roll(x, -step, x.ndim - 1))


def lanes_at(x, index):
    return jnp.take_along_axis(x, index, axis=1, mode="promise_in_bounds")


def pair_lanes(x, step):
    axis = x.ndim - 1
    return x + jnp.where(lane_bit(x, step) == 0, roll(x, -step, axis), roll(x, step, axis))


def harmonic(a, b):
    low, high = jnp.minimum(a, b), jnp.maximum(a, b)
    return jnp.where((low == 0.0) | (low == high), high, MIXED)


def store(ref, i, value):
    ref[i] = value.astype(ref.dtype)


def wide(ref, i):
    return ref[i].astype(jnp.float32)


def quarter(x):
    return (0.25 * x).astype(jnp.bfloat16).astype(jnp.float32)


def kernel(ngx, ngy, counts, f_hbm, phase_hbm, scaled_ref, rest_ref, *refs):
    gx, gy = lax.axis_index("gx"), lax.axis_index("gy")
    n = ngx * ngy
    me = gx * ngy + gy
    lx, ly, nz = f_hbm.shape
    by, cy = ly // 2, ly // 4
    refs = list(refs)

    def take(count):
        out = refs[:count]
        del refs[:count]
        return out

    (w0, wn, wc, wp, w1, wh, gf, gt, g2) = take(9)
    (phase_ref, p_pack, f_pack, c_pack, g1_pack, h_pack, f2_pack, t_pack, g2_pack, temp) = take(10)
    (b1, e2) = take(2)
    level_refs = [take(10 if l < 2 else 11) for l in range(LEVELS + 1)]
    apart_refs = [take(1)[0] for l in range(LEVELS + 1)]
    (s0, r0, s1, r1, sp, rp, sg, rg, st, rt, sr, rr, si, all_in) = take(14)

    own_f = w0.at[pl.ds(HALO, lx), pl.ds(EDGE, ly), :]
    load_phase = pltpu.make_async_copy(phase_hbm, phase_ref, si.at[0])
    load_f = pltpu.make_async_copy(f_hbm, own_f, si.at[1])
    load_phase.start()
    load_f.start()

    for start in (0, EDGE + ly):
        w0[:, pl.ds(start, EDGE), :] = jnp.zeros((w0.shape[0], EDGE, nz), w0.dtype)
    for ref in (wn, wc, wp, w1, wh):
        ref[...] = jnp.zeros(ref.shape, ref.dtype)

    barrier = pltpu.get_barrier_semaphore()

    m = max(k for k in range(1, ngx + 1) if ngx % k == 0 and k * k <= ngx)
    greeted = 0

    def greet(x, y, there):
        pl.when(there)(
            lambda: pl.semaphore_signal(barrier, inc=1, device_id=(x, y), device_id_type=MESH)
        )
        return greeted + jnp.where(there, 1, 0)

    mates = [(c * m + gx % m, gy, gx // m != c) for c in range(ngx // m)]
    for d in sorted(range(-REACH, REACH + 1), key=abs):
        for e in (0, 1, -1):
            if (d, e) != (0, 0):
                x, y = gx + d, gy + e
                greeted = greet(x, y, (x >= 0) & (x < ngx) & (y >= 0) & (y < ngy))
    for x, y, there in mates:
        greeted = greet(x, y, there & (jnp.abs(x - gx) > REACH))
    for a in range(m):
        for y in range(ngy):
            x = gx // m * m + a
            column = (x == gx) & (y == gy)
            if m - 1 > REACH or ngy > 2:
                greeted = greet(x, y, ((jnp.abs(x - gx) > REACH) | (jnp.abs(y - gy) > 1)) & ~column)

    for l in range(2):
        for v in level_refs[l][:2]:
            zero = jnp.zeros(v.shape[1:], v.dtype)
            v[0] = zero
            v[v.shape[0] - 1] = zero

    load_phase.wait()
    for plane in range(0, lx, 4):
        beta = [
            jnp.where(phase_ref[plane + 2 * k, pl.ds(0, by, 2), :] == 1, GAS, LIQUID) for k in range(2)
        ]
        p_pack[0] = jnp.where(lane_bit(beta[0], 1) == 0, beta[0], beta[1]).astype(jnp.bfloat16)
    load_f.wait()
    f_pack[...] = own_f[...].astype(jnp.bfloat16)
    for side, start in enumerate((EDGE, ly)):
        for k in range(lx // 2):
            rows = [w0[HALO + 2 * k + i, pl.ds(start, EDGE), :] for i in range(2)]
            c_pack[side, k] = jnp.concatenate(rows, axis=0).astype(c_pack.dtype)

    pl.semaphore_wait(barrier, greeted)

    def window_copy(src, dst, send, recv, reach, edge, d, e, to):
        lead, rows = src.shape[0], src.shape[1]
        count = rows if e == 0 else edge
        source = src.at[:, pl.ds(rows - edge if e == 1 else 0, count), :]
        start = {0: edge, 1: 0, -1: edge + rows}[e]
        target = dst.at[pl.ds((reach - d) * lead, lead), pl.ds(start, count), :]
        k = (d + reach) * 3 + e + 1
        return pltpu.make_async_remote_copy(
            src_ref=source, dst_ref=target, send_sem=send.at[k], recv_sem=recv.at[k],
            device_id=(gx + to * d, gy + to * e), device_id_type=MESH,
        )

    def source_copy(d, e, to):
        if e == 0 and abs(d) > 1:
            source, target = h_pack, wh.at[pl.ds(REACH - d, 1)]
        else:
            return window_copy(g1_pack, w1, s1, r1, REACH, EDGE, d, e, to)
        k = (d + REACH) * 3 + e + 1
        return pltpu.make_async_remote_copy(
            src_ref=source, dst_ref=target, send_sem=s1.at[k], recv_sem=r1.at[k],
            device_id=(gx + to * d, gy + to * e), device_id_type=MESH,
        )

    def phase_copy(d, e, to):
        return window_copy(p_pack, wp, sp, rp, REACH, EDGE_PHASE, d, e, to)

    def f_copy(d, e, to):
        first, count = {0: (0, lx), 1: (0, lx), -1: (0, lx), 2: (lx - 2, 2), -2: (0, 2)}[d]
        low = {0: 0, 1: HALO - lx, 2: 0, -1: HALO, -2: HALO + lx}[d]
        side = 0 if e == 1 else 1
        if d == 0:
            source = own_f.at[:, pl.ds(ly - EDGE if e == 1 else 0, EDGE), :]
            target = w0.at[pl.ds(HALO, lx), pl.ds(0 if e == 1 else EDGE + ly, EDGE), :]
        elif e == 0:
            source, target = f_pack.at[pl.ds(first, count)], wn.at[pl.ds(low, count)]
        else:
            source = c_pack.at[1 - side, pl.ds(first // 2, count // 2)]
            target = wc.at[side, pl.ds(low // 2, count // 2)]
        k = (d + 2) * 3 + e + 1
        return pltpu.make_async_remote_copy(
            src_ref=source, dst_ref=target, send_sem=s0.at[k], recv_sem=r0.at[k],
            device_id=(gx + to * d, gy + to * e), device_id_type=MESH,
        )

    def each_near(low, high, body, near=None, to=1):
        for d in sorted(range(-high, high + 1), key=abs):
            for e in (0, 1, -1):
                if (d, e) != (0, 0) and (abs(d) >= low or (near is not None and e != 0)):
                    x, y = gx + to * d, gy + to * e
                    pl.when((x >= 0) & (x < ngx) & (y >= 0) & (y < ngy))(functools.partial(body, d, e))

    def window_send(copy, low, high, near=None):
        each_near(low, high, lambda d, e: copy(d, e, 1).start(), near)

    def window_wait(copy, low, high, near=None):
        each_near(low, high, lambda d, e: copy(d, e, -1).wait_recv(), near, -1)

    def window_done(copy, low, high, near=None):
        each_near(low, high, lambda d, e: copy(d, e, 1).wait_send(), near)

    def gather_send(src, dst, k):
        def body(t, carry):
            other = jnp.where(t <= me, t - 1, t)
            pltpu.make_async_remote_copy(
                src_ref=src, dst_ref=dst.at[pl.ds(me, 1)], send_sem=sg.at[k], recv_sem=rg.at[k],
                device_id=(other // ngy, other % ngy), device_id_type=MESH,
            ).start()
            return carry

        lax.fori_loop(1, n, body, 0)

    def gather_all(dst, k):
        every = dst.at[pl.ds(0, n - 1)]
        return pltpu.make_async_remote_copy(
            src_ref=every, dst_ref=every, send_sem=sg.at[k], recv_sem=rg.at[k],
            device_id=(gx, (gy + 1) % ngy), device_id_type=MESH,
        )

    def top_copy(j, other):
        return pltpu.make_async_remote_copy(
            src_ref=t_pack, dst_ref=gt.at[j], send_sem=st.at[0], recv_sem=rt.at[j],
            device_id=(other // ngy, other % ngy), device_id_type=MESH,
        )

    window_send(phase_copy, 0, 2)
    window_send(f_copy, 0, 2)
    for x, y, there in mates:
        pl.when(there)(functools.partial(pl.semaphore_signal, all_in, inc=1, device_id=(x, y), device_id_type=MESH))
    wp[REACH, pl.ds(EDGE_PHASE, by), :] = p_pack[0]

    slots = temp.shape[0]

    def stretch(value, slot):
        rows = value.shape[0]
        temp[slot, pl.ds(0, rows, 2), :] = value
        temp[slot, pl.ds(1, rows, 2), :] = value

    def pair_rows(value, slot, first=True, second=True):
        rows = value.shape[0]
        temp[slot, pl.ds(0, rows), :] = value
        out = 0.0
        if first:
            out = out + temp[slot, pl.ds(0, rows // 2, 2), :]
        if second:
            out = out + temp[slot, pl.ds(1, rows // 2, 2), :]
        return out

    def neighbours(level, v_ref, i, step):
        (_, _, _, _, _, fx, fyl, fyh, fzl, fzh) = level
        v = v_ref[i + 1]
        return (
            wide(fx, i) * v_ref[i] + wide(fx, i + 1) * v_ref[i + 2]
            + wide(fyl, i) * roll(v, 1, 0) + wide(fyh, i) * roll(v, -1, 0)
            + wide(fzl, i) * roll(v, step, 1) + wide(fzh, i) * roll(v, -step, 1)
        )

    def sweep(level, source, target, step, first, last):
        f, inverse = level[2], level[3]

        def body(k):
            i = k + first
            target[i + 1] = (1.0 - OMEGA) * source[i + 1] + inverse[i] * (f[i] + neighbours(level, source, i, step))

        each(last - first, body)

    def rest_of(level, v_ref, i, step):
        return level[2][i] - level[4][i] * v_ref[i + 1] + neighbours(level, v_ref, i, step)

    def put_faces(level, i, inside, lows, step, edges):
        (_, _, _, inverse, centre, fx, fyl, fyh, fzl, fzh) = level
        (yl, yh, zl, zh) = lows
        total = wide(fx, i) + wide(fx, i + 1) + yl + yh + zl + zh
        inverse[i] = jnp.where(inside, OMEGA / jnp.where(inside, total, 1.0), 0.0)
        centre[i] = total
        lane = index_along(zl.shape, 1)
        fzl[i] = jnp.where(lane < step, 0.0, zl).astype(fzl.dtype)
        fzh[i] = jnp.where(lane >= nz - step, 0.0, zh).astype(fzh.dtype)
        if edges is not None:
            row = index_along(yl.shape, 0)
            yl = jnp.where(row == 0, 0.0, yl)
            yh = jnp.where(row >= edges - 1, 0.0, yh)
        fyl[i] = yl.astype(fyl.dtype)
        fyh[i] = yh.astype(fyh.dtype)

    def cell_faces(b, step):
        lane = index_along(b.shape, 1)
        yl, yh = harmonic(roll(b, 1, 0), b), harmonic(b, roll(b, -1, 0))
        zl = harmonic(jnp.where(lane < step, 0.0, roll(b, step, 1)), b)
        zh = harmonic(b, jnp.where(lane >= nz - step, 0.0, roll(b, -step, 1)))
        return yl, yh, zl, zh

    def phase_block(t):
        packed = wp[t].astype(jnp.float32)[EDGE_PHASE - EDGE : EDGE_PHASE + by + EDGE]
        b1[2 * t] = even_part(packed, 1)
        b1[2 * t + 1] = odd_part(packed, 1)

    window_wait(phase_copy, 0, 1)
    for t in range(REACH - 1, REACH + 2):
        phase_block(t)

    own1 = 2 * REACH
    level1 = level_refs[1]
    (ua, ub, f1, inv1, c1, fx1) = level1[:6]
    planes1 = 2 * (2 * REACH + 1)
    near = range(own1 - 2, own1 + 4)

    def own_faces():
        own = slice(EDGE, EDGE + by)
        below, low, high, above = [b1[own1 + k] for k in range(-1, 3)]
        lane = index_along((by, nz), 1)
        pair = [low, high]
        mine = [b[own] for b in pair]
        x_low = quarter(pair_lanes(pair_rows(harmonic(below, low)[own], 0), 2))
        x_high = quarter(pair_lanes(pair_rows(harmonic(high, above)[own], 1), 2))
        y_low = sum(harmonic(roll(b, 1, 0), b)[own] for b in pair)
        y_high = sum(harmonic(b, roll(b, -1, 0))[own] for b in pair)
        z_low = sum(harmonic(jnp.where(lane < 2, 0.0, roll(b, 2, 1)), b) for b in mine)
        z_high = sum(harmonic(b, jnp.where(lane >= nz - 2, 0.0, roll(b, -2, 1))) for b in mine)
        y_low = quarter(pair_lanes(pair_rows(y_low, 2, second=False), 2))
        y_high = quarter(pair_lanes(pair_rows(y_high, 3, first=False), 2))
        z_low = quarter(even_part(pair_rows(z_low, 4), 2))
        z_high = quarter(odd_part(pair_rows(z_high, 5), 2))
        row, lane = index_along((cy, nz), 0), index_along((cy, nz), 1)
        corner = (row == cy - 2) & (lane // 4 == nz // 4 - 2)
        edge = jnp.where(corner, roll(roll(z_high, -1, 0), -4, 1), z_high)
        edge = jnp.where(row == cy - 1, y_high, edge)
        mixed = edge
        for k, value in enumerate((x_low, y_low, z_low)):
            mixed = jnp.where(lane % 4 == k, value, mixed)
        f2_pack[0] = mixed.astype(f2_pack.dtype)
        t_pack[0] = x_high.astype(t_pack.dtype)

    own_faces()
    pl.semaphore_wait(all_in, ngx // m - 1)
    def column_copy(t):
        other = jnp.where(t <= gx, t - 1, t)
        return pltpu.make_async_remote_copy(
            src_ref=f2_pack, dst_ref=gf.at[gy, pl.ds(gx, 1)], send_sem=sg.at[0], recv_sem=rg.at[0],
            device_id=(other, gy), device_id_type=MESH,
        )

    lax.fori_loop(1, ngx, lambda t, carry: (column_copy(t).start(), carry)[1], 0)
    gf[gy, gx] = f2_pack[0]
    for j in range(ngy):
        @pl.when((gx == ngx - 1) & (gy == j))
        def _():
            def body(t, carry):
                top_copy(j, (me + t) % n).start()
                return carry

            lax.fori_loop(1, n, body, 0)
            gt[j, 0] = t_pack[0]
    window_wait(phase_copy, 2, 2)
    phase_block(REACH - 2)
    phase_block(REACH + 2)

    level0 = list(level_refs[0])
    level0[2] = w0
    (va, vb, f0, inv0, c0, fx0) = level0[:6]
    rows0 = ly + 2 * EDGE
    planes0 = lx + 2 * HALO
    blocks = planes0 // 2
    first_block = own1 - HALO // 2

    def fine_beta(j):
        slot = (j + 1) % slots
        stretch(b1[first_block + j], slot)
        return temp[slot, pl.ds(EDGE, rows0), :]

    def fine_faces(j):
        lows = cell_faces(beta0[j], 1)
        for i in (2 * j, 2 * j + 1):
            put_faces(level0, i, beta0[j] > 0.0, lows, 1, None)

    beta0 = [fine_beta(j) for j in range(-1, blocks + 1)]
    for j in range(blocks + 1):
        fx0[2 * j] = harmonic(beta0[j], beta0[j + 1])
        if j < blocks:
            fx0[2 * j + 1] = beta0[j + 1]
    beta0 = beta0[1:-1]
    for j in range(blocks):
        fine_faces(j)

    window_send(phase_copy, REACH, REACH)

    for i in range(near[0], near[-1] + 2):
        fx1[i] = harmonic(b1[i - 1], b1[i])
    for i in near:
        put_faces(level1, i, b1[i] > 0.0, cell_faces(b1[i], 2), 2, None)

    for i in near:
        f1[i] = jnp.zeros(f1.shape[1:], f1.dtype)

    def fill(planes):
        for plane in planes:
            i = plane if plane < HALO else plane - lx
            w0[plane, pl.ds(EDGE, ly), :] = wn[i].astype(w0.dtype)
            for side, start in enumerate((0, EDGE + ly)):
                rows = wc[side, i // 2, pl.ds(0, 2 * EDGE), :].astype(w0.dtype)
                w0[plane, pl.ds(start, EDGE), :] = rows[EDGE:] if i % 2 else rows[:EDGE]

    def start_fine(planes):
        for i in planes:
            va[i + 1] = inv0[i] * w0[i]

    def source_plane(k):
        plane = 2 * (near[0] + k - first_block)
        r = rest_of(level0, vb, plane, 1) + rest_of(level0, vb, plane + 1, 1)
        f1[near[0] + k, pl.ds(EDGE // 2, rows0 // 2), :] = 0.5 * pair_lanes(pair_rows(r, k % slots), 1)

    inner = range(HALO - lx, HALO + 2 * lx)
    outer = [i for i in range(planes0) if i not in inner]
    window_wait(f_copy, 0, 1)
    fill([i for i in inner if not HALO <= i < HALO + lx])
    start_fine(inner)
    sweep(level0, va, vb, 1, inner[0] + 1, inner[-1])
    for k in range(1, len(near) - 1):
        source_plane(k)
    coarse = [f1[own1 + k, pl.ds(EDGE, by), :] for k in range(2)]
    packed = jnp.where(lane_bit(coarse[0], 1) == 0, coarse[0], coarse[1])
    g1_pack[0] = packed
    h_pack[0] = packed.astype(h_pack.dtype)
    window_send(source_copy, 2, REACH, True)

    window_wait(f_copy, 2, 2)
    fill(outer)
    start_fine(outer)
    sweep(level0, va, vb, 1, 1, inner[0] + 1)
    sweep(level0, va, vb, 1, inner[-1], planes0 - 1)
    source_plane(0)
    source_plane(len(near) - 1)
    for i in near:
        ua[i + 1] = inv1[i] * f1[i]
    sweep(level1, ua, ub, 2, near[0] + 1, near[-1])
    rests = [rest_of(level1, ub, own1 + i, 2)[EDGE : EDGE + by] for i in range(2)]
    coarse = 0.5 * pair_lanes(pair_rows(rests[0] + rests[1], 0), 2)
    half = cy // 2
    coarse = lanes_at(coarse, index_along(coarse.shape, 1) % (nz // PACK) * PACK)
    packed = jnp.where(lane_bit(coarse[:half], nz // PACK) == 0, coarse[:half], coarse[half:])
    g2_pack[0] = packed
    gather_send(g2_pack, g2, 1)
    g2[me] = packed

    window_wait(phase_copy, REACH, REACH)
    phase_block(0)
    phase_block(2 * REACH)
    far = [i for i in range(1, planes1 - 1) if i not in near]
    for i in range(1, planes1):
        if not near[0] <= i <= near[-1] + 1:
            fx1[i] = harmonic(b1[i - 1], b1[i])
    for i in far:
        put_faces(level1, i, b1[i] > 0.0, cell_faces(b1[i], 2), 2, None)

    def column_all():
        every = gf.at[pl.ds(gy, 1), pl.ds(0, ngx - 1)]
        return pltpu.make_async_remote_copy(
            src_ref=every, dst_ref=every, send_sem=sg.at[0], recv_sem=rg.at[0],
            device_id=(gx, (gy + 1) % ngy), device_id_type=MESH,
        )

    def row_copy(k, to):
        part = gf.at[pl.ds(gy if to > 0 else (gy + ngy - k) % ngy, 1)]
        return pltpu.make_async_remote_copy(
            src_ref=part, dst_ref=part, send_sem=sr.at[k], recv_sem=rr.at[k],
            device_id=(gx, (gy + ngy + to * k) % ngy), device_id_type=MESH,
        )

    column_all().wait_recv()
    for k in range(1, ngy):
        row_copy(k, 1).start()
    for k in range(1, ngy):
        row_copy(k, -1).wait_recv()
    for j in range(ngy):
        @pl.when((gx < ngx - 1) | (gy != j))
        def _():
            top_copy(j, me).wait_recv()

    shape2 = counts[2]
    (nx2, ny2) = shape2
    level2 = level_refs[2]
    span = nz // PACK

    def groups(l):
        return max(counts[l][0] // PACK, 1)

    def lane_step(l):
        return nz // min(counts[l][0], PACK)

    row_p, lane_p = index_along((nz, PACK * nz), 0), index_along((nz, PACK * nz), 1)
    picks = []
    for q in range(PACK):
        chosen = (row_p == PACK * (lane_p % span) + lane_p // nz) & (lane_p % nz // span == q)
        picks.append(jnp.where(chosen, 1.0, 0.0).astype(jnp.bfloat16))

    def whole_plane(ref, k):
        return jnp.concatenate([ref[j, k].astype(jnp.float32) for j in range(ngy)], axis=0)

    def spread(x, columns):
        return jnp.dot(x.astype(jnp.bfloat16), columns, preferred_element_type=jnp.float32)

    many = groups(2)
    row2, lane2 = index_along((ny2, nz), 0), index_along((ny2, nz), 1)

    def faces2(t):
        parts = sum(spread(whole_plane(gf, q * many + t), picks[q]) for q in range(PACK))
        x_low, y_low, z_low, edge = [parts[:, k * nz : (k + 1) * nz] for k in range(4)]
        y_high = jnp.where(row2 == ny2 - 1, edge, roll(y_low, -1, 0))
        z_edge = jnp.where(row2 % cy == cy - 1, roll(roll(edge, 1, 0), 1, 1), edge)
        z_high = jnp.where(lane2 % span == span - 1, z_edge, roll(z_low, -1, 1))
        for ref, value in zip(level2[5:6] + level2[7:], (x_low, y_low, y_high, z_low, z_high)):
            store(ref, t, value)

    each_group(many, faces2)
    top = spread(whole_plane(gt, 0), picks[PACK - 1])[:, :nz]

    def faces2_high(t):
        after = wide(level2[5], (t + 1) % many)
        around = jnp.where(lane2 >= nz - span, top, roll(after, -span, 1))
        store(level2[6], t, jnp.where(t == many - 1, around, after))

    each_group(many, faces2_high)

    for l in range(2, LEVELS + 1):
        nx, ny = counts[l]
        step, across, many = 2 ** (l - 2), lane_step(l), groups(l)
        level = level_refs[l]
        if l < LEVELS:
            coarser = level_refs[l + 1]
            size = max(ny // 2, 4)
            if ny // 2 < EDGE:
                for ref in coarser[5:]:
                    ref[...] = jnp.zeros(ref.shape, ref.dtype)

            def put(ref, s, value):
                ref[s, pl.ds(0, size), :] = quarter(value).astype(ref.dtype)

            def coarsen(s):
                slot = 4 * (s % 2)
                if many > 1:
                    low = lambda ref: wide(ref, 2 * s)
                    high = lambda ref: wide(ref, 2 * s + 1)
                    both = lambda ref: low(ref) + high(ref)
                else:
                    low = lambda ref: even_part(wide(ref, 0), across)
                    high = lambda ref: odd_part(wide(ref, 0), across)
                    both = lambda ref: pair_lanes(wide(ref, 0), across)
                (xl, xh, yl, yh, zl, zh) = level[5:]
                put(coarser[5], s, pair_lanes(pair_rows(low(xl), slot), step))
                put(coarser[6], s, pair_lanes(pair_rows(high(xh), slot + 1), step))
                put(coarser[7], s, pair_lanes(pair_rows(both(yl), slot + 2, second=False), step))
                put(coarser[8], s, pair_lanes(pair_rows(both(yh), slot + 3, first=False), step))
                put(coarser[9], s, even_part(pair_rows(both(zl), slot), step))
                put(coarser[10], s, odd_part(pair_rows(both(zh), slot + 1), step))

            each_group(groups(l + 1), coarsen)

        def finish(s):
            (xl, xh, yl, yh, zl, zh) = [wide(ref, s) for ref in level[5:]]
            row, lane = index_along(xl.shape, 0), index_along(xl.shape, 1)
            inside = row < ny
            total = xl + xh + yl + yh + zl + zh
            inverse = jnp.where(inside, OMEGA / jnp.where(inside, total, 1.0), 0.0)
            level[3][s] = inverse
            level[4][s] = jnp.where(inside, (1.0 / OMEGA) * total, 0.0)
            ends = (
                (lane < across) & (s == 0), (lane >= nz - across) & (s == many - 1), row == 0, row >= ny - 1,
                lane % span < step, lane % span >= span - step,
            )
            for ref, value, end in zip(level[5:], (xl, xh, yl, yh, zl, zh), ends):
                ref[s] = jnp.where(end, 0.0, value * inverse)

        each_group(many, finish)

    apart = next(
        (l for l in range(3, LEVELS + 1) if counts[l - 1][0] <= PACK and counts[l - 1][1] == EDGE), LEVELS + 1
    )

    def cells(l):
        return [(x, z) for x in range(counts[l][0]) for z in range(nz >> l)]

    def first_lane(l, x, z):
        return x * lane_step(l) + z * 2 ** (l - 2)

    def lane_of(value, lane):
        return lanes_at(value, jnp.full(value.shape, lane, jnp.int32))

    def set_apart(l):
        for k, ref in enumerate(level_refs[l][3:]):
            value = ref[0]
            for repeat in range((EDGE // counts[l][1]).bit_length() - 1):
                stretch(value, k)
                value = temp[k, pl.ds(0, EDGE), :]
            for i, (x, z) in enumerate(cells(l)):
                apart_refs[l][k, i] = lane_of(value, first_lane(l, x, z))

    for l in range(apart, LEVELS + 1):
        set_apart(l)

    window_wait(source_copy, 2, REACH, True)
    for t in range(2 * REACH + 1):
        for k, part in enumerate((even_part, odd_part)):
            i = 2 * t + k
            if abs(t - REACH) > 1:
                f1[i] = part(w1[t], 1)
                f1[i, pl.ds(EDGE, by), :] = part(wh[t].astype(jnp.float32), 1)
            else:
                for start in (0, EDGE + by):
                    f1[i, pl.ds(start, EDGE), :] = part(w1[t, pl.ds(start, EDGE), :], 1)
    for i in range(1, planes1 - 1):
        ua[i + 1] = inv1[i] * f1[i]
    sweep(level1, ua, ub, 2, 2, planes1 - 2)

    window_done(phase_copy, 0, REACH)
    window_done(f_copy, 0, 2)
    window_done(source_copy, 2, REACH, True)
    column_all().wait_send()
    for k in range(1, ngy):
        row_copy(k, 1).wait_send()
    @pl.when(gx == ngx - 1)
    def _():
        every = g2.at[pl.ds(0, n - 1)]
        pltpu.make_async_remote_copy(
            src_ref=every, dst_ref=every, send_sem=st.at[0], recv_sem=rt.at[0],
            device_id=(gx, (gy + 1) % ngy), device_id_type=MESH,
        ).wait_send()

    gather_all(g2, 1).wait_recv()

    f2 = level2[2]

    def unpack(t):
        place = index_along((half, nz), 1) // span
        for j in range(ngy):
            packs = [g2[(q * groups(2) + t) * ngy + j] for q in range(PACK)]
            moved = [roll(pack, span, 1) for pack in packs]
            for a in range(2):
                out = packs[a]
                for q in range(PACK):
                    out = jnp.where(place == q, packs[q] if q % 2 == a else moved[q], out)
                f2[t, pl.ds(j * cy + a * half, half), :] = out

    each_group(groups(2), unpack)

    def beside(l, v, s):
        many, across = groups(l), lane_step(l)
        low, high = v[(s + many - 1) % many], v[(s + 1) % many]
        if isinstance(s, int):
            low = roll(low, across, 1) if s == 0 else low
            high = roll(high, -across, 1) if s == many - 1 else high
        else:
            low = jnp.where(s == 0, roll(low, across, 1), low)
            high = jnp.where(s == many - 1, roll(high, -across, 1), high)
        return low, high

    def around(l, v, s):
        step = 2 ** (l - 2)
        faces = level_refs[l][5:]
        here = v[s]
        parts = [
            faces[4][s] * roll(here, step, 1) + faces[5][s] * roll(here, -step, 1),
            faces[2][s] * roll(here, 1, 0) + faces[3][s] * roll(here, -1, 0),
        ]
        if counts[l][0] == 2:
            parts.append((faces[0][s] + faces[1][s]) * roll(here, lane_step(l), 1))
        elif counts[l][0] > 1:
            low, high = beside(l, v, s)
            parts.append(faces[0][s] * low + faces[1][s] * high)
        return parts

    def made(l, ref, value):
        many = groups(l)
        if many <= GROUPS:
            return [value(s) for s in range(many)]
        each_group(many, lambda s: store(ref, s, value(s)))
        return ref

    def smooth(l, constant, v, ref):
        def value(s):
            parts = around(l, v, s)
            total = (1.0 - OMEGA) * v[s] + constant[s]
            return sum(parts[1:], parts[0]) + total

        return made(l, ref, value)

    def pair_copies(value, copies):
        even = index_along(value.shape, 0) // copies % 2 == 0
        return value + jnp.where(even, roll(value, -copies, 0), roll(value, copies, 0))

    def cycle_apart(l, f):
        copies = EDGE // counts[l][1]
        every = cells(l)
        weights = {c: [apart_refs[l][k, i] for k in range(8)] for i, c in enumerate(every)}
        constant = {c: weights[c][0] * f[c] for c in every}

        def smooth_apart(v):
            out = {}
            for x, z in every:
                here = v[x, z]
                (xl, xh, yl, yh, zl, zh) = weights[x, z][2:]
                out[x, z] = (yl * roll(here, copies, 0) + yh * roll(here, -copies, 0)) + (
                    (1.0 - OMEGA) * here + constant[x, z]
                )
                beside_x = [w * v[x + d, z] for w, d in ((xl, -1), (xh, 1)) if (x + d, z) in v]
                beside_z = [w * v[x, z + d] for w, d in ((zl, -1), (zh, 1)) if (x, z + d) in v]
                rest = beside_x + beside_z
                if rest:
                    out[x, z] = out[x, z] + sum(rest[1:], rest[0])
            return out

        v = constant
        for repeat in range((COARSE_SWEEPS if l == LEVELS else NU) - 1):
            v = smooth_apart(v)
        if l == LEVELS:
            return v
        later = smooth_apart(v)
        rest = {c: weights[c][1] * (later[c] - v[c]) for c in every}
        source = {}
        for x, z in cells(l + 1):
            total = sum(rest[2 * x + a, 2 * z + b] for a in range(2) for b in range(2))
            source[x, z] = 0.5 * pair_copies(total, copies)
        e = cycle_apart(l + 1, source)
        v = {(x, z): v[x, z] + e[x // 2, z // 2] for x, z in every}
        for repeat in range(NU):
            v = smooth_apart(v)
        return v

    def from_apart(l, rest):
        copies = EDGE // counts[l - 1][1]
        paired = pair_copies(rest, copies)
        source = {}
        for x, z in cells(l):
            lanes = [first_lane(l - 1, 2 * x + a, 2 * z + b) for a in range(2) for b in range(2)]
            parts = [lane_of(paired, lane) for lane in lanes]
            source[x, z] = 0.5 * ((parts[0] + parts[1]) + (parts[2] + parts[3]))
        e = cycle_apart(l, source)
        lane = index_along(rest.shape, 1)
        out = None
        for x in range(counts[l][0]):
            plane = e[x, 0]
            for z in range(1, nz >> l):
                plane = jnp.where(lane % span >= z * 2 ** (l - 2), e[x, z], plane)
            out = plane if out is None else jnp.where(lane >= x * lane_step(l), plane, out)
        return out

    def cycle(l):
        nx, ny = counts[l]
        (xa, xb, f, inverse, centre) = level_refs[l][:5]
        many, across = groups(l), lane_step(l)
        constant = made(l, f, lambda s: inverse[s] * f[s])
        x, free, other = constant, xa, xb
        for repeat in range((COARSE_SWEEPS if l == LEVELS else NU) - 1):
            x = smooth(l, constant, x, free)
            free, other = other, free
        if l == LEVELS:
            return x
        later = smooth(l, constant, x, free)

        def rest(s):
            return centre[s] * (later[s] - x[s])

        if l + 1 == apart:
            x = [x[0] + from_apart(l + 1, rest(0))]
            for repeat in range(NU):
                x = smooth(l, constant, x, free)
            return x
        f_next = level_refs[l + 1][2]
        size = max(ny // 2, 4)
        if ny // 2 < EDGE:
            f_next[...] = jnp.zeros(f_next.shape, f_next.dtype)

        def restrict(s):
            r = rest(2 * s) + rest(2 * s + 1) if many > 1 else pair_lanes(rest(0), across)
            f_next[s, pl.ds(0, size), :] = 0.5 * pair_lanes(pair_rows(r, s % slots), 2 ** (l - 2))

        each_group(groups(l + 1), restrict)
        fine = cycle(l + 1)
        rows = xa.shape[1]

        def correction(s):
            slot = s % slots
            stretch(fine[s], slot)
            return temp[slot, pl.ds(0, rows), :]

        if many <= GROUPS:
            added = [correction(s) for s in range(groups(l + 1))]
            x = [x[s] + added[s // 2 if many > 1 else 0] for s in range(many)]
        else:
            def correct(s):
                e = correction(s)
                for k in (2 * s, 2 * s + 1):
                    free[k] = x[k] + e

            each_group(groups(l + 1), correct)
            x, free, other = free, other, free
        for repeat in range(NU):
            x = smooth(l, constant, x, free)
            free, other = other, free
        return x

    found = cycle(2)
    found_ref = level_refs[2][0]
    for k in range(groups(2)):
        found_ref[k] = found[k]
    found = found_ref

    row2 = pl.multiple_of(gy * cy, 8)
    below2 = pl.multiple_of(jnp.maximum(gy * cy - EDGE, 0), 8)
    above2 = pl.multiple_of(jnp.minimum(gy * cy + cy, ny2 - EDGE), 8)
    for t in range(1, 2 * REACH):
        x = gx + t - REACH
        there = (x >= 0) & (x < nx2)
        plane = jnp.clip(x, 0, nx2 - 1)
        first, group = plane // groups(2) * span, plane % groups(2)
        ends = (gy > 0, True, gy < ngy - 1)
        for row, start, count, end in zip((below2, row2, above2), (0, EDGE, EDGE + cy), (EDGE, cy, EDGE), ends):
            part = found[group, pl.ds(row, count), :]
            part = lanes_at(part, first + index_along(part.shape, 1) // PACK)
            e2[t, pl.ds(start, count), :] = jnp.where(there & end, part, 0.0)

    for t in range(1, 2 * REACH):
        slot = t % slots
        stretch(e2[t], slot)
        e = temp[slot, pl.ds(EDGE, by + 2 * EDGE), :]
        ua[2 * t + 1] = ub[2 * t + 1] + e
        ua[2 * t + 2] = ub[2 * t + 2] + e
    sweep(level1, ua, ub, 2, 3, planes1 - 3)
    sweep(level1, ub, ua, 2, 4, planes1 - 4)

    for j in range(1, blocks - 1):
        slot = j % slots
        stretch(ua[first_block + j + 1], slot)
        e = temp[slot, pl.ds(EDGE, rows0), :]
        va[2 * j + 1] = vb[2 * j + 1] + e
        va[2 * j + 2] = vb[2 * j + 2] + e
    sweep(level0, va, vb, 1, HALO - 2, HALO + lx + 2)
    sweep(level0, vb, va, 1, HALO - 1, HALO + lx + 1)
    for i in range(lx):
        k = HALO + i
        product = c0[k] * va[k + 1]
        near_sum = neighbours(level0, va, k, 1)
        own = slice(EDGE, EDGE + ly)
        scaled_ref[i] = product[own]
        rest_ref[i] = w0[k, pl.ds(EDGE, ly), :] - product[own] + near_sum[own]

    gather_all(g2, 1).wait_send()


def write(scaled_ref, rest_ref, scaled_out, rest_out, sems):
    copies = [
        pltpu.make_async_copy(source, target, sems.at[k])
        for k, (source, target) in enumerate(((scaled_ref, scaled_out), (rest_ref, rest_out)))
    ]
    for copy in copies:
        copy.start()
    for copy in copies:
        copy.wait()


def solution(mesh):
    ngx, ngy = mesh.shape["gx"], mesh.shape["gy"]
    n = ngx * ngy

    def on_device(right_side, phase):
        lx, ly, nz = right_side.shape
        assert lx == 4 and ly % 32 == 0 and NU == 2
        by, cy = ly // 2, ly // 4
        counts = [(lx * ngx >> l, ly * ngy >> l) for l in range(LEVELS + 1)]
        blocks = 2 * REACH + 1

        def level_scratch(planes, rows, padded_source=False):
            shapes = [planes + 2, planes + 2, planes, planes, planes, planes + 1] + [planes] * 4
            if padded_source:
                shapes[2] = 1
            large = planes * rows * nz * 4 >= LARGE
            types = [jnp.float32] * 5 + [jnp.bfloat16 if large else jnp.float32] * 5
            return [pltpu.VMEM((k, rows, nz), dtype) for k, dtype in zip(shapes, types)]

        def packed_scratch(many, rows):
            return [pltpu.VMEM((many, rows, nz), jnp.float32)] * 11

        assert counts[2][0] % PACK == 0 and nz >> 2 == nz // PACK
        scratch = [
            pltpu.VMEM((lx + 2 * HALO, ly + 2 * EDGE, nz), jnp.float32),
            pltpu.VMEM((2 * HALO, ly, nz), jnp.bfloat16),
            pltpu.VMEM((2, HALO, 2 * EDGE, nz), jnp.bfloat16),
            pltpu.VMEM((blocks, by + 2 * EDGE_PHASE, nz), jnp.bfloat16),
            pltpu.VMEM((blocks, by + 2 * EDGE, nz), jnp.float32),
            pltpu.VMEM((blocks, by, nz), jnp.bfloat16),
            pltpu.VMEM((ngy, ngx, cy, nz), jnp.bfloat16),
            pltpu.VMEM((ngy, 1, cy, nz), jnp.bfloat16),
            pltpu.VMEM((n, cy // 2, nz), jnp.float32),
            pltpu.VMEM((lx, ly, nz), jnp.int32),
            pltpu.VMEM((1, by, nz), jnp.bfloat16),
            pltpu.VMEM((lx, ly, nz), jnp.bfloat16),
            pltpu.VMEM((2, lx // 2, 2 * EDGE, nz), jnp.bfloat16),
            pltpu.VMEM((1, by, nz), jnp.float32),
            pltpu.VMEM((1, by, nz), jnp.bfloat16),
            pltpu.VMEM((1, cy, nz), jnp.bfloat16),
            pltpu.VMEM((1, cy, nz), jnp.bfloat16),
            pltpu.VMEM((1, cy // 2, nz), jnp.float32),
            pltpu.VMEM((8, max(2 * (by + 2 * EDGE), 2 * counts[2][1], 2 * (cy + 2 * EDGE)), nz), jnp.float32),
            pltpu.VMEM((2 * blocks, by + 2 * EDGE, nz), jnp.float32),
            pltpu.VMEM((blocks, cy + 2 * EDGE, nz), jnp.float32),
        ]
        scratch += level_scratch(lx + 2 * HALO, ly + 2 * EDGE, True)
        scratch += level_scratch(2 * blocks, by + 2 * EDGE)
        for l in range(2, LEVELS + 1):
            scratch += packed_scratch(max(counts[l][0] // PACK, 1), max(counts[l][1], EDGE))
        for l in range(LEVELS + 1):
            small = counts[l][1] < EDGE
            scratch += [pltpu.VMEM((8, counts[l][0] * (nz >> l) if small else 1, EDGE, nz), jnp.float32)]
        scratch += [pltpu.SemaphoreType.DMA((15,))] * 2
        scratch += [pltpu.SemaphoreType.DMA((3 * blocks,))] * 4
        scratch += [pltpu.SemaphoreType.DMA((2,))] * 2
        scratch += [pltpu.SemaphoreType.DMA((1,)), pltpu.SemaphoreType.DMA((ngy,))]
        scratch += [pltpu.SemaphoreType.DMA((ngy,)), pltpu.SemaphoreType.DMA((ngy,)), pltpu.SemaphoreType.DMA((2,))]
        scratch += [pltpu.SemaphoreType.REGULAR]
        anywhere = pl.BlockSpec(memory_space=pl.ANY)
        inside = pl.BlockSpec(memory_space=pltpu.VMEM)
        right_side, phase = [pltpu.with_memory_space_constraint(x, pltpu.HBM) for x in (right_side, phase)]
        found = pl.pallas_call(
            functools.partial(kernel, ngx, ngy, counts),
            out_shape=[pltpu.VMEM(right_side.shape, jnp.float32)] * 2,
            in_specs=[anywhere] * 2,
            out_specs=[inside] * 2,
            scratch_shapes=scratch,
            compiler_params=pltpu.CompilerParams(
                collective_id=0, has_side_effects=True, vmem_limit_bytes=64_000_000
            ),
        )(right_side, phase)
        return pl.pallas_call(
            write,
            out_shape=[jax.ShapeDtypeStruct(right_side.shape, jnp.float32)] * 2,
            in_specs=[inside] * 2,
            out_specs=[anywhere] * 2,
            scratch_shapes=[pltpu.SemaphoreType.DMA((2,))],
        )(*[pltpu.with_memory_space_constraint(x, pltpu.VMEM) for x in found])

    placed = P("gx", "gy", None)
    return jax.shard_map(
        on_device, mesh=mesh, in_specs=(placed, placed), out_specs=(placed, placed), check_vma=False
    )
```

```python
import functools

import jax
import jax.numpy as jnp
import numpy as np
from jax import lax
from jax.experimental import pallas as pl
from jax.experimental.pallas import tpu as pltpu
from jax.sharding import PartitionSpec as P

LEVELS = 6
NU = 2
COARSE_SWEEPS = 6
OMEGA = 0.8
LIQUID, GAS = 1.0, 1000.0
MIXED = float(np.asarray(2.0 * LIQUID * GAS / (LIQUID + GAS), jnp.bfloat16))
MESH = pl.DeviceIdType.MESH
REACH = 3
HALO = 6
PACK = 4
GROUPS = 4
EDGE = 8
EDGE_PHASE = 16
UNROLL = 16
LARGE = 1 << 20


def each(count, body):
    if count <= UNROLL:
        for i in range(count):
            body(i)
    else:
        lax.fori_loop(0, count, lambda i, carry: (body(i), carry)[1], 0)


def each_group(count, body):
    if count <= GROUPS:
        for i in range(count):
            body(i)
    else:
        lax.fori_loop(0, count, lambda i, carry: (body(i), carry)[1], 0)


def index_along(shape, axis):
    return lax.broadcasted_iota(jnp.int32, shape, axis)


def roll(x, shift, axis):
    return pltpu.roll(x, shift % x.shape[axis], axis)


def lane_bit(x, step):
    return index_along(x.shape, x.ndim - 1) // step % 2


def even_part(x, step):
    return jnp.where(lane_bit(x, step) == 0, x, roll(x, step, x.ndim - 1))


def odd_part(x, step):
    return jnp.where(lane_bit(x, step) == 1, x, roll(x, -step, x.ndim - 1))


def lanes_at(x, index):
    return jnp.take_along_axis(x, index, axis=1, mode="promise_in_bounds")


def pair_lanes(x, step):
    axis = x.ndim - 1
    return x + jnp.where(lane_bit(x, step) == 0, roll(x, -step, axis), roll(x, step, axis))


def harmonic(a, b):
    low, high = jnp.minimum(a, b), jnp.maximum(a, b)
    return jnp.where((low == 0.0) | (low == high), high, MIXED)


def store(ref, i, value):
    ref[i] = value.astype(ref.dtype)


def wide(ref, i):
    return ref[i].astype(jnp.float32)


def quarter(x):
    return (0.25 * x).astype(jnp.bfloat16).astype(jnp.float32)


def kernel(ngx, ngy, counts, f_hbm, phase_hbm, scaled_ref, rest_ref, *refs):
    gx, gy = lax.axis_index("gx"), lax.axis_index("gy")
    n = ngx * ngy
    me = gx * ngy + gy
    lx, ly, nz = f_hbm.shape
    by, cy = ly // 2, ly // 4
    refs = list(refs)

    def take(count):
        out = refs[:count]
        del refs[:count]
        return out

    (w0, wn, wc, wp, w1, wh, gf, gt, g2) = take(9)
    (phase_ref, p_pack, f_pack, c_pack, g1_pack, h_pack, f2_pack, t_pack, g2_pack, temp) = take(10)
    (b1, e2) = take(2)
    level_refs = [take(10 if l < 2 else 11) for l in range(LEVELS + 1)]
    apart_refs = [take(1)[0] for l in range(LEVELS + 1)]
    (s0, r0, s1, r1, sp, rp, sg, rg, st, rt, sr, rr, si, all_in) = take(14)

    own_f = w0.at[pl.ds(HALO, lx), pl.ds(EDGE, ly), :]
    load_phase = pltpu.make_async_copy(phase_hbm, phase_ref, si.at[0])
    load_f = pltpu.make_async_copy(f_hbm, own_f, si.at[1])
    load_phase.start()
    load_f.start()

    for start in (0, EDGE + ly):
        w0[:, pl.ds(start, EDGE), :] = jnp.zeros((w0.shape[0], EDGE, nz), w0.dtype)
    for ref in (wn, wc, wp, w1, wh):
        ref[...] = jnp.zeros(ref.shape, ref.dtype)

    barrier = pltpu.get_barrier_semaphore()

    m = max(k for k in range(1, ngx + 1) if ngx % k == 0 and k * k <= ngx)
    greeted = 0

    def greet(x, y, there):
        pl.when(there)(
            lambda: pl.semaphore_signal(barrier, inc=1, device_id=(x, y), device_id_type=MESH)
        )
        return greeted + jnp.where(there, 1, 0)

    mates = [(c * m + gx % m, gy, gx // m != c) for c in range(ngx // m)]
    for d in sorted(range(-REACH, REACH + 1), key=abs):
        for e in (0, 1, -1):
            if (d, e) != (0, 0):
                x, y = gx + d, gy + e
                greeted = greet(x, y, (x >= 0) & (x < ngx) & (y >= 0) & (y < ngy))
    for x, y, there in mates:
        greeted = greet(x, y, there & (jnp.abs(x - gx) > REACH))
    for a in range(m):
        for y in range(ngy):
            x = gx // m * m + a
            column = (x == gx) & (y == gy)
            if m - 1 > REACH or ngy > 2:
                greeted = greet(x, y, ((jnp.abs(x - gx) > REACH) | (jnp.abs(y - gy) > 1)) & ~column)

    for l in range(2):
        for v in level_refs[l][:2]:
            zero = jnp.zeros(v.shape[1:], v.dtype)
            v[0] = zero
            v[v.shape[0] - 1] = zero

    load_phase.wait()
    for plane in range(0, lx, 4):
        beta = [
            jnp.where(phase_ref[plane + 2 * k, pl.ds(0, by, 2), :] == 1, GAS, LIQUID) for k in range(2)
        ]
        p_pack[0] = jnp.where(lane_bit(beta[0], 1) == 0, beta[0], beta[1]).astype(jnp.bfloat16)
    load_f.wait()
    f_pack[...] = own_f[...].astype(jnp.bfloat16)
    for side, start in enumerate((EDGE, ly)):
        for k in range(lx // 2):
            rows = [w0[HALO + 2 * k + i, pl.ds(start, EDGE), :] for i in range(2)]
            c_pack[side, k] = jnp.concatenate(rows, axis=0).astype(c_pack.dtype)

    pl.semaphore_wait(barrier, greeted)

    def window_copy(src, dst, send, recv, reach, edge, d, e, to):
        lead, rows = src.shape[0], src.shape[1]
        count = rows if e == 0 else edge
        source = src.at[:, pl.ds(rows - edge if e == 1 else 0, count), :]
        start = {0: edge, 1: 0, -1: edge + rows}[e]
        target = dst.at[pl.ds((reach - d) * lead, lead), pl.ds(start, count), :]
        k = (d + reach) * 3 + e + 1
        return pltpu.make_async_remote_copy(
            src_ref=source, dst_ref=target, send_sem=send.at[k], recv_sem=recv.at[k],
            device_id=(gx + to * d, gy + to * e), device_id_type=MESH,
        )

    def source_copy(d, e, to):
        if e == 0 and abs(d) > 1:
            source, target = h_pack, wh.at[pl.ds(REACH - d, 1)]
        else:
            return window_copy(g1_pack, w1, s1, r1, REACH, EDGE, d, e, to)
        k = (d + REACH) * 3 + e + 1
        return pltpu.make_async_remote_copy(
            src_ref=source, dst_ref=target, send_sem=s1.at[k], recv_sem=r1.at[k],
            device_id=(gx + to * d, gy + to * e), device_id_type=MESH,
        )

    def phase_copy(d, e, to):
        return window_copy(p_pack, wp, sp, rp, REACH, EDGE_PHASE, d, e, to)

    def f_copy(d, e, to):
        first, count = {0: (0, lx), 1: (0, lx), -1: (0, lx), 2: (lx - 2, 2), -2: (0, 2)}[d]
        low = {0: 0, 1: HALO - lx, 2: 0, -1: HALO, -2: HALO + lx}[d]
        side = 0 if e == 1 else 1
        if d == 0:
            source = own_f.at[:, pl.ds(ly - EDGE if e == 1 else 0, EDGE), :]
            target = w0.at[pl.ds(HALO, lx), pl.ds(0 if e == 1 else EDGE + ly, EDGE), :]
        elif e == 0:
            source, target = f_pack.at[pl.ds(first, count)], wn.at[pl.ds(low, count)]
        else:
            source = c_pack.at[1 - side, pl.ds(first // 2, count // 2)]
            target = wc.at[side, pl.ds(low // 2, count // 2)]
        k = (d + 2) * 3 + e + 1
        return pltpu.make_async_remote_copy(
            src_ref=source, dst_ref=target, send_sem=s0.at[k], recv_sem=r0.at[k],
            device_id=(gx + to * d, gy + to * e), device_id_type=MESH,
        )

    def each_near(low, high, body, near=None, to=1):
        for d in sorted(range(-high, high + 1), key=abs):
            for e in (0, 1, -1):
                if (d, e) != (0, 0) and (abs(d) >= low or (near is not None and e != 0)):
                    x, y = gx + to * d, gy + to * e
                    pl.when((x >= 0) & (x < ngx) & (y >= 0) & (y < ngy))(functools.partial(body, d, e))

    def window_send(copy, low, high, near=None):
        each_near(low, high, lambda d, e: copy(d, e, 1).start(), near)

    def window_wait(copy, low, high, near=None):
        each_near(low, high, lambda d, e: copy(d, e, -1).wait_recv(), near, -1)

    def window_done(copy, low, high, near=None):
        each_near(low, high, lambda d, e: copy(d, e, 1).wait_send(), near)

    def gather_send(src, dst, k):
        def body(t, carry):
            other = jnp.where(t <= me, t - 1, t)
            pltpu.make_async_remote_copy(
                src_ref=src, dst_ref=dst.at[pl.ds(me, 1)], send_sem=sg.at[k], recv_sem=rg.at[k],
                device_id=(other // ngy, other % ngy), device_id_type=MESH,
            ).start()
            return carry

        lax.fori_loop(1, n, body, 0)

    def gather_all(dst, k):
        every = dst.at[pl.ds(0, n - 1)]
        return pltpu.make_async_remote_copy(
            src_ref=every, dst_ref=every, send_sem=sg.at[k], recv_sem=rg.at[k],
            device_id=(gx, (gy + 1) % ngy), device_id_type=MESH,
        )

    def top_copy(j, other):
        return pltpu.make_async_remote_copy(
            src_ref=t_pack, dst_ref=gt.at[j], send_sem=st.at[0], recv_sem=rt.at[j],
            device_id=(other // ngy, other % ngy), device_id_type=MESH,
        )

    window_send(phase_copy, 0, 2)
    window_send(f_copy, 0, 2)
    for x, y, there in mates:
        pl.when(there)(functools.partial(pl.semaphore_signal, all_in, inc=1, device_id=(x, y), device_id_type=MESH))
    wp[REACH, pl.ds(EDGE_PHASE, by), :] = p_pack[0]

    slots = temp.shape[0]

    def stretch(value, slot):
        rows = value.shape[0]
        temp[slot, pl.ds(0, rows, 2), :] = value
        temp[slot, pl.ds(1, rows, 2), :] = value

    def pair_rows(value, slot, first=True, second=True):
        rows = value.shape[0]
        temp[slot, pl.ds(0, rows), :] = value
        out = 0.0
        if first:
            out = out + temp[slot, pl.ds(0, rows // 2, 2), :]
        if second:
            out = out + temp[slot, pl.ds(1, rows // 2, 2), :]
        return out

    def neighbours(level, v_ref, i, step):
        (_, _, _, _, _, fx, fyl, fyh, fzl, fzh) = level
        v = v_ref[i + 1]
        return (
            wide(fx, i) * v_ref[i] + wide(fx, i + 1) * v_ref[i + 2]
            + wide(fyl, i) * roll(v, 1, 0) + wide(fyh, i) * roll(v, -1, 0)
            + wide(fzl, i) * roll(v, step, 1) + wide(fzh, i) * roll(v, -step, 1)
        )

    def sweep(level, source, target, step, first, last):
        f, inverse = level[2], level[3]

        def body(k):
            i = k + first
            target[i + 1] = (1.0 - OMEGA) * source[i + 1] + inverse[i] * (f[i] + neighbours(level, source, i, step))

        each(last - first, body)

    def rest_of(level, v_ref, i, step):
        return level[2][i] - level[4][i] * v_ref[i + 1] + neighbours(level, v_ref, i, step)

    def put_faces(level, i, inside, lows, step, edges):
        (_, _, _, inverse, centre, fx, fyl, fyh, fzl, fzh) = level
        (yl, yh, zl, zh) = lows
        total = wide(fx, i) + wide(fx, i + 1) + yl + yh + zl + zh
        inverse[i] = jnp.where(inside, OMEGA / jnp.where(inside, total, 1.0), 0.0)
        centre[i] = total
        lane = index_along(zl.shape, 1)
        fzl[i] = jnp.where(lane < step, 0.0, zl).astype(fzl.dtype)
        fzh[i] = jnp.where(lane >= nz - step, 0.0, zh).astype(fzh.dtype)
        if edges is not None:
            row = index_along(yl.shape, 0)
            yl = jnp.where(row == 0, 0.0, yl)
            yh = jnp.where(row >= edges - 1, 0.0, yh)
        fyl[i] = yl.astype(fyl.dtype)
        fyh[i] = yh.astype(fyh.dtype)

    def cell_faces(b, step):
        lane = index_along(b.shape, 1)
        yl, yh = harmonic(roll(b, 1, 0), b), harmonic(b, roll(b, -1, 0))
        zl = harmonic(jnp.where(lane < step, 0.0, roll(b, step, 1)), b)
        zh = harmonic(b, jnp.where(lane >= nz - step, 0.0, roll(b, -step, 1)))
        return yl, yh, zl, zh

    def phase_block(t):
        packed = wp[t].astype(jnp.float32)[EDGE_PHASE - EDGE : EDGE_PHASE + by + EDGE]
        b1[2 * t] = even_part(packed, 1)
        b1[2 * t + 1] = odd_part(packed, 1)

    window_wait(phase_copy, 0, 1)
    for t in range(REACH - 1, REACH + 2):
        phase_block(t)

    own1 = 2 * REACH
    level1 = level_refs[1]
    (ua, ub, f1, inv1, c1, fx1) = level1[:6]
    planes1 = 2 * (2 * REACH + 1)
    near = range(own1 - 2, own1 + 4)

    def own_faces():
        own = slice(EDGE, EDGE + by)
        below, low, high, above = [b1[own1 + k] for k in range(-1, 3)]
        lane = index_along((by, nz), 1)
        pair = [low, high]
        mine = [b[own] for b in pair]
        x_low = quarter(pair_lanes(pair_rows(harmonic(below, low)[own], 0), 2))
        x_high = quarter(pair_lanes(pair_rows(harmonic(high, above)[own], 1), 2))
        y_low = sum(harmonic(roll(b, 1, 0), b)[own] for b in pair)
        y_high = sum(harmonic(b, roll(b, -1, 0))[own] for b in pair)
        z_low = sum(harmonic(jnp.where(lane < 2, 0.0, roll(b, 2, 1)), b) for b in mine)
        z_high = sum(harmonic(b, jnp.where(lane >= nz - 2, 0.0, roll(b, -2, 1))) for b in mine)
        y_low = quarter(pair_lanes(pair_rows(y_low, 2, second=False), 2))
        y_high = quarter(pair_lanes(pair_rows(y_high, 3, first=False), 2))
        z_low = quarter(even_part(pair_rows(z_low, 4), 2))
        z_high = quarter(odd_part(pair_rows(z_high, 5), 2))
        row, lane = index_along((cy, nz), 0), index_along((cy, nz), 1)
        corner = (row == cy - 2) & (lane // 4 == nz // 4 - 2)
        edge = jnp.where(corner, roll(roll(z_high, -1, 0), -4, 1), z_high)
        edge = jnp.where(row == cy - 1, y_high, edge)
        mixed = edge
        for k, value in enumerate((x_low, y_low, z_low)):
            mixed = jnp.where(lane % 4 == k, value, mixed)
        f2_pack[0] = mixed.astype(f2_pack.dtype)
        t_pack[0] = x_high.astype(t_pack.dtype)

    own_faces()
    pl.semaphore_wait(all_in, ngx // m - 1)
    def column_copy(t):
        other = jnp.where(t <= gx, t - 1, t)
        return pltpu.make_async_remote_copy(
            src_ref=f2_pack, dst_ref=gf.at[gy, pl.ds(gx, 1)], send_sem=sg.at[0], recv_sem=rg.at[0],
            device_id=(other, gy), device_id_type=MESH,
        )

    lax.fori_loop(1, ngx, lambda t, carry: (column_copy(t).start(), carry)[1], 0)
    gf[gy, gx] = f2_pack[0]
    for j in range(ngy):
        @pl.when((gx == ngx - 1) & (gy == j))
        def _():
            def body(t, carry):
                top_copy(j, (me + t) % n).start()
                return carry

            lax.fori_loop(1, n, body, 0)
            gt[j, 0] = t_pack[0]
    window_wait(phase_copy, 2, 2)
    phase_block(REACH - 2)
    phase_block(REACH + 2)

    level0 = list(level_refs[0])
    level0[2] = w0
    (va, vb, f0, inv0, c0, fx0) = level0[:6]
    rows0 = ly + 2 * EDGE
    planes0 = lx + 2 * HALO
    blocks = planes0 // 2
    first_block = own1 - HALO // 2

    def fine_beta(j):
        slot = (j + 1) % slots
        stretch(b1[first_block + j], slot)
        return temp[slot, pl.ds(EDGE, rows0), :]

    def fine_faces(j):
        lows = cell_faces(beta0[j], 1)
        for i in (2 * j, 2 * j + 1):
            put_faces(level0, i, beta0[j] > 0.0, lows, 1, None)

    beta0 = [fine_beta(j) for j in range(-1, blocks + 1)]
    for j in range(blocks + 1):
        fx0[2 * j] = harmonic(beta0[j], beta0[j + 1])
        if j < blocks:
            fx0[2 * j + 1] = beta0[j + 1]
    beta0 = beta0[1:-1]
    for j in range(blocks):
        fine_faces(j)

    window_send(phase_copy, REACH, REACH)

    for i in range(near[0], near[-1] + 2):
        fx1[i] = harmonic(b1[i - 1], b1[i])
    for i in near:
        put_faces(level1, i, b1[i] > 0.0, cell_faces(b1[i], 2), 2, None)

    for i in near:
        f1[i] = jnp.zeros(f1.shape[1:], f1.dtype)

    def fill(planes):
        for plane in planes:
            i = plane if plane < HALO else plane - lx
            w0[plane, pl.ds(EDGE, ly), :] = wn[i].astype(w0.dtype)
            for side, start in enumerate((0, EDGE + ly)):
                rows = wc[side, i // 2, pl.ds(0, 2 * EDGE), :].astype(w0.dtype)
                w0[plane, pl.ds(start, EDGE), :] = rows[EDGE:] if i % 2 else rows[:EDGE]

    def start_fine(planes):
        for i in planes:
            va[i + 1] = inv0[i] * w0[i]

    def source_plane(k):
        plane = 2 * (near[0] + k - first_block)
        r = rest_of(level0, vb, plane, 1) + rest_of(level0, vb, plane + 1, 1)
        f1[near[0] + k, pl.ds(EDGE // 2, rows0 // 2), :] = 0.5 * pair_lanes(pair_rows(r, k % slots), 1)

    inner = range(HALO - lx, HALO + 2 * lx)
    outer = [i for i in range(planes0) if i not in inner]
    own = range(HALO, HALO + lx)
    window_wait(f_copy, 0, 0)
    start_fine(own)
    sweep(level0, va, vb, 1, own[0] + 1, own[-1])
    window_wait(f_copy, 1, 1)
    fill([i for i in inner if i not in own])
    start_fine([i for i in inner if i not in own])
    sweep(level0, va, vb, 1, inner[0] + 1, own[0] + 1)
    sweep(level0, va, vb, 1, own[-1], inner[-1])
    for k in range(1, len(near) - 1):
        source_plane(k)
    coarse = [f1[own1 + k, pl.ds(EDGE, by), :] for k in range(2)]
    packed = jnp.where(lane_bit(coarse[0], 1) == 0, coarse[0], coarse[1])
    g1_pack[0] = packed
    h_pack[0] = packed.astype(h_pack.dtype)

    window_wait(f_copy, 2, 2)
    fill(outer)
    start_fine(outer)
    sweep(level0, va, vb, 1, 1, inner[0] + 1)
    sweep(level0, va, vb, 1, inner[-1], planes0 - 1)
    source_plane(0)
    source_plane(len(near) - 1)
    for i in near:
        ua[i + 1] = inv1[i] * f1[i]
    sweep(level1, ua, ub, 2, near[0] + 1, near[-1])
    rests = [rest_of(level1, ub, own1 + i, 2)[EDGE : EDGE + by] for i in range(2)]
    coarse = 0.5 * pair_lanes(pair_rows(rests[0] + rests[1], 0), 2)
    half = cy // 2
    coarse = lanes_at(coarse, index_along(coarse.shape, 1) % (nz // PACK) * PACK)
    packed = jnp.where(lane_bit(coarse[:half], nz // PACK) == 0, coarse[:half], coarse[half:])
    g2_pack[0] = packed
    gather_send(g2_pack, g2, 1)
    g2[me] = packed
    window_send(source_copy, 2, REACH, True)

    window_wait(phase_copy, REACH, REACH)
    phase_block(0)
    phase_block(2 * REACH)
    far = [i for i in range(1, planes1 - 1) if i not in near]
    for i in range(1, planes1):
        if not near[0] <= i <= near[-1] + 1:
            fx1[i] = harmonic(b1[i - 1], b1[i])
    for i in far:
        put_faces(level1, i, b1[i] > 0.0, cell_faces(b1[i], 2), 2, None)

    def column_all():
        every = gf.at[pl.ds(gy, 1), pl.ds(0, ngx - 1)]
        return pltpu.make_async_remote_copy(
            src_ref=every, dst_ref=every, send_sem=sg.at[0], recv_sem=rg.at[0],
            device_id=(gx, (gy + 1) % ngy), device_id_type=MESH,
        )

    def row_copy(k, to):
        part = gf.at[pl.ds(gy if to > 0 else (gy + ngy - k) % ngy, 1)]
        return pltpu.make_async_remote_copy(
            src_ref=part, dst_ref=part, send_sem=sr.at[k], recv_sem=rr.at[k],
            device_id=(gx, (gy + ngy + to * k) % ngy), device_id_type=MESH,
        )

    column_all().wait_recv()
    for k in range(1, ngy):
        row_copy(k, 1).start()
    for k in range(1, ngy):
        row_copy(k, -1).wait_recv()
    for j in range(ngy):
        @pl.when((gx < ngx - 1) | (gy != j))
        def _():
            top_copy(j, me).wait_recv()

    shape2 = counts[2]
    (nx2, ny2) = shape2
    level2 = level_refs[2]
    span = nz // PACK

    def groups(l):
        return max(counts[l][0] // PACK, 1)

    def lane_step(l):
        return nz // min(counts[l][0], PACK)

    row_p, lane_p = index_along((nz, PACK * nz), 0), index_along((nz, PACK * nz), 1)
    picks = []
    for q in range(PACK):
        chosen = (row_p == PACK * (lane_p % span) + lane_p // nz) & (lane_p % nz // span == q)
        picks.append(jnp.where(chosen, 1.0, 0.0).astype(jnp.bfloat16))

    def whole_plane(ref, k):
        return jnp.concatenate([ref[j, k].astype(jnp.float32) for j in range(ngy)], axis=0)

    def spread(x, columns):
        return jnp.dot(x.astype(jnp.bfloat16), columns, preferred_element_type=jnp.float32)

    many = groups(2)
    row2, lane2 = index_along((ny2, nz), 0), index_along((ny2, nz), 1)

    def faces2(t):
        parts = sum(spread(whole_plane(gf, q * many + t), picks[q]) for q in range(PACK))
        x_low, y_low, z_low, edge = [parts[:, k * nz : (k + 1) * nz] for k in range(4)]
        y_high = jnp.where(row2 == ny2 - 1, edge, roll(y_low, -1, 0))
        z_edge = jnp.where(row2 % cy == cy - 1, roll(roll(edge, 1, 0), 1, 1), edge)
        z_high = jnp.where(lane2 % span == span - 1, z_edge, roll(z_low, -1, 1))
        for ref, value in zip(level2[5:6] + level2[7:], (x_low, y_low, y_high, z_low, z_high)):
            store(ref, t, value)

    each_group(many, faces2)
    top = spread(whole_plane(gt, 0), picks[PACK - 1])[:, :nz]

    def faces2_high(t):
        after = wide(level2[5], (t + 1) % many)
        around = jnp.where(lane2 >= nz - span, top, roll(after, -span, 1))
        store(level2[6], t, jnp.where(t == many - 1, around, after))

    each_group(many, faces2_high)

    for l in range(2, LEVELS + 1):
        nx, ny = counts[l]
        step, across, many = 2 ** (l - 2), lane_step(l), groups(l)
        level = level_refs[l]
        if l < LEVELS:
            coarser = level_refs[l + 1]
            size = max(ny // 2, 4)
            if ny // 2 < EDGE:
                for ref in coarser[5:]:
                    ref[...] = jnp.zeros(ref.shape, ref.dtype)

            def put(ref, s, value):
                ref[s, pl.ds(0, size), :] = quarter(value).astype(ref.dtype)

            def coarsen(s):
                slot = 4 * (s % 2)
                if many > 1:
                    low = lambda ref: wide(ref, 2 * s)
                    high = lambda ref: wide(ref, 2 * s + 1)
                    both = lambda ref: low(ref) + high(ref)
                else:
                    low = lambda ref: even_part(wide(ref, 0), across)
                    high = lambda ref: odd_part(wide(ref, 0), across)
                    both = lambda ref: pair_lanes(wide(ref, 0), across)
                (xl, xh, yl, yh, zl, zh) = level[5:]
                put(coarser[5], s, pair_lanes(pair_rows(low(xl), slot), step))
                put(coarser[6], s, pair_lanes(pair_rows(high(xh), slot + 1), step))
                put(coarser[7], s, pair_lanes(pair_rows(both(yl), slot + 2, second=False), step))
                put(coarser[8], s, pair_lanes(pair_rows(both(yh), slot + 3, first=False), step))
                put(coarser[9], s, even_part(pair_rows(both(zl), slot), step))
                put(coarser[10], s, odd_part(pair_rows(both(zh), slot + 1), step))

            each_group(groups(l + 1), coarsen)

        def finish(s):
            (xl, xh, yl, yh, zl, zh) = [wide(ref, s) for ref in level[5:]]
            row, lane = index_along(xl.shape, 0), index_along(xl.shape, 1)
            inside = row < ny
            total = xl + xh + yl + yh + zl + zh
            inverse = jnp.where(inside, OMEGA / jnp.where(inside, total, 1.0), 0.0)
            level[3][s] = inverse
            level[4][s] = jnp.where(inside, (1.0 / OMEGA) * total, 0.0)
            ends = (
                (lane < across) & (s == 0), (lane >= nz - across) & (s == many - 1), row == 0, row >= ny - 1,
                lane % span < step, lane % span >= span - step,
            )
            for ref, value, end in zip(level[5:], (xl, xh, yl, yh, zl, zh), ends):
                ref[s] = jnp.where(end, 0.0, value * inverse)

        each_group(many, finish)

    apart = next(
        (l for l in range(3, LEVELS + 1) if counts[l - 1][0] <= PACK and counts[l - 1][1] == EDGE), LEVELS + 1
    )

    def cells(l):
        return [(x, z) for x in range(counts[l][0]) for z in range(nz >> l)]

    def first_lane(l, x, z):
        return x * lane_step(l) + z * 2 ** (l - 2)

    def lane_of(value, lane):
        return lanes_at(value, jnp.full(value.shape, lane, jnp.int32))

    def set_apart(l):
        for k, ref in enumerate(level_refs[l][3:]):
            value = ref[0]
            for repeat in range((EDGE // counts[l][1]).bit_length() - 1):
                stretch(value, k)
                value = temp[k, pl.ds(0, EDGE), :]
            for i, (x, z) in enumerate(cells(l)):
                apart_refs[l][k, i] = lane_of(value, first_lane(l, x, z))

    for l in range(apart, LEVELS + 1):
        set_apart(l)

    window_wait(source_copy, 2, REACH, True)
    for t in range(2 * REACH + 1):
        for k, part in enumerate((even_part, odd_part)):
            i = 2 * t + k
            if abs(t - REACH) > 1:
                f1[i] = part(w1[t], 1)
                f1[i, pl.ds(EDGE, by), :] = part(wh[t].astype(jnp.float32), 1)
            else:
                for start in (0, EDGE + by):
                    f1[i, pl.ds(start, EDGE), :] = part(w1[t, pl.ds(start, EDGE), :], 1)
    for i in range(1, planes1 - 1):
        ua[i + 1] = inv1[i] * f1[i]
    sweep(level1, ua, ub, 2, 2, planes1 - 2)

    window_done(phase_copy, 0, REACH)
    window_done(f_copy, 0, 2)
    window_done(source_copy, 2, REACH, True)
    column_all().wait_send()
    for k in range(1, ngy):
        row_copy(k, 1).wait_send()
    @pl.when(gx == ngx - 1)
    def _():
        every = g2.at[pl.ds(0, n - 1)]
        pltpu.make_async_remote_copy(
            src_ref=every, dst_ref=every, send_sem=st.at[0], recv_sem=rt.at[0],
            device_id=(gx, (gy + 1) % ngy), device_id_type=MESH,
        ).wait_send()

    gather_all(g2, 1).wait_recv()

    f2 = level2[2]

    def unpack(t):
        place = index_along((half, nz), 1) // span
        for j in range(ngy):
            packs = [g2[(q * groups(2) + t) * ngy + j] for q in range(PACK)]
            moved = [roll(pack, span, 1) for pack in packs]
            for a in range(2):
                out = packs[a]
                for q in range(PACK):
                    out = jnp.where(place == q, packs[q] if q % 2 == a else moved[q], out)
                f2[t, pl.ds(j * cy + a * half, half), :] = out

    each_group(groups(2), unpack)

    def beside(l, v, s):
        many, across = groups(l), lane_step(l)
        low, high = v[(s + many - 1) % many], v[(s + 1) % many]
        if isinstance(s, int):
            low = roll(low, across, 1) if s == 0 else low
            high = roll(high, -across, 1) if s == many - 1 else high
        else:
            low = jnp.where(s == 0, roll(low, across, 1), low)
            high = jnp.where(s == many - 1, roll(high, -across, 1), high)
        return low, high

    def around(l, v, s):
        step = 2 ** (l - 2)
        faces = level_refs[l][5:]
        here = v[s]
        parts = [
            faces[4][s] * roll(here, step, 1) + faces[5][s] * roll(here, -step, 1),
            faces[2][s] * roll(here, 1, 0) + faces[3][s] * roll(here, -1, 0),
        ]
        if counts[l][0] == 2:
            parts.append((faces[0][s] + faces[1][s]) * roll(here, lane_step(l), 1))
        elif counts[l][0] > 1:
            low, high = beside(l, v, s)
            parts.append(faces[0][s] * low + faces[1][s] * high)
        return parts

    def made(l, ref, value):
        many = groups(l)
        if many <= GROUPS:
            return [value(s) for s in range(many)]
        each_group(many, lambda s: store(ref, s, value(s)))
        return ref

    def smooth(l, constant, v, ref):
        def value(s):
            parts = around(l, v, s)
            total = (1.0 - OMEGA) * v[s] + constant[s]
            return sum(parts[1:], parts[0]) + total

        return made(l, ref, value)

    def pair_copies(value, copies):
        even = index_along(value.shape, 0) // copies % 2 == 0
        return value + jnp.where(even, roll(value, -copies, 0), roll(value, copies, 0))

    def cycle_apart(l, f):
        copies = EDGE // counts[l][1]
        every = cells(l)
        weights = {c: [apart_refs[l][k, i] for k in range(8)] for i, c in enumerate(every)}
        constant = {c: weights[c][0] * f[c] for c in every}

        def smooth_apart(v):
            out = {}
            for x, z in every:
                here = v[x, z]
                (xl, xh, yl, yh, zl, zh) = weights[x, z][2:]
                out[x, z] = (yl * roll(here, copies, 0) + yh * roll(here, -copies, 0)) + (
                    (1.0 - OMEGA) * here + constant[x, z]
                )
                beside_x = [w * v[x + d, z] for w, d in ((xl, -1), (xh, 1)) if (x + d, z) in v]
                beside_z = [w * v[x, z + d] for w, d in ((zl, -1), (zh, 1)) if (x, z + d) in v]
                rest = beside_x + beside_z
                if rest:
                    out[x, z] = out[x, z] + sum(rest[1:], rest[0])
            return out

        v = constant
        for repeat in range((COARSE_SWEEPS if l == LEVELS else NU) - 1):
            v = smooth_apart(v)
        if l == LEVELS:
            return v
        later = smooth_apart(v)
        rest = {c: weights[c][1] * (later[c] - v[c]) for c in every}
        source = {}
        for x, z in cells(l + 1):
            total = sum(rest[2 * x + a, 2 * z + b] for a in range(2) for b in range(2))
            source[x, z] = 0.5 * pair_copies(total, copies)
        e = cycle_apart(l + 1, source)
        v = {(x, z): v[x, z] + e[x // 2, z // 2] for x, z in every}
        for repeat in range(NU):
            v = smooth_apart(v)
        return v

    def from_apart(l, rest):
        copies = EDGE // counts[l - 1][1]
        paired = pair_copies(rest, copies)
        source = {}
        for x, z in cells(l):
            lanes = [first_lane(l - 1, 2 * x + a, 2 * z + b) for a in range(2) for b in range(2)]
            parts = [lane_of(paired, lane) for lane in lanes]
            source[x, z] = 0.5 * ((parts[0] + parts[1]) + (parts[2] + parts[3]))
        e = cycle_apart(l, source)
        lane = index_along(rest.shape, 1)
        out = None
        for x in range(counts[l][0]):
            plane = e[x, 0]
            for z in range(1, nz >> l):
                plane = jnp.where(lane % span >= z * 2 ** (l - 2), e[x, z], plane)
            out = plane if out is None else jnp.where(lane >= x * lane_step(l), plane, out)
        return out

    def cycle(l):
        nx, ny = counts[l]
        (xa, xb, f, inverse, centre) = level_refs[l][:5]
        many, across = groups(l), lane_step(l)
        constant = made(l, f, lambda s: inverse[s] * f[s])
        x, free, other = constant, xa, xb
        for repeat in range((COARSE_SWEEPS if l == LEVELS else NU) - 1):
            x = smooth(l, constant, x, free)
            free, other = other, free
        if l == LEVELS:
            return x
        later = smooth(l, constant, x, free)

        def rest(s):
            return centre[s] * (later[s] - x[s])

        if l + 1 == apart:
            x = [x[0] + from_apart(l + 1, rest(0))]
            for repeat in range(NU):
                x = smooth(l, constant, x, free)
            return x
        f_next = level_refs[l + 1][2]
        size = max(ny // 2, 4)
        if ny // 2 < EDGE:
            f_next[...] = jnp.zeros(f_next.shape, f_next.dtype)

        def restrict(s):
            r = rest(2 * s) + rest(2 * s + 1) if many > 1 else pair_lanes(rest(0), across)
            f_next[s, pl.ds(0, size), :] = 0.5 * pair_lanes(pair_rows(r, s % slots), 2 ** (l - 2))

        each_group(groups(l + 1), restrict)
        fine = cycle(l + 1)
        rows = xa.shape[1]

        def correction(s):
            slot = s % slots
            stretch(fine[s], slot)
            return temp[slot, pl.ds(0, rows), :]

        if many <= GROUPS:
            added = [correction(s) for s in range(groups(l + 1))]
            x = [x[s] + added[s // 2 if many > 1 else 0] for s in range(many)]
        else:
            def correct(s):
                e = correction(s)
                for k in (2 * s, 2 * s + 1):
                    free[k] = x[k] + e

            each_group(groups(l + 1), correct)
            x, free, other = free, other, free
        for repeat in range(NU):
            x = smooth(l, constant, x, free)
            free, other = other, free
        return x

    found = cycle(2)
    found_ref = level_refs[2][0]
    for k in range(groups(2)):
        found_ref[k] = found[k]
    found = found_ref

    row2 = pl.multiple_of(gy * cy, 8)
    below2 = pl.multiple_of(jnp.maximum(gy * cy - EDGE, 0), 8)
    above2 = pl.multiple_of(jnp.minimum(gy * cy + cy, ny2 - EDGE), 8)
    for t in range(1, 2 * REACH):
        x = gx + t - REACH
        there = (x >= 0) & (x < nx2)
        plane = jnp.clip(x, 0, nx2 - 1)
        first, group = plane // groups(2) * span, plane % groups(2)
        ends = (gy > 0, True, gy < ngy - 1)
        for row, start, count, end in zip((below2, row2, above2), (0, EDGE, EDGE + cy), (EDGE, cy, EDGE), ends):
            part = found[group, pl.ds(row, count), :]
            part = lanes_at(part, first + index_along(part.shape, 1) // PACK)
            e2[t, pl.ds(start, count), :] = jnp.where(there & end, part, 0.0)

    for t in range(1, 2 * REACH):
        slot = t % slots
        stretch(e2[t], slot)
        e = temp[slot, pl.ds(EDGE, by + 2 * EDGE), :]
        ua[2 * t + 1] = ub[2 * t + 1] + e
        ua[2 * t + 2] = ub[2 * t + 2] + e
    sweep(level1, ua, ub, 2, 3, planes1 - 3)
    sweep(level1, ub, ua, 2, 4, planes1 - 4)

    for j in range(1, blocks - 1):
        slot = j % slots
        stretch(ua[first_block + j + 1], slot)
        e = temp[slot, pl.ds(EDGE, rows0), :]
        va[2 * j + 1] = vb[2 * j + 1] + e
        va[2 * j + 2] = vb[2 * j + 2] + e
    sweep(level0, va, vb, 1, HALO - 2, HALO + lx + 2)
    sweep(level0, vb, va, 1, HALO - 1, HALO + lx + 1)
    for i in range(lx):
        k = HALO + i
        product = c0[k] * va[k + 1]
        near_sum = neighbours(level0, va, k, 1)
        own = slice(EDGE, EDGE + ly)
        scaled_ref[i] = product[own]
        rest_ref[i] = w0[k, pl.ds(EDGE, ly), :] - product[own] + near_sum[own]

    gather_all(g2, 1).wait_send()


def write(scaled_ref, rest_ref, scaled_out, rest_out, sems):
    copies = [
        pltpu.make_async_copy(source, target, sems.at[k])
        for k, (source, target) in enumerate(((scaled_ref, scaled_out), (rest_ref, rest_out)))
    ]
    for copy in copies:
        copy.start()
    for copy in copies:
        copy.wait()


def solution(mesh):
    ngx, ngy = mesh.shape["gx"], mesh.shape["gy"]
    n = ngx * ngy

    def on_device(right_side, phase):
        lx, ly, nz = right_side.shape
        assert lx == 4 and ly % 32 == 0 and NU == 2
        by, cy = ly // 2, ly // 4
        counts = [(lx * ngx >> l, ly * ngy >> l) for l in range(LEVELS + 1)]
        blocks = 2 * REACH + 1

        def level_scratch(planes, rows, padded_source=False):
            shapes = [planes + 2, planes + 2, planes, planes, planes, planes + 1] + [planes] * 4
            if padded_source:
                shapes[2] = 1
            large = planes * rows * nz * 4 >= LARGE
            types = [jnp.float32] * 5 + [jnp.bfloat16 if large else jnp.float32] * 5
            return [pltpu.VMEM((k, rows, nz), dtype) for k, dtype in zip(shapes, types)]

        def packed_scratch(many, rows):
            return [pltpu.VMEM((many, rows, nz), jnp.float32)] * 11

        assert counts[2][0] % PACK == 0 and nz >> 2 == nz // PACK
        scratch = [
            pltpu.VMEM((lx + 2 * HALO, ly + 2 * EDGE, nz), jnp.float32),
            pltpu.VMEM((2 * HALO, ly, nz), jnp.bfloat16),
            pltpu.VMEM((2, HALO, 2 * EDGE, nz), jnp.bfloat16),
            pltpu.VMEM((blocks, by + 2 * EDGE_PHASE, nz), jnp.bfloat16),
            pltpu.VMEM((blocks, by + 2 * EDGE, nz), jnp.float32),
            pltpu.VMEM((blocks, by, nz), jnp.bfloat16),
            pltpu.VMEM((ngy, ngx, cy, nz), jnp.bfloat16),
            pltpu.VMEM((ngy, 1, cy, nz), jnp.bfloat16),
            pltpu.VMEM((n, cy // 2, nz), jnp.float32),
            pltpu.VMEM((lx, ly, nz), jnp.int32),
            pltpu.VMEM((1, by, nz), jnp.bfloat16),
            pltpu.VMEM((lx, ly, nz), jnp.bfloat16),
            pltpu.VMEM((2, lx // 2, 2 * EDGE, nz), jnp.bfloat16),
            pltpu.VMEM((1, by, nz), jnp.float32),
            pltpu.VMEM((1, by, nz), jnp.bfloat16),
            pltpu.VMEM((1, cy, nz), jnp.bfloat16),
            pltpu.VMEM((1, cy, nz), jnp.bfloat16),
            pltpu.VMEM((1, cy // 2, nz), jnp.float32),
            pltpu.VMEM((8, max(2 * (by + 2 * EDGE), 2 * counts[2][1], 2 * (cy + 2 * EDGE)), nz), jnp.float32),
            pltpu.VMEM((2 * blocks, by + 2 * EDGE, nz), jnp.float32),
            pltpu.VMEM((blocks, cy + 2 * EDGE, nz), jnp.float32),
        ]
        scratch += level_scratch(lx + 2 * HALO, ly + 2 * EDGE, True)
        scratch += level_scratch(2 * blocks, by + 2 * EDGE)
        for l in range(2, LEVELS + 1):
            scratch += packed_scratch(max(counts[l][0] // PACK, 1), max(counts[l][1], EDGE))
        for l in range(LEVELS + 1):
            small = counts[l][1] < EDGE
            scratch += [pltpu.VMEM((8, counts[l][0] * (nz >> l) if small else 1, EDGE, nz), jnp.float32)]
        scratch += [pltpu.SemaphoreType.DMA((15,))] * 2
        scratch += [pltpu.SemaphoreType.DMA((3 * blocks,))] * 4
        scratch += [pltpu.SemaphoreType.DMA((2,))] * 2
        scratch += [pltpu.SemaphoreType.DMA((1,)), pltpu.SemaphoreType.DMA((ngy,))]
        scratch += [pltpu.SemaphoreType.DMA((ngy,)), pltpu.SemaphoreType.DMA((ngy,)), pltpu.SemaphoreType.DMA((2,))]
        scratch += [pltpu.SemaphoreType.REGULAR]
        anywhere = pl.BlockSpec(memory_space=pl.ANY)
        inside = pl.BlockSpec(memory_space=pltpu.VMEM)
        right_side, phase = [pltpu.with_memory_space_constraint(x, pltpu.HBM) for x in (right_side, phase)]
        found = pl.pallas_call(
            functools.partial(kernel, ngx, ngy, counts),
            out_shape=[pltpu.VMEM(right_side.shape, jnp.float32)] * 2,
            in_specs=[anywhere] * 2,
            out_specs=[inside] * 2,
            scratch_shapes=scratch,
            compiler_params=pltpu.CompilerParams(
                collective_id=0, has_side_effects=True, vmem_limit_bytes=64_000_000
            ),
        )(right_side, phase)
        return pl.pallas_call(
            write,
            out_shape=[jax.ShapeDtypeStruct(right_side.shape, jnp.float32)] * 2,
            in_specs=[inside] * 2,
            out_specs=[anywhere] * 2,
            scratch_shapes=[pltpu.SemaphoreType.DMA((2,))],
        )(*[pltpu.with_memory_space_constraint(x, pltpu.VMEM) for x in found])

    placed = P("gx", "gy", None)
    return jax.shard_map(
        on_device, mesh=mesh, in_specs=(placed, placed), out_specs=(placed, placed), check_vma=False
    )
```

```python
import functools

import jax
import jax.numpy as jnp
import numpy as np
from jax import lax
from jax.experimental import pallas as pl
from jax.experimental.pallas import tpu as pltpu
from jax.sharding import PartitionSpec as P

LEVELS = 6
NU = 2
COARSE_SWEEPS = 6
OMEGA = 0.8
LIQUID, GAS = 1.0, 1000.0
MIXED = float(np.asarray(2.0 * LIQUID * GAS / (LIQUID + GAS), jnp.bfloat16))
MESH = pl.DeviceIdType.MESH
REACH = 3
HALO = 6
PACK = 4
GROUPS = 4
EDGE = 8
EDGE_PHASE = 16
UNROLL = 16
LARGE = 1 << 20


def each(count, body):
    if count <= UNROLL:
        for i in range(count):
            body(i)
    else:
        lax.fori_loop(0, count, lambda i, carry: (body(i), carry)[1], 0)


def each_group(count, body):
    if count <= GROUPS:
        for i in range(count):
            body(i)
    else:
        lax.fori_loop(0, count, lambda i, carry: (body(i), carry)[1], 0)


def index_along(shape, axis):
    return lax.broadcasted_iota(jnp.int32, shape, axis)


def roll(x, shift, axis):
    return pltpu.roll(x, shift % x.shape[axis], axis)


def lane_bit(x, step):
    return index_along(x.shape, x.ndim - 1) // step % 2


def even_part(x, step):
    return jnp.where(lane_bit(x, step) == 0, x, roll(x, step, x.ndim - 1))


def odd_part(x, step):
    return jnp.where(lane_bit(x, step) == 1, x, roll(x, -step, x.ndim - 1))


def lanes_at(x, index):
    return jnp.take_along_axis(x, index, axis=1, mode="promise_in_bounds")


def pair_lanes(x, step):
    axis = x.ndim - 1
    return x + jnp.where(lane_bit(x, step) == 0, roll(x, -step, axis), roll(x, step, axis))


def harmonic(a, b):
    low, high = jnp.minimum(a, b), jnp.maximum(a, b)
    return jnp.where((low == 0.0) | (low == high), high, MIXED)


def store(ref, i, value):
    ref[i] = value.astype(ref.dtype)


def wide(ref, i):
    return ref[i].astype(jnp.float32)


def quarter(x):
    return (0.25 * x).astype(jnp.bfloat16).astype(jnp.float32)


def kernel(ngx, ngy, counts, f_hbm, phase_hbm, scaled_ref, rest_ref, *refs):
    gx, gy = lax.axis_index("gx"), lax.axis_index("gy")
    n = ngx * ngy
    me = gx * ngy + gy
    lx, ly, nz = f_hbm.shape
    by, cy = ly // 2, ly // 4
    refs = list(refs)

    def take(count):
        out = refs[:count]
        del refs[:count]
        return out

    (w0, wn, wc, wp, w1, wh, gf, gt, g2) = take(9)
    (phase_ref, p_pack, f_pack, c_pack, g1_pack, h_pack, f2_pack, t_pack, g2_pack, temp) = take(10)
    (b1, e2) = take(2)
    level_refs = [take(10 if l < 2 else 11) for l in range(LEVELS + 1)]
    apart_refs = [take(1)[0] for l in range(LEVELS + 1)]
    (s0, r0, s1, r1, sp, rp, sg, rg, st, rt, sr, rr, si, all_in) = take(14)

    own_f = w0.at[pl.ds(HALO, lx), pl.ds(EDGE, ly), :]
    load_phase = pltpu.make_async_copy(phase_hbm, phase_ref, si.at[0])
    load_f = pltpu.make_async_copy(f_hbm, own_f, si.at[1])
    load_phase.start()
    load_f.start()

    for start in (0, EDGE + ly):
        w0[:, pl.ds(start, EDGE), :] = jnp.zeros((w0.shape[0], EDGE, nz), w0.dtype)
    for ref in (wn, wc, wp, w1, wh):
        ref[...] = jnp.zeros(ref.shape, ref.dtype)

    barrier = pltpu.get_barrier_semaphore()

    m = max(k for k in range(1, ngx + 1) if ngx % k == 0 and k * k <= ngx)
    greeted = 0

    def greet(x, y, there):
        pl.when(there)(
            lambda: pl.semaphore_signal(barrier, inc=1, device_id=(x, y), device_id_type=MESH)
        )
        return greeted + jnp.where(there, 1, 0)

    mates = [(c * m + gx % m, gy, gx // m != c) for c in range(ngx // m)]
    for d in sorted(range(-REACH, REACH + 1), key=abs):
        for e in (0, 1, -1):
            if (d, e) != (0, 0):
                x, y = gx + d, gy + e
                greeted = greet(x, y, (x >= 0) & (x < ngx) & (y >= 0) & (y < ngy))
    for x, y, there in mates:
        greeted = greet(x, y, there & (jnp.abs(x - gx) > REACH))
    for a in range(m):
        for y in range(ngy):
            x = gx // m * m + a
            column = (x == gx) & (y == gy)
            if m - 1 > REACH or ngy > 2:
                greeted = greet(x, y, ((jnp.abs(x - gx) > REACH) | (jnp.abs(y - gy) > 1)) & ~column)

    for l in range(2):
        for v in level_refs[l][:2]:
            zero = jnp.zeros(v.shape[1:], v.dtype)
            v[0] = zero
            v[v.shape[0] - 1] = zero

    load_phase.wait()
    for plane in range(0, lx, 4):
        beta = [
            jnp.where(phase_ref[plane + 2 * k, pl.ds(0, by, 2), :] == 1, GAS, LIQUID) for k in range(2)
        ]
        p_pack[0] = jnp.where(lane_bit(beta[0], 1) == 0, beta[0], beta[1]).astype(jnp.bfloat16)
    load_f.wait()
    f_pack[...] = own_f[...].astype(jnp.bfloat16)
    for side, start in enumerate((EDGE, ly)):
        for k in range(lx // 2):
            rows = [w0[HALO + 2 * k + i, pl.ds(start, EDGE), :] for i in range(2)]
            c_pack[side, k] = jnp.concatenate(rows, axis=0).astype(c_pack.dtype)

    pl.semaphore_wait(barrier, greeted)

    def window_copy(src, dst, send, recv, reach, edge, d, e, to):
        lead, rows = src.shape[0], src.shape[1]
        count = rows if e == 0 else edge
        source = src.at[:, pl.ds(rows - edge if e == 1 else 0, count), :]
        start = {0: edge, 1: 0, -1: edge + rows}[e]
        target = dst.at[pl.ds((reach - d) * lead, lead), pl.ds(start, count), :]
        k = (d + reach) * 3 + e + 1
        return pltpu.make_async_remote_copy(
            src_ref=source, dst_ref=target, send_sem=send.at[k], recv_sem=recv.at[k],
            device_id=(gx + to * d, gy + to * e), device_id_type=MESH,
        )

    def source_copy(d, e, to):
        if e == 0 and abs(d) > 1:
            source, target = h_pack, wh.at[pl.ds(REACH - d, 1)]
        else:
            return window_copy(g1_pack, w1, s1, r1, REACH, EDGE, d, e, to)
        k = (d + REACH) * 3 + e + 1
        return pltpu.make_async_remote_copy(
            src_ref=source, dst_ref=target, send_sem=s1.at[k], recv_sem=r1.at[k],
            device_id=(gx + to * d, gy + to * e), device_id_type=MESH,
        )

    def phase_copy(d, e, to):
        return window_copy(p_pack, wp, sp, rp, REACH, EDGE_PHASE, d, e, to)

    def f_copy(d, e, to):
        first, count = {0: (0, lx), 1: (0, lx), -1: (0, lx), 2: (lx - 2, 2), -2: (0, 2)}[d]
        low = {0: 0, 1: HALO - lx, 2: 0, -1: HALO, -2: HALO + lx}[d]
        side = 0 if e == 1 else 1
        if d == 0:
            source = own_f.at[:, pl.ds(ly - EDGE if e == 1 else 0, EDGE), :]
            target = w0.at[pl.ds(HALO, lx), pl.ds(0 if e == 1 else EDGE + ly, EDGE), :]
        elif e == 0:
            source, target = f_pack.at[pl.ds(first, count)], wn.at[pl.ds(low, count)]
        else:
            source = c_pack.at[1 - side, pl.ds(first // 2, count // 2)]
            target = wc.at[side, pl.ds(low // 2, count // 2)]
        k = (d + 2) * 3 + e + 1
        return pltpu.make_async_remote_copy(
            src_ref=source, dst_ref=target, send_sem=s0.at[k], recv_sem=r0.at[k],
            device_id=(gx + to * d, gy + to * e), device_id_type=MESH,
        )

    def each_near(low, high, body, near=None, to=1):
        for d in sorted(range(-high, high + 1), key=abs):
            for e in (0, 1, -1):
                if (d, e) != (0, 0) and (abs(d) >= low or (near is not None and e != 0)):
                    x, y = gx + to * d, gy + to * e
                    pl.when((x >= 0) & (x < ngx) & (y >= 0) & (y < ngy))(functools.partial(body, d, e))

    def window_send(copy, low, high, near=None):
        each_near(low, high, lambda d, e: copy(d, e, 1).start(), near)

    def window_wait(copy, low, high, near=None):
        each_near(low, high, lambda d, e: copy(d, e, -1).wait_recv(), near, -1)

    def window_done(copy, low, high, near=None):
        each_near(low, high, lambda d, e: copy(d, e, 1).wait_send(), near)

    def gather_send(src, dst, k):
        def body(t, carry):
            other = jnp.where(t <= me, t - 1, t)
            pltpu.make_async_remote_copy(
                src_ref=src, dst_ref=dst.at[pl.ds(me, 1)], send_sem=sg.at[k], recv_sem=rg.at[k],
                device_id=(other // ngy, other % ngy), device_id_type=MESH,
            ).start()
            return carry

        lax.fori_loop(1, n, body, 0)

    def gather_all(dst, k):
        every = dst.at[pl.ds(0, n - 1)]
        return pltpu.make_async_remote_copy(
            src_ref=every, dst_ref=every, send_sem=sg.at[k], recv_sem=rg.at[k],
            device_id=(gx, (gy + 1) % ngy), device_id_type=MESH,
        )

    def top_copy(j, other):
        return pltpu.make_async_remote_copy(
            src_ref=t_pack, dst_ref=gt.at[j], send_sem=st.at[0], recv_sem=rt.at[j],
            device_id=(other // ngy, other % ngy), device_id_type=MESH,
        )

    window_send(phase_copy, 0, 2)
    for x, y, there in mates:
        pl.when(there)(functools.partial(pl.semaphore_signal, all_in, inc=1, device_id=(x, y), device_id_type=MESH))
    window_send(f_copy, 0, 2)
    wp[REACH, pl.ds(EDGE_PHASE, by), :] = p_pack[0]

    slots = temp.shape[0]

    def stretch(value, slot):
        rows = value.shape[0]
        temp[slot, pl.ds(0, rows, 2), :] = value
        temp[slot, pl.ds(1, rows, 2), :] = value

    def pair_rows(value, slot, first=True, second=True):
        rows = value.shape[0]
        temp[slot, pl.ds(0, rows), :] = value
        out = 0.0
        if first:
            out = out + temp[slot, pl.ds(0, rows // 2, 2), :]
        if second:
            out = out + temp[slot, pl.ds(1, rows // 2, 2), :]
        return out

    def neighbours(level, v_ref, i, step):
        (_, _, _, _, _, fx, fyl, fyh, fzl, fzh) = level
        v = v_ref[i + 1]
        return (
            wide(fx, i) * v_ref[i] + wide(fx, i + 1) * v_ref[i + 2]
            + wide(fyl, i) * roll(v, 1, 0) + wide(fyh, i) * roll(v, -1, 0)
            + wide(fzl, i) * roll(v, step, 1) + wide(fzh, i) * roll(v, -step, 1)
        )

    def sweep(level, source, target, step, first, last):
        f, inverse = level[2], level[3]

        def body(k):
            i = k + first
            target[i + 1] = (1.0 - OMEGA) * source[i + 1] + inverse[i] * (f[i] + neighbours(level, source, i, step))

        each(last - first, body)

    def rest_of(level, v_ref, i, step):
        return level[2][i] - level[4][i] * v_ref[i + 1] + neighbours(level, v_ref, i, step)

    def put_faces(level, i, inside, lows, step, edges):
        (_, _, _, inverse, centre, fx, fyl, fyh, fzl, fzh) = level
        (yl, yh, zl, zh) = lows
        total = wide(fx, i) + wide(fx, i + 1) + yl + yh + zl + zh
        inverse[i] = jnp.where(inside, OMEGA / jnp.where(inside, total, 1.0), 0.0)
        centre[i] = total
        lane = index_along(zl.shape, 1)
        fzl[i] = jnp.where(lane < step, 0.0, zl).astype(fzl.dtype)
        fzh[i] = jnp.where(lane >= nz - step, 0.0, zh).astype(fzh.dtype)
        if edges is not None:
            row = index_along(yl.shape, 0)
            yl = jnp.where(row == 0, 0.0, yl)
            yh = jnp.where(row >= edges - 1, 0.0, yh)
        fyl[i] = yl.astype(fyl.dtype)
        fyh[i] = yh.astype(fyh.dtype)

    def cell_faces(b, step):
        lane = index_along(b.shape, 1)
        yl, yh = harmonic(roll(b, 1, 0), b), harmonic(b, roll(b, -1, 0))
        zl = harmonic(jnp.where(lane < step, 0.0, roll(b, step, 1)), b)
        zh = harmonic(b, jnp.where(lane >= nz - step, 0.0, roll(b, -step, 1)))
        return yl, yh, zl, zh

    def phase_block(t):
        packed = wp[t].astype(jnp.float32)[EDGE_PHASE - EDGE : EDGE_PHASE + by + EDGE]
        b1[2 * t] = even_part(packed, 1)
        b1[2 * t + 1] = odd_part(packed, 1)

    window_wait(phase_copy, 0, 1)
    for t in range(REACH - 1, REACH + 2):
        phase_block(t)

    own1 = 2 * REACH
    level1 = level_refs[1]
    (ua, ub, f1, inv1, c1, fx1) = level1[:6]
    planes1 = 2 * (2 * REACH + 1)
    near = range(own1 - 2, own1 + 4)

    def own_faces():
        own = slice(EDGE, EDGE + by)
        below, low, high, above = [b1[own1 + k] for k in range(-1, 3)]
        lane = index_along((by, nz), 1)
        pair = [low, high]
        mine = [b[own] for b in pair]
        x_low = quarter(pair_lanes(pair_rows(harmonic(below, low)[own], 0), 2))
        x_high = quarter(pair_lanes(pair_rows(harmonic(high, above)[own], 1), 2))
        y_low = sum(harmonic(roll(b, 1, 0), b)[own] for b in pair)
        y_high = sum(harmonic(b, roll(b, -1, 0))[own] for b in pair)
        z_low = sum(harmonic(jnp.where(lane < 2, 0.0, roll(b, 2, 1)), b) for b in mine)
        z_high = sum(harmonic(b, jnp.where(lane >= nz - 2, 0.0, roll(b, -2, 1))) for b in mine)
        y_low = quarter(pair_lanes(pair_rows(y_low, 2, second=False), 2))
        y_high = quarter(pair_lanes(pair_rows(y_high, 3, first=False), 2))
        z_low = quarter(even_part(pair_rows(z_low, 4), 2))
        z_high = quarter(odd_part(pair_rows(z_high, 5), 2))
        row, lane = index_along((cy, nz), 0), index_along((cy, nz), 1)
        corner = (row == cy - 2) & (lane // 4 == nz // 4 - 2)
        edge = jnp.where(corner, roll(roll(z_high, -1, 0), -4, 1), z_high)
        edge = jnp.where(row == cy - 1, y_high, edge)
        mixed = edge
        for k, value in enumerate((x_low, y_low, z_low)):
            mixed = jnp.where(lane % 4 == k, value, mixed)
        f2_pack[0] = mixed.astype(f2_pack.dtype)
        t_pack[0] = x_high.astype(t_pack.dtype)

    own_faces()
    pl.semaphore_wait(all_in, ngx // m - 1)
    def column_copy(t):
        other = jnp.where(t <= gx, t - 1, t)
        return pltpu.make_async_remote_copy(
            src_ref=f2_pack, dst_ref=gf.at[gy, pl.ds(gx, 1)], send_sem=sg.at[0], recv_sem=rg.at[0],
            device_id=(other, gy), device_id_type=MESH,
        )

    lax.fori_loop(1, ngx, lambda t, carry: (column_copy(t).start(), carry)[1], 0)
    gf[gy, gx] = f2_pack[0]
    for j in range(ngy):
        @pl.when((gx == ngx - 1) & (gy == j))
        def _():
            def body(t, carry):
                top_copy(j, (me + t) % n).start()
                return carry

            lax.fori_loop(1, n, body, 0)
            gt[j, 0] = t_pack[0]
    window_wait(phase_copy, 2, 2)
    phase_block(REACH - 2)
    phase_block(REACH + 2)

    level0 = list(level_refs[0])
    level0[2] = w0
    (va, vb, f0, inv0, c0, fx0) = level0[:6]
    rows0 = ly + 2 * EDGE
    planes0 = lx + 2 * HALO
    blocks = planes0 // 2
    first_block = own1 - HALO // 2

    def fine_beta(j):
        slot = (j + 1) % slots
        stretch(b1[first_block + j], slot)
        return temp[slot, pl.ds(EDGE, rows0), :]

    def fine_faces(j):
        lows = cell_faces(beta0[j], 1)
        for i in (2 * j, 2 * j + 1):
            put_faces(level0, i, beta0[j] > 0.0, lows, 1, None)

    beta0 = [fine_beta(j) for j in range(-1, blocks + 1)]
    for j in range(blocks + 1):
        fx0[2 * j] = harmonic(beta0[j], beta0[j + 1])
        if j < blocks:
            fx0[2 * j + 1] = beta0[j + 1]
    beta0 = beta0[1:-1]
    for j in range(blocks):
        fine_faces(j)

    window_send(phase_copy, REACH, REACH)

    for i in range(near[0], near[-1] + 2):
        fx1[i] = harmonic(b1[i - 1], b1[i])
    for i in near:
        put_faces(level1, i, b1[i] > 0.0, cell_faces(b1[i], 2), 2, None)

    for i in near:
        f1[i] = jnp.zeros(f1.shape[1:], f1.dtype)

    def fill(planes):
        for plane in planes:
            i = plane if plane < HALO else plane - lx
            w0[plane, pl.ds(EDGE, ly), :] = wn[i].astype(w0.dtype)
            for side, start in enumerate((0, EDGE + ly)):
                rows = wc[side, i // 2, pl.ds(0, 2 * EDGE), :].astype(w0.dtype)
                w0[plane, pl.ds(start, EDGE), :] = rows[EDGE:] if i % 2 else rows[:EDGE]

    def start_fine(planes):
        for i in planes:
            va[i + 1] = inv0[i] * w0[i]

    def source_plane(k):
        plane = 2 * (near[0] + k - first_block)
        r = rest_of(level0, vb, plane, 1) + rest_of(level0, vb, plane + 1, 1)
        f1[near[0] + k, pl.ds(EDGE // 2, rows0 // 2), :] = 0.5 * pair_lanes(pair_rows(r, k % slots), 1)

    inner = range(HALO - lx, HALO + 2 * lx)
    outer = [i for i in range(planes0) if i not in inner]
    own = range(HALO, HALO + lx)
    window_wait(f_copy, 0, 0)
    start_fine(own)
    sweep(level0, va, vb, 1, own[0] + 1, own[-1])
    window_wait(f_copy, 1, 1)
    fill([i for i in inner if i not in own])
    start_fine([i for i in inner if i not in own])
    sweep(level0, va, vb, 1, inner[0] + 1, own[0] + 1)
    sweep(level0, va, vb, 1, own[-1], inner[-1])
    for k in range(1, len(near) - 1):
        source_plane(k)
    coarse = [f1[own1 + k, pl.ds(EDGE, by), :] for k in range(2)]
    packed = jnp.where(lane_bit(coarse[0], 1) == 0, coarse[0], coarse[1])
    g1_pack[0] = packed
    h_pack[0] = packed.astype(h_pack.dtype)

    window_wait(f_copy, 2, 2)
    fill(outer)
    start_fine(outer)
    sweep(level0, va, vb, 1, 1, inner[0] + 1)
    sweep(level0, va, vb, 1, inner[-1], planes0 - 1)
    source_plane(0)
    source_plane(len(near) - 1)
    for i in near:
        ua[i + 1] = inv1[i] * f1[i]
    sweep(level1, ua, ub, 2, near[0] + 1, near[-1])
    rests = [rest_of(level1, ub, own1 + i, 2)[EDGE : EDGE + by] for i in range(2)]
    paired = pair_rows(rests[0] + rests[1], 0)
    half = cy // 2
    lane = index_along(paired.shape, 1) % (nz // PACK) * PACK
    coarse = 0.5 * (lanes_at(paired, lane) + lanes_at(paired, lane + 2))
    packed = jnp.where(lane_bit(coarse[:half], nz // PACK) == 0, coarse[:half], coarse[half:])
    g2_pack[0] = packed
    gather_send(g2_pack, g2, 1)
    g2[me] = packed
    window_send(source_copy, 2, REACH, True)

    window_wait(phase_copy, REACH, REACH)
    phase_block(0)
    phase_block(2 * REACH)
    far = [i for i in range(1, planes1 - 1) if i not in near]
    for i in range(1, planes1):
        if not near[0] <= i <= near[-1] + 1:
            fx1[i] = harmonic(b1[i - 1], b1[i])
    for i in far:
        put_faces(level1, i, b1[i] > 0.0, cell_faces(b1[i], 2), 2, None)

    def column_all():
        every = gf.at[pl.ds(gy, 1), pl.ds(0, ngx - 1)]
        return pltpu.make_async_remote_copy(
            src_ref=every, dst_ref=every, send_sem=sg.at[0], recv_sem=rg.at[0],
            device_id=(gx, (gy + 1) % ngy), device_id_type=MESH,
        )

    def row_copy(k, to):
        part = gf.at[pl.ds(gy if to > 0 else (gy + ngy - k) % ngy, 1)]
        return pltpu.make_async_remote_copy(
            src_ref=part, dst_ref=part, send_sem=sr.at[k], recv_sem=rr.at[k],
            device_id=(gx, (gy + ngy + to * k) % ngy), device_id_type=MESH,
        )

    column_all().wait_recv()
    for k in range(1, ngy):
        row_copy(k, 1).start()
    for k in range(1, ngy):
        row_copy(k, -1).wait_recv()
    for j in range(ngy):
        @pl.when((gx < ngx - 1) | (gy != j))
        def _():
            top_copy(j, me).wait_recv()

    shape2 = counts[2]
    (nx2, ny2) = shape2
    level2 = level_refs[2]
    span = nz // PACK

    def groups(l):
        return max(counts[l][0] // PACK, 1)

    def lane_step(l):
        return nz // min(counts[l][0], PACK)

    row_p, lane_p = index_along((nz, PACK * nz), 0), index_along((nz, PACK * nz), 1)
    picks = []
    for q in range(PACK):
        chosen = (row_p == PACK * (lane_p % span) + lane_p // nz) & (lane_p % nz // span == q)
        picks.append(jnp.where(chosen, 1.0, 0.0).astype(jnp.bfloat16))

    def whole_plane(ref, k):
        return jnp.concatenate([ref[j, k].astype(jnp.float32) for j in range(ngy)], axis=0)

    def spread(x, columns):
        return jnp.dot(x.astype(jnp.bfloat16), columns, preferred_element_type=jnp.float32)

    many = groups(2)
    row2, lane2 = index_along((ny2, nz), 0), index_along((ny2, nz), 1)

    def faces2(t):
        parts = sum(spread(whole_plane(gf, q * many + t), picks[q]) for q in range(PACK))
        x_low, y_low, z_low, edge = [parts[:, k * nz : (k + 1) * nz] for k in range(4)]
        y_high = jnp.where(row2 == ny2 - 1, edge, roll(y_low, -1, 0))
        z_edge = jnp.where(row2 % cy == cy - 1, roll(roll(edge, 1, 0), 1, 1), edge)
        z_high = jnp.where(lane2 % span == span - 1, z_edge, roll(z_low, -1, 1))
        for ref, value in zip(level2[5:6] + level2[7:], (x_low, y_low, y_high, z_low, z_high)):
            store(ref, t, value)

    each_group(many, faces2)
    top = spread(whole_plane(gt, 0), picks[PACK - 1])[:, :nz]

    def faces2_high(t):
        after = wide(level2[5], (t + 1) % many)
        around = jnp.where(lane2 >= nz - span, top, roll(after, -span, 1))
        store(level2[6], t, jnp.where(t == many - 1, around, after))

    each_group(many, faces2_high)

    for l in range(2, LEVELS + 1):
        nx, ny = counts[l]
        step, across, many = 2 ** (l - 2), lane_step(l), groups(l)
        level = level_refs[l]
        if l < LEVELS:
            coarser = level_refs[l + 1]
            size = max(ny // 2, 4)
            if ny // 2 < EDGE:
                for ref in coarser[5:]:
                    ref[...] = jnp.zeros(ref.shape, ref.dtype)

            def put(ref, s, value):
                ref[s, pl.ds(0, size), :] = quarter(value).astype(ref.dtype)

            def coarsen(s):
                slot = 4 * (s % 2)
                if many > 1:
                    low = lambda ref: wide(ref, 2 * s)
                    high = lambda ref: wide(ref, 2 * s + 1)
                    both = lambda ref: low(ref) + high(ref)
                else:
                    low = lambda ref: even_part(wide(ref, 0), across)
                    high = lambda ref: odd_part(wide(ref, 0), across)
                    both = lambda ref: pair_lanes(wide(ref, 0), across)
                (xl, xh, yl, yh, zl, zh) = level[5:]
                put(coarser[5], s, pair_lanes(pair_rows(low(xl), slot), step))
                put(coarser[6], s, pair_lanes(pair_rows(high(xh), slot + 1), step))
                put(coarser[7], s, pair_lanes(pair_rows(both(yl), slot + 2, second=False), step))
                put(coarser[8], s, pair_lanes(pair_rows(both(yh), slot + 3, first=False), step))
                put(coarser[9], s, even_part(pair_rows(both(zl), slot), step))
                put(coarser[10], s, odd_part(pair_rows(both(zh), slot + 1), step))

            each_group(groups(l + 1), coarsen)

        def finish(s):
            (xl, xh, yl, yh, zl, zh) = [wide(ref, s) for ref in level[5:]]
            row, lane = index_along(xl.shape, 0), index_along(xl.shape, 1)
            inside = row < ny
            total = xl + xh + yl + yh + zl + zh
            inverse = jnp.where(inside, OMEGA / jnp.where(inside, total, 1.0), 0.0)
            level[3][s] = inverse
            level[4][s] = jnp.where(inside, (1.0 / OMEGA) * total, 0.0)
            ends = (
                (lane < across) & (s == 0), (lane >= nz - across) & (s == many - 1), row == 0, row >= ny - 1,
                lane % span < step, lane % span >= span - step,
            )
            for ref, value, end in zip(level[5:], (xl, xh, yl, yh, zl, zh), ends):
                ref[s] = jnp.where(end, 0.0, value * inverse)

        each_group(many, finish)

    apart = next(
        (l for l in range(3, LEVELS + 1) if counts[l - 1][0] <= PACK and counts[l - 1][1] == EDGE), LEVELS + 1
    )

    def cells(l):
        return [(x, z) for x in range(counts[l][0]) for z in range(nz >> l)]

    def first_lane(l, x, z):
        return x * lane_step(l) + z * 2 ** (l - 2)

    def lane_of(value, lane):
        return lanes_at(value, jnp.full(value.shape, lane, jnp.int32))

    def set_apart(l):
        for k, ref in enumerate(level_refs[l][3:]):
            value = ref[0]
            for repeat in range((EDGE // counts[l][1]).bit_length() - 1):
                stretch(value, k)
                value = temp[k, pl.ds(0, EDGE), :]
            for i, (x, z) in enumerate(cells(l)):
                apart_refs[l][k, i] = lane_of(value, first_lane(l, x, z))

    for l in range(apart, LEVELS + 1):
        set_apart(l)

    window_wait(source_copy, 2, REACH, True)
    for t in range(2 * REACH + 1):
        for k, part in enumerate((even_part, odd_part)):
            i = 2 * t + k
            if abs(t - REACH) > 1:
                f1[i] = part(w1[t], 1)
                f1[i, pl.ds(EDGE, by), :] = part(wh[t].astype(jnp.float32), 1)
            else:
                for start in (0, EDGE + by):
                    f1[i, pl.ds(start, EDGE), :] = part(w1[t, pl.ds(start, EDGE), :], 1)
    for i in range(1, planes1 - 1):
        ua[i + 1] = inv1[i] * f1[i]
    sweep(level1, ua, ub, 2, 2, planes1 - 2)

    window_done(phase_copy, 0, REACH)
    window_done(f_copy, 0, 2)
    window_done(source_copy, 2, REACH, True)
    column_all().wait_send()
    for k in range(1, ngy):
        row_copy(k, 1).wait_send()
    @pl.when(gx == ngx - 1)
    def _():
        every = g2.at[pl.ds(0, n - 1)]
        pltpu.make_async_remote_copy(
            src_ref=every, dst_ref=every, send_sem=st.at[0], recv_sem=rt.at[0],
            device_id=(gx, (gy + 1) % ngy), device_id_type=MESH,
        ).wait_send()

    gather_all(g2, 1).wait_recv()

    f2 = level2[2]

    def unpack(t):
        place = index_along((half, nz), 1) // span
        for j in range(ngy):
            packs = [g2[(q * groups(2) + t) * ngy + j] for q in range(PACK)]
            moved = [roll(pack, span, 1) for pack in packs]
            for a in range(2):
                out = packs[a]
                for q in range(PACK):
                    out = jnp.where(place == q, packs[q] if q % 2 == a else moved[q], out)
                f2[t, pl.ds(j * cy + a * half, half), :] = out

    each_group(groups(2), unpack)

    def beside(l, v, s):
        many, across = groups(l), lane_step(l)
        low, high = v[(s + many - 1) % many], v[(s + 1) % many]
        if isinstance(s, int):
            low = roll(low, across, 1) if s == 0 else low
            high = roll(high, -across, 1) if s == many - 1 else high
        else:
            low = jnp.where(s == 0, roll(low, across, 1), low)
            high = jnp.where(s == many - 1, roll(high, -across, 1), high)
        return low, high

    def around(l, v, s):
        step = 2 ** (l - 2)
        faces = level_refs[l][5:]
        here = v[s]
        parts = [
            faces[4][s] * roll(here, step, 1) + faces[5][s] * roll(here, -step, 1),
            faces[2][s] * roll(here, 1, 0) + faces[3][s] * roll(here, -1, 0),
        ]
        if counts[l][0] == 2:
            parts.append((faces[0][s] + faces[1][s]) * roll(here, lane_step(l), 1))
        elif counts[l][0] > 1:
            low, high = beside(l, v, s)
            parts.append(faces[0][s] * low + faces[1][s] * high)
        return parts

    def made(l, ref, value):
        many = groups(l)
        if many <= GROUPS:
            return [value(s) for s in range(many)]
        each_group(many, lambda s: store(ref, s, value(s)))
        return ref

    def smooth(l, constant, v, ref):
        def value(s):
            parts = around(l, v, s)
            total = (1.0 - OMEGA) * v[s] + constant[s]
            return sum(parts[1:], parts[0]) + total

        return made(l, ref, value)

    def pair_copies(value, copies):
        even = index_along(value.shape, 0) // copies % 2 == 0
        return value + jnp.where(even, roll(value, -copies, 0), roll(value, copies, 0))

    def cycle_apart(l, f):
        copies = EDGE // counts[l][1]
        every = cells(l)
        weights = {c: [apart_refs[l][k, i] for k in range(8)] for i, c in enumerate(every)}
        constant = {c: weights[c][0] * f[c] for c in every}

        def smooth_apart(v):
            out = {}
            for x, z in every:
                here = v[x, z]
                (xl, xh, yl, yh, zl, zh) = weights[x, z][2:]
                out[x, z] = (yl * roll(here, copies, 0) + yh * roll(here, -copies, 0)) + (
                    (1.0 - OMEGA) * here + constant[x, z]
                )
                beside_x = [w * v[x + d, z] for w, d in ((xl, -1), (xh, 1)) if (x + d, z) in v]
                beside_z = [w * v[x, z + d] for w, d in ((zl, -1), (zh, 1)) if (x, z + d) in v]
                rest = beside_x + beside_z
                if rest:
                    out[x, z] = out[x, z] + sum(rest[1:], rest[0])
            return out

        v = constant
        for repeat in range((COARSE_SWEEPS if l == LEVELS else NU) - 1):
            v = smooth_apart(v)
        if l == LEVELS:
            return v
        later = smooth_apart(v)
        rest = {c: weights[c][1] * (later[c] - v[c]) for c in every}
        source = {}
        for x, z in cells(l + 1):
            total = sum(rest[2 * x + a, 2 * z + b] for a in range(2) for b in range(2))
            source[x, z] = 0.5 * pair_copies(total, copies)
        e = cycle_apart(l + 1, source)
        v = {(x, z): v[x, z] + e[x // 2, z // 2] for x, z in every}
        for repeat in range(NU):
            v = smooth_apart(v)
        return v

    def from_apart(l, rest):
        copies = EDGE // counts[l - 1][1]
        paired = pair_copies(rest, copies)
        source = {}
        for x, z in cells(l):
            lanes = [first_lane(l - 1, 2 * x + a, 2 * z + b) for a in range(2) for b in range(2)]
            parts = [lane_of(paired, lane) for lane in lanes]
            source[x, z] = 0.5 * ((parts[0] + parts[1]) + (parts[2] + parts[3]))
        e = cycle_apart(l, source)
        lane = index_along(rest.shape, 1)
        out = None
        for x in range(counts[l][0]):
            plane = e[x, 0]
            for z in range(1, nz >> l):
                plane = jnp.where(lane % span >= z * 2 ** (l - 2), e[x, z], plane)
            out = plane if out is None else jnp.where(lane >= x * lane_step(l), plane, out)
        return out

    def cycle(l):
        nx, ny = counts[l]
        (xa, xb, f, inverse, centre) = level_refs[l][:5]
        many, across = groups(l), lane_step(l)
        constant = made(l, f, lambda s: inverse[s] * f[s])
        x, free, other = constant, xa, xb
        for repeat in range((COARSE_SWEEPS if l == LEVELS else NU) - 1):
            x = smooth(l, constant, x, free)
            free, other = other, free
        if l == LEVELS:
            return x
        later = smooth(l, constant, x, free)

        def rest(s):
            return centre[s] * (later[s] - x[s])

        if l + 1 == apart:
            x = [x[0] + from_apart(l + 1, rest(0))]
            for repeat in range(NU):
                x = smooth(l, constant, x, free)
            return x
        f_next = level_refs[l + 1][2]
        size = max(ny // 2, 4)
        if ny // 2 < EDGE:
            f_next[...] = jnp.zeros(f_next.shape, f_next.dtype)

        def restrict(s):
            r = rest(2 * s) + rest(2 * s + 1) if many > 1 else pair_lanes(rest(0), across)
            f_next[s, pl.ds(0, size), :] = 0.5 * pair_lanes(pair_rows(r, s % slots), 2 ** (l - 2))

        each_group(groups(l + 1), restrict)
        fine = cycle(l + 1)
        rows = xa.shape[1]

        def correction(s):
            slot = s % slots
            stretch(fine[s], slot)
            return temp[slot, pl.ds(0, rows), :]

        if many <= GROUPS:
            added = [correction(s) for s in range(groups(l + 1))]
            x = [x[s] + added[s // 2 if many > 1 else 0] for s in range(many)]
        else:
            def correct(s):
                e = correction(s)
                for k in (2 * s, 2 * s + 1):
                    free[k] = x[k] + e

            each_group(groups(l + 1), correct)
            x, free, other = free, other, free
        for repeat in range(NU):
            x = smooth(l, constant, x, free)
            free, other = other, free
        return x

    found = cycle(2)
    found_ref = level_refs[2][0]
    for k in range(groups(2)):
        found_ref[k] = found[k]
    found = found_ref

    row2 = pl.multiple_of(gy * cy, 8)
    below2 = pl.multiple_of(jnp.maximum(gy * cy - EDGE, 0), 8)
    above2 = pl.multiple_of(jnp.minimum(gy * cy + cy, ny2 - EDGE), 8)
    for t in range(1, 2 * REACH):
        x = gx + t - REACH
        there = (x >= 0) & (x < nx2)
        plane = jnp.clip(x, 0, nx2 - 1)
        first, group = plane // groups(2) * span, plane % groups(2)
        ends = (gy > 0, True, gy < ngy - 1)
        for row, start, count, end in zip((below2, row2, above2), (0, EDGE, EDGE + cy), (EDGE, cy, EDGE), ends):
            part = found[group, pl.ds(row, count), :]
            part = lanes_at(part, first + index_along(part.shape, 1) // PACK)
            e2[t, pl.ds(start, count), :] = jnp.where(there & end, part, 0.0)

    for t in range(1, 2 * REACH):
        slot = t % slots
        stretch(e2[t], slot)
        e = temp[slot, pl.ds(EDGE, by + 2 * EDGE), :]
        ua[2 * t + 1] = ub[2 * t + 1] + e
        ua[2 * t + 2] = ub[2 * t + 2] + e
    sweep(level1, ua, ub, 2, 3, planes1 - 3)
    sweep(level1, ub, ua, 2, 4, planes1 - 4)

    for j in range(1, blocks - 1):
        slot = j % slots
        stretch(ua[first_block + j + 1], slot)
        e = temp[slot, pl.ds(EDGE, rows0), :]
        va[2 * j + 1] = vb[2 * j + 1] + e
        va[2 * j + 2] = vb[2 * j + 2] + e
    sweep(level0, va, vb, 1, HALO - 2, HALO + lx + 2)
    sweep(level0, vb, va, 1, HALO - 1, HALO + lx + 1)
    for i in range(lx):
        k = HALO + i
        product = c0[k] * va[k + 1]
        near_sum = neighbours(level0, va, k, 1)
        own = slice(EDGE, EDGE + ly)
        scaled_ref[i] = product[own]
        rest_ref[i] = w0[k, pl.ds(EDGE, ly), :] - product[own] + near_sum[own]

    gather_all(g2, 1).wait_send()


def write(scaled_ref, rest_ref, scaled_out, rest_out, sems):
    copies = [
        pltpu.make_async_copy(source, target, sems.at[k])
        for k, (source, target) in enumerate(((scaled_ref, scaled_out), (rest_ref, rest_out)))
    ]
    for copy in copies:
        copy.start()
    for copy in copies:
        copy.wait()


def solution(mesh):
    ngx, ngy = mesh.shape["gx"], mesh.shape["gy"]
    n = ngx * ngy

    def on_device(right_side, phase):
        lx, ly, nz = right_side.shape
        assert lx == 4 and ly % 32 == 0 and NU == 2
        by, cy = ly // 2, ly // 4
        counts = [(lx * ngx >> l, ly * ngy >> l) for l in range(LEVELS + 1)]
        blocks = 2 * REACH + 1

        def level_scratch(planes, rows, padded_source=False):
            shapes = [planes + 2, planes + 2, planes, planes, planes, planes + 1] + [planes] * 4
            if padded_source:
                shapes[2] = 1
            large = planes * rows * nz * 4 >= LARGE
            types = [jnp.float32] * 5 + [jnp.bfloat16 if large else jnp.float32] * 5
            return [pltpu.VMEM((k, rows, nz), dtype) for k, dtype in zip(shapes, types)]

        def packed_scratch(many, rows):
            return [pltpu.VMEM((many, rows, nz), jnp.float32)] * 11

        assert counts[2][0] % PACK == 0 and nz >> 2 == nz // PACK
        scratch = [
            pltpu.VMEM((lx + 2 * HALO, ly + 2 * EDGE, nz), jnp.float32),
            pltpu.VMEM((2 * HALO, ly, nz), jnp.bfloat16),
            pltpu.VMEM((2, HALO, 2 * EDGE, nz), jnp.bfloat16),
            pltpu.VMEM((blocks, by + 2 * EDGE_PHASE, nz), jnp.bfloat16),
            pltpu.VMEM((blocks, by + 2 * EDGE, nz), jnp.float32),
            pltpu.VMEM((blocks, by, nz), jnp.bfloat16),
            pltpu.VMEM((ngy, ngx, cy, nz), jnp.bfloat16),
            pltpu.VMEM((ngy, 1, cy, nz), jnp.bfloat16),
            pltpu.VMEM((n, cy // 2, nz), jnp.float32),
            pltpu.VMEM((lx, ly, nz), jnp.int32),
            pltpu.VMEM((1, by, nz), jnp.bfloat16),
            pltpu.VMEM((lx, ly, nz), jnp.bfloat16),
            pltpu.VMEM((2, lx // 2, 2 * EDGE, nz), jnp.bfloat16),
            pltpu.VMEM((1, by, nz), jnp.float32),
            pltpu.VMEM((1, by, nz), jnp.bfloat16),
            pltpu.VMEM((1, cy, nz), jnp.bfloat16),
            pltpu.VMEM((1, cy, nz), jnp.bfloat16),
            pltpu.VMEM((1, cy // 2, nz), jnp.float32),
            pltpu.VMEM((8, max(2 * (by + 2 * EDGE), 2 * counts[2][1], 2 * (cy + 2 * EDGE)), nz), jnp.float32),
            pltpu.VMEM((2 * blocks, by + 2 * EDGE, nz), jnp.float32),
            pltpu.VMEM((blocks, cy + 2 * EDGE, nz), jnp.float32),
        ]
        scratch += level_scratch(lx + 2 * HALO, ly + 2 * EDGE, True)
        scratch += level_scratch(2 * blocks, by + 2 * EDGE)
        for l in range(2, LEVELS + 1):
            scratch += packed_scratch(max(counts[l][0] // PACK, 1), max(counts[l][1], EDGE))
        for l in range(LEVELS + 1):
            small = counts[l][1] < EDGE
            scratch += [pltpu.VMEM((8, counts[l][0] * (nz >> l) if small else 1, EDGE, nz), jnp.float32)]
        scratch += [pltpu.SemaphoreType.DMA((15,))] * 2
        scratch += [pltpu.SemaphoreType.DMA((3 * blocks,))] * 4
        scratch += [pltpu.SemaphoreType.DMA((2,))] * 2
        scratch += [pltpu.SemaphoreType.DMA((1,)), pltpu.SemaphoreType.DMA((ngy,))]
        scratch += [pltpu.SemaphoreType.DMA((ngy,)), pltpu.SemaphoreType.DMA((ngy,)), pltpu.SemaphoreType.DMA((2,))]
        scratch += [pltpu.SemaphoreType.REGULAR]
        anywhere = pl.BlockSpec(memory_space=pl.ANY)
        inside = pl.BlockSpec(memory_space=pltpu.VMEM)
        right_side, phase = [pltpu.with_memory_space_constraint(x, pltpu.HBM) for x in (right_side, phase)]
        found = pl.pallas_call(
            functools.partial(kernel, ngx, ngy, counts),
            out_shape=[pltpu.VMEM(right_side.shape, jnp.float32)] * 2,
            in_specs=[anywhere] * 2,
            out_specs=[inside] * 2,
            scratch_shapes=scratch,
            compiler_params=pltpu.CompilerParams(
                collective_id=0, has_side_effects=True, vmem_limit_bytes=64_000_000
            ),
        )(right_side, phase)
        return pl.pallas_call(
            write,
            out_shape=[jax.ShapeDtypeStruct(right_side.shape, jnp.float32)] * 2,
            in_specs=[inside] * 2,
            out_specs=[anywhere] * 2,
            scratch_shapes=[pltpu.SemaphoreType.DMA((2,))],
        )(*[pltpu.with_memory_space_constraint(x, pltpu.VMEM) for x in found])

    placed = P("gx", "gy", None)
    return jax.shard_map(
        on_device, mesh=mesh, in_specs=(placed, placed), out_specs=(placed, placed), check_vma=False
    )
```
